32 devices in a mesh: gx: 2 (over x), gy: 4 (over y, core), gz: 4 (over z).
Axes of the slice: x: 2, y: 2, z: 4, core: 2. Of those that a mesh axis runs over, the one named last changes fastest.
Arguments:
- positions: float32 [3, 4, 8, 8, 128], P(None, 'gx', 'gy', 'gz'), may hold values from 0 to 1
- velocities: float32 [3, 4, 8, 8, 128], P(None, 'gx', 'gy', 'gz'), may hold values from -3 to 3
- masses: float32 [4, 8, 8, 128], P('gx', 'gy', 'gz'), may hold values from 0.004 to 0.016
- alphas: float32 [4, 8, 8, 128], P('gx', 'gy', 'gz'), may hold values from 0.2 to 2
- counts: int32 [4, 8, 8], P('gx', 'gy', 'gz'), may hold values from 64 to 128, as said below
Outputs:
- density: float32 [4, 8, 8, 128], P('gx', 'gy', 'gz')
- acceleration: float32 [3, 4, 8, 8, 128], P(None, 'gx', 'gy', 'gz')
- heating: float32 [4, 8, 8, 128], P('gx', 'gy', 'gz')
The draws below stay inside these ranges and needn't reach their ends.
Inputs may be any that keep to these rules, and one draw needn't show every extreme that they name: `counts`: every cell holds 64 to 128 live particles in its first slots, and some cell holds 128.
All inputs are finite; a program needn't handle non-finite values.
Results may differ from the reference program's by a relative error of at most 0.0001.
Values sent between devices are 32-bit elements; how exact they have to be, the bound alone decides.
No kernel may reach another device: no remote copies, remote signals or barrier semaphores. Data moves between devices by JAX's collectives and lax.ppermute only.
A program may use at most 64 MiB of HBM per device.

```python
import math
import jax
import jax.numpy as jnp
from jax import lax

P_SIZE = 128
NX = 4
NY = 8
NZ = 8


def draw_counts(key, part):
    first_key, second_key = jax.random.split(jax.random.fold_in(key, 17))
    base_counts = jax.random.randint(first_key, (NX * NY * NZ,), P_SIZE // 2, P_SIZE + 1).astype(jnp.int32)
    chosen = jax.random.randint(second_key, (), 0, NX * NY * NZ)
    base_counts = base_counts.at[chosen].set(P_SIZE)
    return base_counts.reshape(NX, NY, NZ).astype(jnp.int32)


def shard_levels(rng, dims, cuts, smallest, largest):
    gain = 1.0
    for position, shards_of in cuts:
        steps = jax.random.uniform(jax.random.fold_in(jax.random.fold_in(rng, 6), position), (shards_of,), jnp.float32, smallest / len(cuts), largest / len(cuts))
        gain = gain * jnp.repeat(jnp.exp(steps), dims[position] // shards_of).reshape((-1,) + (1,) * (len(dims) - 1 - position))
    return gain


def normal_values(rng, dims, width, most, shards=(), kind=jnp.bfloat16):
    array = jax.random.normal(rng, dims, jnp.float32) * width
    if len(shards) > 0:
        array = shard_levels(rng, dims, shards, -0.22, 0.18) * array
    return jnp.clip(array, min=-most, max=most).astype(kind)


def setup_inputs(seed: int = 0) -> dict:
    key_list = jax.random.split(jax.random.key(seed), 6)
    positions = jnp.clip(1.0 * jax.random.uniform(key_list[0], (3, NX, NY, NZ, P_SIZE), jnp.float32) ** shard_levels(key_list[0], (3, NX, NY, NZ, P_SIZE), ((1, 2), (2, 4), (3, 4)), -0.2, 0.2), 0.0, 1.0)
    velocities = normal_values(key_list[1], (3, NX, NY, NZ, P_SIZE), 0.5, 3.0, ((1, 2), (2, 4), (3, 4)), jnp.float32)
    masses = jnp.clip(jnp.exp(math.log(0.016) - 1.3862944 * jax.random.uniform(key_list[2], (NX, NY, NZ, P_SIZE), jnp.float32) ** shard_levels(key_list[2], (NX, NY, NZ, P_SIZE), ((0, 2), (1, 4), (2, 4)), -0.2, 0.2)), 0.004, 0.016)
    alphas = jnp.clip(jnp.exp(math.log(2.0) - 2.3025851 * jax.random.uniform(key_list[3], (NX, NY, NZ, P_SIZE), jnp.float32) ** shard_levels(key_list[3], (NX, NY, NZ, P_SIZE), ((0, 2), (1, 4), (2, 4)), -0.2, 0.2)), 0.2, 2.0)
    counts = draw_counts(jax.random.fold_in(key_list[5], 71), 0)
    return {"positions": positions, "velocities": velocities, "masses": masses, "alphas": alphas, "counts": counts}


kernel_norm = 21.0 / (2.0 * math.pi)
neighbour_shifts = [(shift_x, shift_y, shift_z) for shift_x in (-1, 0, 1) for shift_y in (-1, 0, 1) for shift_z in (-1, 0, 1)]

def pair_geometry(own_rows, neighbour, cell_shift):
    offset_parts = [own_rows[axis_id][:, :, None] - neighbour[axis_id][:, None, :] - float(cell_shift[axis_id]) for axis_id in range(3)]
    dist_sq = offset_parts[0] * offset_parts[0] + offset_parts[1] * offset_parts[1] + offset_parts[2] * offset_parts[2]
    scaled = jnp.minimum(jnp.sqrt(dist_sq), 1.0)
    falloff = 1.0 - scaled
    kernel_value = kernel_norm * falloff ** 4 * (1.0 + 4.0 * scaled)
    kernel_slope = -20.0 * kernel_norm * falloff ** 3
    approach = sum(((own_rows[3 + axis_id][:, :, None] - neighbour[3 + axis_id][:, None, :]) * offset_parts[axis_id] for axis_id in range(3)))
    return (offset_parts, dist_sq, kernel_value, kernel_slope, approach)

def density_terms(own_rows, neighbour, cell_shift):
    offset_parts, dist_sq, kernel_value, kernel_slope, approach = pair_geometry(own_rows, neighbour, cell_shift)
    other_mass = neighbour[6][:, None, :]
    return (lax.optimization_barrier(jnp.sum(other_mass * kernel_value, -1)), lax.optimization_barrier(jnp.sum(other_mass * kernel_slope * approach, -1)))

def force_terms(own_rows, neighbour, cell_shift):
    offset_parts, dist_sq, kernel_value, kernel_slope, approach = pair_geometry(own_rows, neighbour, cell_shift)
    rho_own = own_rows[7][:, :, None]
    rho_other = neighbour[7][:, None, :]
    converge = jnp.minimum(approach, 0.0) / (dist_sq + 0.01)
    viscous = -(own_rows[8][:, :, None] + neighbour[8][:, None, :]) * converge / (rho_own + rho_other)
    mslope = neighbour[6][:, None, :] * kernel_slope
    pair_force = mslope * (1.0 / rho_own + 1.0 / rho_other + viscous)
    accel_terms = jnp.stack([-lax.optimization_barrier(jnp.sum(pair_force * offset_parts[axis_id], -1)) for axis_id in range(3)], 0)
    heating = lax.optimization_barrier(jnp.sum(mslope * (1.0 / rho_own + 0.5 * viscous) * approach, -1))
    return (accel_terms, heating)

def switch_fields(density, div_sum, live_rows, weights):
    rho_live = jnp.where(live_rows > 0, density, 1.0)
    compress = jnp.maximum(div_sum / rho_live, 0.0)
    return jnp.stack([rho_live, weights * compress / (compress + 1.0)], 0)

def over_slabs(terms, fields, neighbour, cell_shift):
    count = fields.shape[0]
    width_x = fields.shape[1]
    own_rows = jnp.moveaxis(fields, 1, 0).reshape(width_x, count, -1, fields.shape[-1])
    other_rows = jnp.moveaxis(neighbour, 1, 0).reshape(width_x, count, -1, fields.shape[-1])

    def one_slab(pair_rows):
        return terms(pair_rows[0], pair_rows[1], cell_shift)
    return lax.map(one_slab, (own_rows, other_rows))

def reference(positions, velocities, masses, alphas, counts):
    slot_count = positions.shape[-1]
    grid = positions.shape[1:4]
    occupied = (jnp.arange(slot_count, dtype=jnp.int32)[None, None, None, :] < counts[..., None]).astype(jnp.float32)
    carried = jnp.concatenate([positions, velocities, (masses * occupied)[None]], 0)
    density = jnp.zeros((grid[0], grid[1] * grid[2], slot_count), jnp.float32)
    div_sum = jnp.zeros((grid[0], grid[1] * grid[2], slot_count), jnp.float32)
    for cell_shift in neighbour_shifts:
        neighbour = jnp.roll(carried, (-cell_shift[0], -cell_shift[1], -cell_shift[2]), axis=(1, 2, 3))
        part_density, part_div = over_slabs(density_terms, carried, neighbour, cell_shift)
        density = density + part_density
        div_sum = div_sum + part_div
    live_rows = occupied.reshape(grid[0], -1, slot_count)
    weights = alphas.reshape(grid[0], -1, slot_count)
    pressure_fields = switch_fields(density, div_sum, live_rows, weights).reshape((2,) + grid + (slot_count,))
    fields = jnp.concatenate([carried, pressure_fields], 0)
    accel_total = jnp.zeros((grid[0], 3, grid[1] * grid[2], slot_count), jnp.float32)
    heat_total = jnp.zeros((grid[0], grid[1] * grid[2], slot_count), jnp.float32)
    for cell_shift in neighbour_shifts:
        neighbour = jnp.roll(fields, (-cell_shift[0], -cell_shift[1], -cell_shift[2]), axis=(1, 2, 3))
        part_accel, part_heat = over_slabs(force_terms, fields, neighbour, cell_shift)
        accel_total = accel_total + part_accel
        heat_total = heat_total + part_heat
    acceleration = jnp.moveaxis(accel_total, 1, 0).reshape((3,) + grid + (slot_count,)) * occupied[None]
    heating = heat_total.reshape(grid + (slot_count,)) * occupied
    return (pressure_fields[0], acceleration, heating)
```

```python
import math

import jax
import jax.numpy as jnp
from jax import lax
from jax.experimental import pallas as pl
from jax.experimental.pallas import tpu as pltpu
from jax.sharding import PartitionSpec as P

f32 = jnp.float32
bf16 = jnp.bfloat16
kernel_norm = 21.0 / (2.0 * math.pi)
axes = ("gx", "gy", "gz")
tile_rows = 8
feature_rows = 64
tiny = 1e-12

vmem = pl.BlockSpec(memory_space=pltpu.VMEM)
smem = pl.BlockSpec(memory_space=pltpu.SMEM)


def shaped(*dims, kind=f32):
    return jax.ShapeDtypeStruct(dims, kind)


def paired(axis):
    return lax.axis_size(axis) % 2 == 0


def first_sends_high(axis):
    return lax.axis_index(axis) % 2 == 0 if paired(axis) else lax.axis_index(axis) >= 0


def first_gives_before(axis):
    return lax.axis_index(axis) % 2 == 1 if paired(axis) else lax.axis_index(axis) >= 0


def routes(axis):
    peers = lax.axis_size(axis)
    if peers % 2 == 0:
        first = [(i, i + 1 if i % 2 == 0 else i - 1) for i in range(peers)]
        second = [(i, (i - 1 if i % 2 == 0 else i + 1) % peers) for i in range(peers)]
    else:
        first = [(i, (i + 1) % peers) for i in range(peers)]
        second = [(i, (i - 1) % peers) for i in range(peers)]
    return first, second


def exchanged(axis, sends):
    first, second = routes(axis)
    if first == second:
        both = lax.ppermute(sends, axis, first)
        return (both,)
    return lax.ppermute(sends[0], axis, first), lax.ppermute(sends[1], axis, second)


def merged(axis, mesh_shape):
    return mesh_shape[axis] == 2


def split3(value):
    high = value.astype(bf16).astype(f32)
    rest = value - high
    middle = rest.astype(bf16).astype(f32)
    return high, middle, rest - middle


def row_ids():
    return lax.broadcasted_iota(jnp.int32, (tile_rows, 128), 0)


def rows_of(*rows):
    ids = row_ids()
    out = jnp.zeros((tile_rows, 128), f32)
    for place, row in enumerate(rows):
        out = jnp.where(ids == place, row, out)
    return out


def moments(tile, offsets):
    ids = row_ids()
    shift = jnp.where(ids == 0, offsets[0], jnp.where(ids == 1, offsets[1], jnp.where(ids == 2, offsets[2], 0.0)))
    moved = tile + shift
    x, y, z, vx, vy, vz = (moved[i : i + 1] for i in range(6))
    sq = x * x + y * y + z * z
    xv = x * vx + y * vy + z * vz
    return jnp.where(ids == 6, sq, jnp.where(ids == 7, xv, moved)), tile[6:7]


def other_features(table, mass):
    p1, p2, p3 = split3(table)
    m1, m2, m3 = split3(mass)
    extra = rows_of(1.0, 1.0, 1.0, m1, m2, m3)
    lanes = jnp.concatenate([p1, p1, p1, p2, p2, p3, extra, jnp.zeros_like(extra)], 0)
    return lanes.T.astype(bf16)


def own_features(table):
    ids = row_ids()
    sq = split3(table[6:7])
    xv = split3(table[7:8])
    down = pltpu.roll(table, 3, 0)
    up = pltpu.roll(table, 5, 0)
    left = jnp.where(ids < 3, -2.0 * table, jnp.where(ids == 6, 1.0, 0.0))
    right = jnp.where(ids < 3, -up, jnp.where(ids < 6, -down, jnp.where(ids == 7, 1.0, 0.0)))
    halves = []
    for part, fixed in ((left, sq), (right, xv)):
        q1, q2, q3 = split3(part)
        extra = rows_of(*fixed)
        halves.append(jnp.concatenate([q1, q2, q3, q1, q2, q1, extra, jnp.zeros_like(extra)], 0))
    return jnp.concatenate(halves, 1).astype(bf16)


def mass_columns(table, mass):
    weighted = mass * table
    w1, w2, _ = split3(weighted)
    m1, m2, _ = split3(mass)
    extra = rows_of(m1, m2)
    return jnp.concatenate([w1, w2, extra, jnp.zeros_like(extra)], 0).astype(bf16)


def picker(first_row):
    ids = lax.broadcasted_iota(jnp.int32, (feature_rows, 128), 0)
    return jnp.where((ids >= first_row) & (ids < first_row + 3), 1.0, 0.0).astype(bf16)


def prepare(tile, offsets, at, feats, masses, columns):
    table, mass = moments(tile, offsets)
    lanes = other_features(table, mass)
    feats[at] = lanes
    masses[at] = jnp.dot(lanes, picker(51), preferred_element_type=f32)
    columns[at] = mass_columns(table, mass)


def density_pairs(own, cells, near, feats, masses, columns, ghi, glo, visc, sums, weighted):
    def one(c, _):
        right = own[c]
        total = jnp.zeros((tile_rows, 128), f32)
        picks = near(c)
        for k, n in enumerate(picks):
            both = jnp.dot(feats[n], right, preferred_element_type=f32)
            for r in range(0, 128, 16):
                dist = jnp.maximum(both[r : r + 16, :128], tiny)
                run = both[r : r + 16, 128:]
                q = dist * lax.rsqrt(dist)
                fall = jnp.maximum(1.0 - q, 0.0)
                g = fall * fall * fall
                part = g * q * masses[n, r : r + 16]
                total = total + part[:8] + part[8:]
                high = g.astype(bf16)
                ghi[c, k * 128 + r : k * 128 + r + 16] = high
                glo[c, k * 128 + r : k * 128 + r + 16] = (g - high.astype(f32)).astype(bf16)
                visc[c, k * 128 + r : k * 128 + r + 16] = g * jnp.minimum(run, 0.0) * (1.0 / (dist + 0.01))
        left = jnp.concatenate([columns[n] for n in picks], 1)
        sums[c] = jnp.dot(left, ghi[c], preferred_element_type=f32) + jnp.dot(
            left, glo[c], preferred_element_type=f32
        )
        weighted[c] = total
        return 0

    lax.fori_loop(0, cells, one, 0)


def prepare_force(tile, offsets, press, at, rhos, columns, gradients):
    table, mass = moments(tile, offsets)
    rho = press[0:1]
    weight = press[1:2]
    heavy = mass * table
    h1, h2, _ = split3(heavy)
    s1, s2, _ = split3(weight * heavy)
    m1, m2, _ = split3(mass)
    w1, w2, _ = split3(weight * mass)
    extra = rows_of(m1, m2, w1, w2)
    columns[at] = jnp.concatenate([h1, h2, s1, s2, extra, jnp.zeros_like(extra)], 0).astype(bf16)
    light = (mass / rho) * jnp.where(row_ids() < 3, table, 1.0)
    l1, l2, _ = split3(light)
    gradients[at] = jnp.concatenate([l1, l2], 0).astype(bf16)
    r1, r2, r3 = split3(rho)
    lanes = jnp.concatenate([rows_of(r1, r2, r3), jnp.zeros((tile_rows, 128), f32)], 0).T.astype(bf16)
    ids = lax.broadcasted_iota(jnp.int32, (16, 128), 0)
    rhos[at] = jnp.dot(lanes, jnp.where(ids < 3, 1.0, 0.0).astype(bf16), preferred_element_type=f32)


def force_pairs(cells, near, press_row, rhos, columns, gradients, ghi, glo, visc, thi, tlo, sums, slopes):
    def one(c, _):
        picks = near(c)
        mine = press_row(c)
        for k, n in enumerate(picks):
            for r in range(0, 128, 16):
                at = slice(k * 128 + r, k * 128 + r + 16)
                t = visc[c, at] * (1.0 / (rhos[n, r : r + 16] + mine))
                high = t.astype(bf16)
                thi[at] = high
                tlo[at] = (t - high.astype(f32)).astype(bf16)
        left = jnp.concatenate([columns[n] for n in picks], 1)
        sums[c] = jnp.dot(left, thi[...], preferred_element_type=f32) + jnp.dot(
            left, tlo[...], preferred_element_type=f32
        )
        left = jnp.concatenate([gradients[n] for n in picks], 1)
        slopes[c] = jnp.dot(left, ghi[c], preferred_element_type=f32) + jnp.dot(
            left, glo[c], preferred_element_type=f32
        )
        return 0

    lax.fori_loop(0, cells, one, 0)


def parts_of(c):
    return c // 4, (c // 2) % 2, c % 2


def flat(*pairs):
    at = 0
    for size, index in pairs:
        at = at * size + index
    return at


def near_own(c):
    return list(range(8))


def near_z(c):
    cx, cy, cz = parts_of(c)
    return [flat((2, cz), (2, x), (2, y)) for x in range(2) for y in range(2)]


def near_y(c):
    cx, cy, cz = parts_of(c)
    return [flat((2, cy), (2, x), (4, cz + dz)) for x in range(2) for dz in range(3)]


def near_x(c):
    cx, cy, cz = parts_of(c)
    return [flat((2, cx), (4, cy + dy), (4, cz + dz)) for dy in range(3) for dz in range(3)]


def place_own(e):
    x, y, z = parts_of(e)
    return x - 1, y - 1, z - 1


def place_z(e):
    side, x, y = parts_of(e)
    return x - 1, y - 1, 3 * side - 2


def place_y(e):
    return (e // 4) % 2 - 1, 3 * (e // 8) - 2, e % 4 - 2


def place_x(e):
    return 3 * (e // 16) - 2, (e // 4) % 4 - 2, e % 4 - 2


def offsets_of(place):
    return [jnp.asarray(v, jnp.int32).astype(f32) for v in place]


groups = {
    "own": (8, near_own, place_own, 8),
    "z": (8, near_z, place_z, 4),
    "y": (16, near_y, place_y, 6),
    "x": (32, near_x, place_x, 9),
}


def scratch_density(entries):
    return [
        pltpu.VMEM((entries, 128, feature_rows), bf16),
        pltpu.VMEM((entries, 128, 128), f32),
        pltpu.VMEM((entries, 32, 128), bf16),
    ]


def pair_outputs(count):
    return [
        shaped(8, count * 128, 128, kind=bf16),
        shaped(8, count * 128, 128, kind=bf16),
        shaped(8, count * 128, 128),
        shaped(8, 32, 128),
        shaped(8, tile_rows, 128),
    ]


def call(body, outs, operands, specs=None, scratch=(), limit=24, name=None):
    return pl.pallas_call(
        body,
        out_shape=tuple(outs),
        in_specs=specs or [vmem] * len(operands),
        out_specs=tuple([vmem] * len(outs)),
        scratch_shapes=list(scratch),
        compiler_params=pltpu.CompilerParams(vmem_limit_bytes=limit << 20),
        name=name,
    )(*operands)


def take_side(before, refs, side, rest):
    if len(refs) == 1:
        one, two = refs[0][(0,) + rest], refs[0][(1,) + rest]
    else:
        one, two = refs[0][rest], refs[1][rest]
    return jnp.where(before, one, two) if side == 0 else jnp.where(before, two, one)


def send_shapes(axis, plane):
    if lax.axis_size(axis) == 2:
        return [shaped(2, *plane)]
    return [shaped(*plane), shaped(*plane)]


def put_sends(axis, refs, high, tile_at, rest):
    top, bottom = tile_at(1), tile_at(0)
    one, two = jnp.where(high, top, bottom), jnp.where(high, bottom, top)
    if len(refs) == 1:
        refs[0][(0,) + rest] = one
        refs[0][(1,) + rest] = two
    else:
        refs[0][rest] = one
        refs[1][rest] = two


def receive(axis, sends):
    if len(sends) == 1:
        return exchanged(axis, sends[0])
    return exchanged(axis, sends)


def pack_y(own, from_z, rows, name):
    sends = send_shapes("gy", (2, 4, rows, 128))
    n = len(from_z)

    def body(own_ref, *refs):
        got, out = refs[:n], refs[n:]
        high = first_sends_high("gy")
        before = first_gives_before("gz")
        for x in range(2):
            for e in range(4):

                def tile_at(y, x=x, e=e):
                    if 1 <= e <= 2:
                        return own_ref[x, y, e - 1]
                    return take_side(before, got, 0 if e == 0 else 1, (x, y))

                put_sends("gy", out, high, tile_at, (x, e))

    return call(body, sends, (own, *from_z), name=name, limit=4)


def pack_x(own, from_z, from_y, rows, name):
    sends = send_shapes("gx", (4, 4, rows, 128))
    n, m = len(from_z), len(from_y)

    def body(own_ref, *refs):
        got_z, got_y, out = refs[:n], refs[n : n + m], refs[n + m :]
        high = first_sends_high("gx")
        before_z = first_gives_before("gz")
        before_y = first_gives_before("gy")
        for a in range(4):
            for e in range(4):

                def tile_at(x, a=a, e=e):
                    if not 1 <= a <= 2:
                        return take_side(before_y, got_y, 0 if a == 0 else 1, (x, e))
                    if 1 <= e <= 2:
                        return own_ref[x, a - 1, e - 1]
                    return take_side(before_z, got_z, 0 if e == 0 else 1, (x, a - 1))

                put_sends("gx", out, high, tile_at, (a, e))

    return call(body, sends, (own, *from_z, *from_y), name=name, limit=4)


inner_dims = {"z": (2, 2), "y": (2, 4), "x": (4, 4)}


def entry_tile(group, before, refs, e, sides):
    a, b = inner_dims[group]
    return take_side(before, refs, sides, (e // b, e % b))


def density_own(own):
    entries, near, place, count = groups["own"]

    def body(own_ref, ghi, glo, visc, sums, weighted, table_ref, feats, masses, columns):
        def one(c, _):
            x, y, z = parts_of(c)
            tile = own_ref[x, y, z]
            offsets = offsets_of(place(c))
            prepare(tile, offsets, c, feats, masses, columns)
            table, _mass = moments(tile, offsets)
            table_ref[c] = own_features(table)
            return 0

        lax.fori_loop(0, 8, one, 0)
        density_pairs(table_ref, 8, near, feats, masses, columns, ghi, glo, visc, sums, weighted)

    outs = pair_outputs(count) + [shaped(8, feature_rows, 256, kind=bf16)]
    return call(body, outs, (own,), scratch=scratch_density(entries), name="density_own")


def density_halo(group, axis, received, own_feats):
    entries, near, place, count = groups[group]
    n = len(received)
    half = entries // 2

    def body(*refs):
        got, own_ref = refs[:n], refs[n]
        ghi, glo, visc, sums, weighted, feats, masses, columns = refs[n + 1 :]
        before = first_gives_before(axis)
        for side in range(2):

            def one(e, _, side=side):
                tile = entry_tile(group, before, got, e, side)
                at = side * half + e
                prepare(tile, offsets_of(place(at)), at, feats, masses, columns)
                return 0

            lax.fori_loop(0, half, one, 0)
        density_pairs(own_ref, 8, near, feats, masses, columns, ghi, glo, visc, sums, weighted)

    return call(
        body,
        pair_outputs(count),
        (*received, own_feats),
        scratch=scratch_density(entries),
        name="density_" + group,
    )


def pressure(own, alphas, counts, partials):
    sends = send_shapes("gz", (2, 2, 2, 128))
    outs = [shaped(2, 2, 2, 2, 128), shaped(2, 2, 2, 128), shaped(8, tile_rows, 128)] + sends
    n = len(partials)

    def body(counts_ref, alphas_ref, own_ref, *refs):
        pieces, (press, density, first), out = refs[:n], refs[n : n + 3], refs[n + 3 :]
        high = first_sends_high("gz")
        lanes = lax.broadcasted_iota(jnp.int32, (1, 128), 1)
        for x in range(2):
            for y in range(2):
                for z in range(2):
                    c = 4 * x + 2 * y + z
                    table, _mass = moments(own_ref[x, y, z], [float(v - 1) for v in (x, y, z)])
                    s = sum(p[c] for p in pieces[0::2])
                    gq = jnp.sum(sum(p[c] for p in pieces[1::2]), 0, keepdims=True)
                    t = s[0:8] + s[8:16]
                    m0 = s[16:17] + s[17:18]
                    pos, vel = table[0:3], table[3:6]
                    x_mx = jnp.sum(pos * t[0:3], 0, keepdims=True)
                    x_mv = jnp.sum(pos * t[3:6], 0, keepdims=True)
                    v_mx = jnp.sum(vel * t[0:3], 0, keepdims=True)
                    gr2 = t[6:7] + table[6:7] * m0 - 2.0 * x_mx
                    rho = kernel_norm * (m0 + 3.0 * gq - 4.0 * gr2)
                    div = -20.0 * kernel_norm * (t[7:8] + table[7:8] * m0 - x_mv - v_mx)
                    rho = jnp.where(lanes < counts_ref[x, y, z], rho, 1.0)
                    compress = jnp.maximum(div / rho, 0.0)
                    weight = alphas_ref[x, y, z : z + 1, :] * compress / (compress + 1.0)
                    press[x, y, z] = jnp.concatenate([rho, weight], 0)
                    density[x, y, z : z + 1, :] = rho
                    first[c] = jnp.concatenate(
                        [pos * m0 - t[0:3], div, jnp.zeros((tile_rows - 4, 128), f32)], 0
                    )
        for x in range(2):
            for y in range(2):
                put_sends("gz", out, high, lambda z, x=x, y=y: press[x, y, z], (x, y))

    operands = (counts, alphas, own, *partials)
    specs = [smem] + [vmem] * (len(operands) - 1)
    return call(body, outs, operands, specs=specs, name="pressure", limit=8)


def scratch_force(entries, count):
    return [
        pltpu.VMEM((entries, 128, 128), f32),
        pltpu.VMEM((entries, 48, 128), bf16),
        pltpu.VMEM((entries, 16, 128), bf16),
        pltpu.VMEM((count * 128, 128), bf16),
        pltpu.VMEM((count * 128, 128), bf16),
    ]


def force_outputs():
    return [shaped(8, 48, 128), shaped(8, 16, 128)]


def force_own(own, press, kept):
    entries, near, place, count = groups["own"]

    def body(own_ref, press_ref, ghi, glo, visc, sums, slopes, rhos, columns, gradients, thi, tlo):
        def one(c, _):
            x, y, z = parts_of(c)
            prepare_force(
                own_ref[x, y, z], offsets_of(place(c)), press_ref[x, y, z], c, rhos, columns, gradients
            )
            return 0

        lax.fori_loop(0, 8, one, 0)

        def mine(c):
            x, y, z = parts_of(c)
            return press_ref[x, y, z, 0:1]

        force_pairs(8, near, mine, rhos, columns, gradients, ghi, glo, visc, thi, tlo, sums, slopes)

    return call(
        body,
        force_outputs(),
        (own, press, *kept),
        scratch=scratch_force(entries, count),
        name="force_own",
    )


def force_halo(group, axis, received, press_received, press, kept):
    entries, near, place, count = groups[group]
    n = len(received)
    half = entries // 2

    def body(*refs):
        got, got_press, press_ref = refs[:n], refs[n : 2 * n], refs[2 * n]
        ghi, glo, visc, sums, slopes, rhos, columns, gradients, thi, tlo = refs[2 * n + 1 :]
        before = first_gives_before(axis)
        for side in range(2):

            def one(e, _, side=side):
                tile = entry_tile(group, before, got, e, side)
                fields = entry_tile(group, before, got_press, e, side)
                at = side * half + e
                prepare_force(tile, offsets_of(place(at)), fields, at, rhos, columns, gradients)
                return 0

            lax.fori_loop(0, half, one, 0)

        def mine(c):
            x, y, z = parts_of(c)
            return press_ref[x, y, z, 0:1]

        force_pairs(8, near, mine, rhos, columns, gradients, ghi, glo, visc, thi, tlo, sums, slopes)

    return call(
        body,
        force_outputs(),
        (*received, *press_received, press, *kept),
        scratch=scratch_force(entries, count),
        name="force_" + group,
    )


def finish(own, press, first, counts, partials):
    outs = [shaped(3, 2, 2, 2, 128), shaped(2, 2, 2, 128)]
    n = len(partials)

    def body(counts_ref, own_ref, press_ref, first_ref, *refs):
        pieces, (accel, heating) = refs[:n], refs[n:]
        lanes = lax.broadcasted_iota(jnp.int32, (1, 128), 1)
        for x in range(2):
            for y in range(2):
                for z in range(2):
                    c = 4 * x + 2 * y + z
                    table, _mass = moments(own_ref[x, y, z], [float(v - 1) for v in (x, y, z)])
                    u = sum(p[c] for p in pieces[0::2])
                    v = sum(p[c] for p in pieces[1::2])
                    plain, scaled = u[0:8] + u[8:16], u[16:24] + u[24:32]
                    a0, b0 = u[32:33] + u[33:34], u[34:35] + u[35:36]
                    g = v[0:8] + v[8:16]
                    rho, weight = press_ref[x, y, z, 0:1], press_ref[x, y, z, 1:2]
                    inverse = 1.0 / rho
                    mixed = weight * plain + scaled
                    zero = weight * a0 + b0
                    pos, vel = table[0:3], table[3:6]
                    total = (
                        inverse * first_ref[c, 0:3]
                        + (pos * g[3:4] - g[0:3])
                        - (pos * zero - mixed[0:3])
                    )
                    live = jnp.where(lanes < counts_ref[x, y, z], 1.0, 0.0)
                    push = (20.0 * kernel_norm) * live * total
                    work = (
                        mixed[7:8]
                        + table[7:8] * zero
                        - jnp.sum(pos * mixed[3:6], 0, keepdims=True)
                        - jnp.sum(vel * mixed[0:3], 0, keepdims=True)
                    )
                    warm = live * (first_ref[c, 3:4] * inverse + (10.0 * kernel_norm) * work)
                    for i in range(3):
                        accel[i, x, y, z : z + 1, :] = push[i : i + 1]
                    heating[x, y, z : z + 1, :] = warm

    operands = (counts, own, press, first, *partials)
    specs = [smem] + [vmem] * (len(operands) - 1)
    return call(body, outs, operands, specs=specs, name="finish", limit=8)


def gather_own(positions, velocities, masses, counts):
    sends = send_shapes("gz", (2, 2, tile_rows, 128))

    def body(counts_ref, pos, vel, mass, own, *out):
        high = first_sends_high("gz")
        lanes = lax.broadcasted_iota(jnp.int32, (1, 128), 1)
        for x in range(2):
            for y in range(2):
                for z in range(2):
                    here = mass[x, y, z : z + 1, :] * jnp.where(lanes < counts_ref[x, y, z], 1.0, 0.0)
                    own[x, y, z] = rows_of(
                        *(pos[i, x, y, z : z + 1, :] for i in range(3)),
                        *(vel[i, x, y, z : z + 1, :] for i in range(3)),
                        here,
                    )
        for x in range(2):
            for y in range(2):
                put_sends("gz", out, high, lambda z, x=x, y=y: own[x, y, z], (x, y))

    outs = [shaped(2, 2, 2, tile_rows, 128)] + sends
    operands = (counts, positions, velocities, masses)
    return call(body, outs, operands, specs=[smem] + [vmem] * 3, name="gather_own", limit=4)


def per_block(positions, velocities, masses, alphas, counts):
    own, *sends = gather_own(positions, velocities, masses, counts)
    from_z = receive("gz", sends)
    *kept_own, sums_own, weighted_own, own_feats = density_own(own)
    from_y = receive("gy", pack_y(own, from_z, tile_rows, "pack_y"))
    *kept_z, sums_z, weighted_z = density_halo("z", "gz", from_z, own_feats)
    from_x = receive("gx", pack_x(own, from_z, from_y, tile_rows, "pack_x"))
    *kept_y, sums_y, weighted_y = density_halo("y", "gy", from_y, own_feats)
    *kept_x, sums_x, weighted_x = density_halo("x", "gx", from_x, own_feats)
    partials = (sums_own, weighted_own, sums_z, weighted_z, sums_y, weighted_y, sums_x, weighted_x)
    press, density, first, *sends = pressure(own, alphas, counts, partials)
    press_z = receive("gz", sends)
    forces = list(force_own(own, press, kept_own))
    press_y = receive("gy", pack_y(press, press_z, 2, "pack_press_y"))
    forces += force_halo("z", "gz", from_z, press_z, press, kept_z)
    press_x = receive("gx", pack_x(press, press_z, press_y, 2, "pack_press_x"))
    forces += force_halo("y", "gy", from_y, press_y, press, kept_y)
    forces += force_halo("x", "gx", from_x, press_x, press, kept_x)
    accel, heating = finish(own, press, first, counts, forces)
    return density, accel, heating


neighbour_shifts = [
    (shift_x, shift_y, shift_z)
    for shift_x in (-1, 0, 1)
    for shift_y in (-1, 0, 1)
    for shift_z in (-1, 0, 1)
]


def extended(shard, sides, width):
    for axis, dim in sides:
        peers, length = (lax.axis_size(axis), shard.shape[dim])
        up = [(i, (i + 1) % peers) for i in range(peers)]
        down = [(j, i) for i, j in up]
        last = lax.slice_in_dim(shard, length - width, length, axis=dim)
        leading = lax.slice_in_dim(shard, 0, width, axis=dim)
        before = lax.ppermute(last, axis, up)
        after = lax.ppermute(leading, axis, down)
        shard = jnp.concatenate([before, shard, after], axis=dim)
    return shard


def pair_geometry(own_rows, neighbour, cell_shift):
    offset_parts = [
        own_rows[axis_id][:, :, None] - neighbour[axis_id][:, None, :] - float(cell_shift[axis_id])
        for axis_id in range(3)
    ]
    dist_sq = (
        offset_parts[0] * offset_parts[0]
        + offset_parts[1] * offset_parts[1]
        + offset_parts[2] * offset_parts[2]
    )
    scaled = jnp.minimum(jnp.sqrt(dist_sq), 1.0)
    falloff = 1.0 - scaled
    kernel_value = kernel_norm * falloff**4 * (1.0 + 4.0 * scaled)
    kernel_slope = -20.0 * kernel_norm * falloff**3
    approach = sum(
        (
            (own_rows[3 + axis_id][:, :, None] - neighbour[3 + axis_id][:, None, :])
            * offset_parts[axis_id]
            for axis_id in range(3)
        )
    )
    return (offset_parts, dist_sq, kernel_value, kernel_slope, approach)


def density_terms(own_rows, neighbour, cell_shift):
    offset_parts, dist_sq, kernel_value, kernel_slope, approach = pair_geometry(
        own_rows, neighbour, cell_shift
    )
    other_mass = neighbour[6][:, None, :]
    return (
        jnp.sum(other_mass * kernel_value, -1),
        jnp.sum(other_mass * kernel_slope * approach, -1),
    )


def force_terms(own_rows, neighbour, cell_shift):
    offset_parts, dist_sq, kernel_value, kernel_slope, approach = pair_geometry(
        own_rows, neighbour, cell_shift
    )
    rho_own = own_rows[7][:, :, None]
    rho_other = neighbour[7][:, None, :]
    converge = jnp.minimum(approach, 0.0) / (dist_sq + 0.01)
    viscous = (
        -(own_rows[8][:, :, None] + neighbour[8][:, None, :]) * converge / (rho_own + rho_other)
    )
    mslope = neighbour[6][:, None, :] * kernel_slope
    pair_force = mslope * (1.0 / rho_own + 1.0 / rho_other + viscous)
    accel_terms = jnp.stack(
        [-jnp.sum(pair_force * offset_parts[axis_id], -1) for axis_id in range(3)], 0
    )
    heating = jnp.sum(mslope * (1.0 / rho_own + 0.5 * viscous) * approach, -1)
    return (accel_terms, heating)


def switch_fields(density, div_sum, live_rows, weights):
    rho_live = jnp.where(live_rows > 0, density, 1.0)
    compress = jnp.maximum(div_sum / rho_live, 0.0)
    return jnp.stack([rho_live, weights * compress / (compress + 1.0)], 0)


def sweep(terms, padded):
    count = padded.shape[0]
    slot_count = padded.shape[-1]
    span_x = padded.shape[1] - 2
    span_y = padded.shape[2] - 2
    span_z = padded.shape[3] - 2
    own_rows = padded[:, 1 : span_x + 1, 1 : span_y + 1, 1 : span_z + 1].reshape(
        count, -1, slot_count
    )
    totals = None
    for cell_shift in neighbour_shifts:
        neighbour = padded[
            :,
            1 + cell_shift[0] : 1 + cell_shift[0] + span_x,
            1 + cell_shift[1] : 1 + cell_shift[1] + span_y,
            1 + cell_shift[2] : 1 + cell_shift[2] + span_z,
        ]
        result = terms(own_rows, neighbour.reshape(count, -1, slot_count), cell_shift)
        totals = (
            result
            if totals is None
            else jax.tree.map(lambda left, right: left + right, totals, result)
        )
    return totals


def per_device(positions, velocities, masses, alphas, counts):
    slot_count = positions.shape[-1]
    cell_shape = positions.shape[1:4]
    occupied = (
        jnp.arange(slot_count, dtype=jnp.int32)[None, None, None, :] < counts[..., None]
    ).astype(jnp.float32)
    live_mass = masses * occupied
    carried = jnp.concatenate([positions, velocities, live_mass[None]], 0)
    padded = extended(carried, (("gx", 1), ("gy", 2), ("gz", 3)), 1)
    density, div_sum = sweep(density_terms, padded)
    live_rows = occupied.reshape(-1, slot_count)
    weights = alphas.reshape(-1, slot_count)
    pressure_fields = switch_fields(density, div_sum, live_rows, weights).reshape(
        (2,) + cell_shape + (slot_count,)
    )
    own_density = pressure_fields[0]
    pressure_pad = extended(pressure_fields, (("gx", 1), ("gy", 2), ("gz", 3)), 1)
    fields = jnp.concatenate([padded, pressure_pad], 0)
    accel_total, heat_total = sweep(force_terms, fields)
    acceleration = accel_total.reshape((3,) + cell_shape + (slot_count,)) * occupied[None]
    heating = heat_total.reshape(cell_shape + (slot_count,)) * occupied
    return (own_density, acceleration, heating)


def per_device_any(positions, velocities, masses, alphas, counts):
    if positions.shape[1:] == (2, 2, 2, 128):
        return per_block(positions, velocities, masses, alphas, counts)
    return per_device(positions, velocities, masses, alphas, counts)


def solution(mesh):
    return jax.shard_map(
        per_device_any,
        mesh=mesh,
        in_specs=(
            P(None, "gx", "gy", "gz", None),
            P(None, "gx", "gy", "gz", None),
            P("gx", "gy", "gz", None),
            P("gx", "gy", "gz", None),
            P("gx", "gy", "gz"),
        ),
        out_specs=(
            P("gx", "gy", "gz", None),
            P(None, "gx", "gy", "gz", None),
            P("gx", "gy", "gz", None),
        ),
        check_vma=False,
    )
```

```python
import math

import jax
import jax.numpy as jnp
from jax import lax
from jax.experimental import pallas as pl
from jax.experimental.pallas import tpu as pltpu
from jax.sharding import PartitionSpec as P

f32 = jnp.float32
bf16 = jnp.bfloat16
kernel_norm = 21.0 / (2.0 * math.pi)
axes = ("gx", "gy", "gz")
tile_rows = 8
feature_rows = 64
tiny = 1e-12
together = 2

vmem = pl.BlockSpec(memory_space=pltpu.VMEM)
smem = pl.BlockSpec(memory_space=pltpu.SMEM)


def shaped(*dims, kind=f32):
    return jax.ShapeDtypeStruct(dims, kind)


def paired(axis):
    return lax.axis_size(axis) % 2 == 0


def first_sends_high(axis):
    return lax.axis_index(axis) % 2 == 0 if paired(axis) else lax.axis_index(axis) >= 0


def first_gives_before(axis):
    return lax.axis_index(axis) % 2 == 1 if paired(axis) else lax.axis_index(axis) >= 0


def routes(axis):
    peers = lax.axis_size(axis)
    if peers % 2 == 0:
        first = [(i, i + 1 if i % 2 == 0 else i - 1) for i in range(peers)]
        second = [(i, (i - 1 if i % 2 == 0 else i + 1) % peers) for i in range(peers)]
    else:
        first = [(i, (i + 1) % peers) for i in range(peers)]
        second = [(i, (i - 1) % peers) for i in range(peers)]
    return first, second


def exchanged(axis, sends):
    first, second = routes(axis)
    if first == second:
        both = lax.ppermute(sends, axis, first)
        return (both,)
    return lax.ppermute(sends[0], axis, first), lax.ppermute(sends[1], axis, second)


def merged(axis, mesh_shape):
    return mesh_shape[axis] == 2


def split3(value):
    high = value.astype(bf16).astype(f32)
    rest = value - high
    middle = rest.astype(bf16).astype(f32)
    return high, middle, rest - middle


def row_ids():
    return lax.broadcasted_iota(jnp.int32, (tile_rows, 128), 0)


def rows_of(*rows):
    ids = row_ids()
    out = jnp.zeros((tile_rows, 128), f32)
    for place, row in enumerate(rows):
        out = jnp.where(ids == place, row, out)
    return out


def moments(tile, offsets):
    ids = row_ids()
    shift = jnp.where(ids == 0, offsets[0], jnp.where(ids == 1, offsets[1], jnp.where(ids == 2, offsets[2], 0.0)))
    moved = tile + shift
    x, y, z, vx, vy, vz = (moved[i : i + 1] for i in range(6))
    sq = x * x + y * y + z * z
    xv = x * vx + y * vy + z * vz
    return jnp.where(ids == 6, sq, jnp.where(ids == 7, xv, moved)), tile[6:7]


def other_features(table, mass):
    p1, p2, p3 = split3(table)
    m1, m2, m3 = split3(mass)
    extra = rows_of(1.0, 1.0, 1.0, m1, m2, m3)
    lanes = jnp.concatenate([p1, p1, p1, p2, p2, p3, extra, jnp.zeros_like(extra)], 0)
    return lanes.T.astype(bf16)


def own_features(table):
    ids = row_ids()
    sq = split3(table[6:7])
    xv = split3(table[7:8])
    down = pltpu.roll(table, 3, 0)
    up = pltpu.roll(table, 5, 0)
    left = jnp.where(ids < 3, -2.0 * table, jnp.where(ids == 6, 1.0, 0.0))
    right = jnp.where(ids < 3, -up, jnp.where(ids < 6, -down, jnp.where(ids == 7, 1.0, 0.0)))
    halves = []
    for part, fixed in ((left, sq), (right, xv)):
        q1, q2, q3 = split3(part)
        extra = rows_of(*fixed)
        halves.append(jnp.concatenate([q1, q2, q3, q1, q2, q1, extra, jnp.zeros_like(extra)], 0))
    return jnp.concatenate(halves, 1).astype(bf16)


def mass_columns(table, mass):
    weighted = mass * table
    w1, w2, _ = split3(weighted)
    m1, m2, _ = split3(mass)
    extra = rows_of(m1, m2)
    left = jnp.concatenate([w1, w2, extra, jnp.zeros_like(extra)], 0).astype(bf16)
    return jnp.concatenate([left, left], 1)


def picker(first_row):
    ids = lax.broadcasted_iota(jnp.int32, (feature_rows, 128), 0)
    return jnp.where((ids >= first_row) & (ids < first_row + 3), 1.0, 0.0).astype(bf16)


def prepare(tile, offsets, at, feats, masses, columns):
    table, mass = moments(tile, offsets)
    lanes = other_features(table, mass)
    feats[at] = lanes
    masses[at] = jnp.dot(lanes, picker(51), preferred_element_type=f32)
    columns[at] = mass_columns(table, mass)


def pipelined(tiles, stages):
    for step in range(len(tiles) + len(stages) - 1):
        for lag, stage in enumerate(stages):
            if 0 <= step - lag < len(tiles):
                stage(*tiles[step - lag])


def over_cells(cells, body):
    lax.fori_loop(0, cells // together, lambda i, _: body([i * together + j for j in range(together)]), 0)


def density_pairs(own, cells, near, feats, masses, columns, slopes, visc, sums, weighted):
    def some(group):
        both, total, sofar = {}, {}, {}
        tiles = [(j, k) for j, c in enumerate(group) for k in range(len(near(c)))]
        picks = [near(c) for c in group]

        def geometry(j, k):
            both[j, k] = jnp.dot(feats[picks[j][k]], own[group[j]], preferred_element_type=f32)

        def terms(j, k):
            c, n = group[j], picks[j][k]
            pair = both.pop((j, k))
            for r in range(0, 128, 16):
                dist = jnp.maximum(pair[r : r + 16, :128], tiny)
                run = pair[r : r + 16, 128:]
                q = dist * lax.rsqrt(dist)
                fall = jnp.maximum(1.0 - q, 0.0)
                g = fall * fall * fall
                part = g * q * masses[n, r : r + 16]
                part = part[:8] + part[8:]
                total[j] = part if j not in total else total[j] + part
                high = g.astype(bf16)
                slopes[c, k, r : r + 16] = high
                slopes[c, k, 128 + r : 128 + r + 16] = (g - high.astype(f32)).astype(bf16)
                visc[c, k, r : r + 16] = g * jnp.minimum(run, 0.0) * (1.0 / (dist + 0.01))

        def reduce(j, k):
            c, n = group[j], picks[j][k]
            part = jnp.dot(columns[n], slopes[c, k], preferred_element_type=f32)
            sofar[j] = part if j not in sofar else sofar[j] + part
            if k == len(picks[j]) - 1:
                sums[c] = sofar[j]
                weighted[c] = total[j]

        pipelined(tiles, (geometry, terms, reduce))
        return 0

    over_cells(cells, some)


def prepare_force(tile, offsets, press, at, rhos, columns, gradients):
    table, mass = moments(tile, offsets)
    rho = press[0:1]
    weight = press[1:2]
    heavy = mass * table
    h1, h2, _ = split3(heavy)
    s1, s2, _ = split3(weight * heavy)
    m1, m2, _ = split3(mass)
    w1, w2, _ = split3(weight * mass)
    extra = rows_of(m1, m2, w1, w2)
    left = jnp.concatenate([h1, h2, s1, s2, extra, jnp.zeros_like(extra)], 0).astype(bf16)
    columns[at] = jnp.concatenate([left, left], 1)
    light = (mass / rho) * jnp.where(row_ids() < 3, table, 1.0)
    l1, l2, _ = split3(light)
    left = jnp.concatenate([l1, l2], 0).astype(bf16)
    gradients[at] = jnp.concatenate([left, left], 1)
    r1, r2, r3 = split3(rho)
    lanes = jnp.concatenate([rows_of(r1, r2, r3), jnp.zeros((tile_rows, 128), f32)], 0).T.astype(bf16)
    ids = lax.broadcasted_iota(jnp.int32, (16, 128), 0)
    rhos[at] = jnp.dot(lanes, jnp.where(ids < 3, 1.0, 0.0).astype(bf16), preferred_element_type=f32)


def force_pairs(cells, near, press_row, rhos, columns, gradients, slopes, visc, sums, pulls):
    def some(group):
        mixed, sofar, pulled = {}, {}, {}
        picks = [near(c) for c in group]
        mine = [press_row(c) for c in group]
        tiles = [(j, k) for j, c in enumerate(group) for k in range(len(near(c)))]

        def terms(j, k):
            c, n = group[j], picks[j][k]
            highs, lows = [], []
            for r in range(0, 128, 16):
                t = visc[c, k, r : r + 16] * (1.0 / (rhos[n, r : r + 16] + mine[j]))
                high = t.astype(bf16)
                highs.append(high)
                lows.append((t - high.astype(f32)).astype(bf16))
            mixed[j, k] = jnp.concatenate(highs + lows, 0)

        def reduce(j, k):
            c, n = group[j], picks[j][k]
            part = jnp.dot(columns[n], mixed.pop((j, k)), preferred_element_type=f32)
            pull = jnp.dot(gradients[n], slopes[c, k], preferred_element_type=f32)
            sofar[j] = part if j not in sofar else sofar[j] + part
            pulled[j] = pull if j not in pulled else pulled[j] + pull
            if k == len(picks[j]) - 1:
                sums[c] = sofar[j]
                pulls[c] = pulled[j]

        pipelined(tiles, (terms, reduce))
        return 0

    over_cells(cells, some)


def parts_of(c):
    return c // 4, (c // 2) % 2, c % 2


def flat(*pairs):
    at = 0
    for size, index in pairs:
        at = at * size + index
    return at


def near_own(c):
    return list(range(8))


def near_z(c):
    cx, cy, cz = parts_of(c)
    return [flat((2, cz), (2, x), (2, y)) for x in range(2) for y in range(2)]


def near_y(c):
    cx, cy, cz = parts_of(c)
    return [flat((2, cy), (2, x), (4, cz + dz)) for x in range(2) for dz in range(3)]


def near_x(c):
    cx, cy, cz = parts_of(c)
    return [flat((2, cx), (4, cy + dy), (4, cz + dz)) for dy in range(3) for dz in range(3)]


def place_own(e):
    x, y, z = parts_of(e)
    return x - 1, y - 1, z - 1


def place_z(e):
    side, x, y = parts_of(e)
    return x - 1, y - 1, 3 * side - 2


def place_y(e):
    return (e // 4) % 2 - 1, 3 * (e // 8) - 2, e % 4 - 2


def place_x(e):
    return 3 * (e // 16) - 2, (e // 4) % 4 - 2, e % 4 - 2


def offsets_of(place):
    return [jnp.asarray(v, jnp.int32).astype(f32) for v in place]


groups = {
    "own": (8, near_own, place_own, 8),
    "z": (8, near_z, place_z, 4),
    "y": (16, near_y, place_y, 6),
    "x": (32, near_x, place_x, 9),
}


def scratch_density(entries):
    return [
        pltpu.VMEM((entries, 128, feature_rows), bf16),
        pltpu.VMEM((entries, 128, 128), f32),
        pltpu.VMEM((entries, 32, 256), bf16),
    ]


def pair_outputs(count):
    return [
        shaped(8, count, 256, 128, kind=bf16),
        shaped(8, count, 128, 128),
        shaped(8, 32, 128),
        shaped(8, tile_rows, 128),
    ]


def call(body, outs, operands, specs=None, scratch=(), limit=24, name=None):
    return pl.pallas_call(
        body,
        out_shape=tuple(outs),
        in_specs=specs or [vmem] * len(operands),
        out_specs=tuple([vmem] * len(outs)),
        scratch_shapes=list(scratch),
        compiler_params=pltpu.CompilerParams(vmem_limit_bytes=limit << 20),
        name=name,
    )(*operands)


def take_side(before, refs, side, rest):
    if len(refs) == 1:
        one, two = refs[0][(0,) + rest], refs[0][(1,) + rest]
    else:
        one, two = refs[0][rest], refs[1][rest]
    return jnp.where(before, one, two) if side == 0 else jnp.where(before, two, one)


def send_shapes(axis, plane):
    if lax.axis_size(axis) == 2:
        return [shaped(2, *plane)]
    return [shaped(*plane), shaped(*plane)]


def put_sends(axis, refs, high, tile_at, rest):
    top, bottom = tile_at(1), tile_at(0)
    one, two = jnp.where(high, top, bottom), jnp.where(high, bottom, top)
    if len(refs) == 1:
        refs[0][(0,) + rest] = one
        refs[0][(1,) + rest] = two
    else:
        refs[0][rest] = one
        refs[1][rest] = two


def receive(axis, sends):
    if len(sends) == 1:
        return exchanged(axis, sends[0])
    return exchanged(axis, sends)


def pack_y(own, from_z, rows, name):
    sends = send_shapes("gy", (2, 4, rows, 128))
    n = len(from_z)

    def body(own_ref, *refs):
        got, out = refs[:n], refs[n:]
        high = first_sends_high("gy")
        before = first_gives_before("gz")
        for x in range(2):
            for e in range(4):

                def tile_at(y, x=x, e=e):
                    if 1 <= e <= 2:
                        return own_ref[x, y, e - 1]
                    return take_side(before, got, 0 if e == 0 else 1, (x, y))

                put_sends("gy", out, high, tile_at, (x, e))

    return call(body, sends, (own, *from_z), name=name, limit=4)


def pack_x(own, from_z, from_y, rows, name):
    sends = send_shapes("gx", (4, 4, rows, 128))
    n, m = len(from_z), len(from_y)

    def body(own_ref, *refs):
        got_z, got_y, out = refs[:n], refs[n : n + m], refs[n + m :]
        high = first_sends_high("gx")
        before_z = first_gives_before("gz")
        before_y = first_gives_before("gy")
        for a in range(4):
            for e in range(4):

                def tile_at(x, a=a, e=e):
                    if not 1 <= a <= 2:
                        return take_side(before_y, got_y, 0 if a == 0 else 1, (x, e))
                    if 1 <= e <= 2:
                        return own_ref[x, a - 1, e - 1]
                    return take_side(before_z, got_z, 0 if e == 0 else 1, (x, a - 1))

                put_sends("gx", out, high, tile_at, (a, e))

    return call(body, sends, (own, *from_z, *from_y), name=name, limit=4)


inner_dims = {"z": (2, 2), "y": (2, 4), "x": (4, 4)}


def entry_tile(group, before, refs, e, sides):
    a, b = inner_dims[group]
    return take_side(before, refs, sides, (e // b, e % b))


def density_own(own):
    entries, near, place, count = groups["own"]

    def body(own_ref, slopes, visc, sums, weighted, table_ref, feats, masses, columns):
        def one(c, _):
            x, y, z = parts_of(c)
            tile = own_ref[x, y, z]
            offsets = offsets_of(place(c))
            prepare(tile, offsets, c, feats, masses, columns)
            table, _mass = moments(tile, offsets)
            table_ref[c] = own_features(table)
            return 0

        lax.fori_loop(0, 8, one, 0, unroll=4)
        density_pairs(table_ref, 8, near, feats, masses, columns, slopes, visc, sums, weighted)

    outs = pair_outputs(count) + [shaped(8, feature_rows, 256, kind=bf16)]
    return call(body, outs, (own,), scratch=scratch_density(entries), name="density_own")


def density_halo(group, axis, received, own_feats):
    entries, near, place, count = groups[group]
    n = len(received)
    half = entries // 2

    def body(*refs):
        got, own_ref = refs[:n], refs[n]
        slopes, visc, sums, weighted, feats, masses, columns = refs[n + 1 :]
        before = first_gives_before(axis)
        for side in range(2):

            def one(e, _, side=side):
                tile = entry_tile(group, before, got, e, side)
                at = side * half + e
                prepare(tile, offsets_of(place(at)), at, feats, masses, columns)
                return 0

            lax.fori_loop(0, half, one, 0, unroll=4)
        density_pairs(own_ref, 8, near, feats, masses, columns, slopes, visc, sums, weighted)

    return call(
        body,
        pair_outputs(count),
        (*received, own_feats),
        scratch=scratch_density(entries),
        name="density_" + group,
    )


def pressure(own, alphas, counts, partials):
    sends = send_shapes("gz", (2, 2, 2, 128))
    outs = [shaped(2, 2, 2, 2, 128), shaped(2, 2, 2, 128), shaped(8, tile_rows, 128)] + sends
    n = len(partials)

    def body(counts_ref, alphas_ref, own_ref, *refs):
        pieces, (press, density, first), out = refs[:n], refs[n : n + 3], refs[n + 3 :]
        high = first_sends_high("gz")
        lanes = lax.broadcasted_iota(jnp.int32, (1, 128), 1)
        for x in range(2):
            for y in range(2):
                for z in range(2):
                    c = 4 * x + 2 * y + z
                    table, _mass = moments(own_ref[x, y, z], [float(v - 1) for v in (x, y, z)])
                    s = sum(p[c] for p in pieces[0::2])
                    gq = jnp.sum(sum(p[c] for p in pieces[1::2]), 0, keepdims=True)
                    t = s[0:8] + s[8:16]
                    m0 = s[16:17] + s[17:18]
                    pos, vel = table[0:3], table[3:6]
                    x_mx = jnp.sum(pos * t[0:3], 0, keepdims=True)
                    x_mv = jnp.sum(pos * t[3:6], 0, keepdims=True)
                    v_mx = jnp.sum(vel * t[0:3], 0, keepdims=True)
                    gr2 = t[6:7] + table[6:7] * m0 - 2.0 * x_mx
                    rho = kernel_norm * (m0 + 3.0 * gq - 4.0 * gr2)
                    div = -20.0 * kernel_norm * (t[7:8] + table[7:8] * m0 - x_mv - v_mx)
                    rho = jnp.where(lanes < counts_ref[x, y, z], rho, 1.0)
                    compress = jnp.maximum(div / rho, 0.0)
                    weight = alphas_ref[x, y, z : z + 1, :] * compress / (compress + 1.0)
                    press[x, y, z] = jnp.concatenate([rho, weight], 0)
                    density[x, y, z : z + 1, :] = rho
                    first[c] = jnp.concatenate(
                        [pos * m0 - t[0:3], div, jnp.zeros((tile_rows - 4, 128), f32)], 0
                    )
        for x in range(2):
            for y in range(2):
                put_sends("gz", out, high, lambda z, x=x, y=y: press[x, y, z], (x, y))

    operands = (counts, alphas, own, *partials)
    specs = [smem] + [vmem] * (len(operands) - 1)
    return call(body, outs, operands, specs=specs, name="pressure", limit=8)


def scratch_force(entries):
    return [
        pltpu.VMEM((entries, 128, 128), f32),
        pltpu.VMEM((entries, 48, 256), bf16),
        pltpu.VMEM((entries, 16, 256), bf16),
    ]


def force_outputs():
    return [shaped(8, 48, 128), shaped(8, 16, 128)]


def force_own(own, press, kept):
    entries, near, place, count = groups["own"]

    def body(own_ref, press_ref, slopes, visc, sums, pulls, rhos, columns, gradients):
        def one(c, _):
            x, y, z = parts_of(c)
            prepare_force(
                own_ref[x, y, z], offsets_of(place(c)), press_ref[x, y, z], c, rhos, columns, gradients
            )
            return 0

        lax.fori_loop(0, 8, one, 0, unroll=4)

        def mine(c):
            x, y, z = parts_of(c)
            return press_ref[x, y, z, 0:1]

        force_pairs(8, near, mine, rhos, columns, gradients, slopes, visc, sums, pulls)

    return call(
        body,
        force_outputs(),
        (own, press, *kept),
        scratch=scratch_force(entries),
        name="force_own",
    )


def force_halo(group, axis, received, press_received, press, kept):
    entries, near, place, count = groups[group]
    n = len(received)
    half = entries // 2

    def body(*refs):
        got, got_press, press_ref = refs[:n], refs[n : 2 * n], refs[2 * n]
        slopes, visc, sums, pulls, rhos, columns, gradients = refs[2 * n + 1 :]
        before = first_gives_before(axis)
        for side in range(2):

            def one(e, _, side=side):
                tile = entry_tile(group, before, got, e, side)
                fields = entry_tile(group, before, got_press, e, side)
                at = side * half + e
                prepare_force(tile, offsets_of(place(at)), fields, at, rhos, columns, gradients)
                return 0

            lax.fori_loop(0, half, one, 0, unroll=4)

        def mine(c):
            x, y, z = parts_of(c)
            return press_ref[x, y, z, 0:1]

        force_pairs(8, near, mine, rhos, columns, gradients, slopes, visc, sums, pulls)

    return call(
        body,
        force_outputs(),
        (*received, *press_received, press, *kept),
        scratch=scratch_force(entries),
        name="force_" + group,
    )


def finish(own, press, first, counts, partials):
    outs = [shaped(3, 2, 2, 2, 128), shaped(2, 2, 2, 128)]
    n = len(partials)

    def body(counts_ref, own_ref, press_ref, first_ref, *refs):
        pieces, (accel, heating) = refs[:n], refs[n:]
        lanes = lax.broadcasted_iota(jnp.int32, (1, 128), 1)
        for x in range(2):
            for y in range(2):
                for z in range(2):
                    c = 4 * x + 2 * y + z
                    table, _mass = moments(own_ref[x, y, z], [float(v - 1) for v in (x, y, z)])
                    u = sum(p[c] for p in pieces[0::2])
                    v = sum(p[c] for p in pieces[1::2])
                    plain, scaled = u[0:8] + u[8:16], u[16:24] + u[24:32]
                    a0, b0 = u[32:33] + u[33:34], u[34:35] + u[35:36]
                    g = v[0:8] + v[8:16]
                    rho, weight = press_ref[x, y, z, 0:1], press_ref[x, y, z, 1:2]
                    inverse = 1.0 / rho
                    mixed = weight * plain + scaled
                    zero = weight * a0 + b0
                    pos, vel = table[0:3], table[3:6]
                    total = (
                        inverse * first_ref[c, 0:3]
                        + (pos * g[3:4] - g[0:3])
                        - (pos * zero - mixed[0:3])
                    )
                    live = jnp.where(lanes < counts_ref[x, y, z], 1.0, 0.0)
                    push = (20.0 * kernel_norm) * live * total
                    work = (
                        mixed[7:8]
                        + table[7:8] * zero
                        - jnp.sum(pos * mixed[3:6], 0, keepdims=True)
                        - jnp.sum(vel * mixed[0:3], 0, keepdims=True)
                    )
                    warm = live * (first_ref[c, 3:4] * inverse + (10.0 * kernel_norm) * work)
                    for i in range(3):
                        accel[i, x, y, z : z + 1, :] = push[i : i + 1]
                    heating[x, y, z : z + 1, :] = warm

    operands = (counts, own, press, first, *partials)
    specs = [smem] + [vmem] * (len(operands) - 1)
    return call(body, outs, operands, specs=specs, name="finish", limit=8)


def gather_own(positions, velocities, masses, counts):
    sends = send_shapes("gz", (2, 2, tile_rows, 128))

    def body(counts_ref, pos, vel, mass, own, *out):
        high = first_sends_high("gz")
        lanes = lax.broadcasted_iota(jnp.int32, (1, 128), 1)
        for x in range(2):
            for y in range(2):
                for z in range(2):
                    here = mass[x, y, z : z + 1, :] * jnp.where(lanes < counts_ref[x, y, z], 1.0, 0.0)
                    own[x, y, z] = rows_of(
                        *(pos[i, x, y, z : z + 1, :] for i in range(3)),
                        *(vel[i, x, y, z : z + 1, :] for i in range(3)),
                        here,
                    )
        for x in range(2):
            for y in range(2):
                put_sends("gz", out, high, lambda z, x=x, y=y: own[x, y, z], (x, y))

    outs = [shaped(2, 2, 2, tile_rows, 128)] + sends
    operands = (counts, positions, velocities, masses)
    return call(body, outs, operands, specs=[smem] + [vmem] * 3, name="gather_own", limit=4)


def per_block(positions, velocities, masses, alphas, counts):
    own, *sends = gather_own(positions, velocities, masses, counts)
    from_z = receive("gz", sends)
    *kept_own, sums_own, weighted_own, own_feats = density_own(own)
    from_y = receive("gy", pack_y(own, from_z, tile_rows, "pack_y"))
    *kept_z, sums_z, weighted_z = density_halo("z", "gz", from_z, own_feats)
    from_x = receive("gx", pack_x(own, from_z, from_y, tile_rows, "pack_x"))
    *kept_y, sums_y, weighted_y = density_halo("y", "gy", from_y, own_feats)
    *kept_x, sums_x, weighted_x = density_halo("x", "gx", from_x, own_feats)
    partials = (sums_own, weighted_own, sums_z, weighted_z, sums_y, weighted_y, sums_x, weighted_x)
    press, density, first, *sends = pressure(own, alphas, counts, partials)
    press_z = receive("gz", sends)
    forces = list(force_own(own, press, kept_own))
    press_y = receive("gy", pack_y(press, press_z, 2, "pack_press_y"))
    forces += force_halo("z", "gz", from_z, press_z, press, kept_z)
    press_x = receive("gx", pack_x(press, press_z, press_y, 2, "pack_press_x"))
    forces += force_halo("y", "gy", from_y, press_y, press, kept_y)
    forces += force_halo("x", "gx", from_x, press_x, press, kept_x)
    accel, heating = finish(own, press, first, counts, forces)
    return density, accel, heating


neighbour_shifts = [
    (shift_x, shift_y, shift_z)
    for shift_x in (-1, 0, 1)
    for shift_y in (-1, 0, 1)
    for shift_z in (-1, 0, 1)
]


def extended(shard, sides, width):
    for axis, dim in sides:
        peers, length = (lax.axis_size(axis), shard.shape[dim])
        up = [(i, (i + 1) % peers) for i in range(peers)]
        down = [(j, i) for i, j in up]
        last = lax.slice_in_dim(shard, length - width, length, axis=dim)
        leading = lax.slice_in_dim(shard, 0, width, axis=dim)
        before = lax.ppermute(last, axis, up)
        after = lax.ppermute(leading, axis, down)
        shard = jnp.concatenate([before, shard, after], axis=dim)
    return shard


def pair_geometry(own_rows, neighbour, cell_shift):
    offset_parts = [
        own_rows[axis_id][:, :, None] - neighbour[axis_id][:, None, :] - float(cell_shift[axis_id])
        for axis_id in range(3)
    ]
    dist_sq = (
        offset_parts[0] * offset_parts[0]
        + offset_parts[1] * offset_parts[1]
        + offset_parts[2] * offset_parts[2]
    )
    scaled = jnp.minimum(jnp.sqrt(dist_sq), 1.0)
    falloff = 1.0 - scaled
    kernel_value = kernel_norm * falloff**4 * (1.0 + 4.0 * scaled)
    kernel_slope = -20.0 * kernel_norm * falloff**3
    approach = sum(
        (
            (own_rows[3 + axis_id][:, :, None] - neighbour[3 + axis_id][:, None, :])
            * offset_parts[axis_id]
            for axis_id in range(3)
        )
    )
    return (offset_parts, dist_sq, kernel_value, kernel_slope, approach)


def density_terms(own_rows, neighbour, cell_shift):
    offset_parts, dist_sq, kernel_value, kernel_slope, approach = pair_geometry(
        own_rows, neighbour, cell_shift
    )
    other_mass = neighbour[6][:, None, :]
    return (
        jnp.sum(other_mass * kernel_value, -1),
        jnp.sum(other_mass * kernel_slope * approach, -1),
    )


def force_terms(own_rows, neighbour, cell_shift):
    offset_parts, dist_sq, kernel_value, kernel_slope, approach = pair_geometry(
        own_rows, neighbour, cell_shift
    )
    rho_own = own_rows[7][:, :, None]
    rho_other = neighbour[7][:, None, :]
    converge = jnp.minimum(approach, 0.0) / (dist_sq + 0.01)
    viscous = (
        -(own_rows[8][:, :, None] + neighbour[8][:, None, :]) * converge / (rho_own + rho_other)
    )
    mslope = neighbour[6][:, None, :] * kernel_slope
    pair_force = mslope * (1.0 / rho_own + 1.0 / rho_other + viscous)
    accel_terms = jnp.stack(
        [-jnp.sum(pair_force * offset_parts[axis_id], -1) for axis_id in range(3)], 0
    )
    heating = jnp.sum(mslope * (1.0 / rho_own + 0.5 * viscous) * approach, -1)
    return (accel_terms, heating)


def switch_fields(density, div_sum, live_rows, weights):
    rho_live = jnp.where(live_rows > 0, density, 1.0)
    compress = jnp.maximum(div_sum / rho_live, 0.0)
    return jnp.stack([rho_live, weights * compress / (compress + 1.0)], 0)


def sweep(terms, padded):
    count = padded.shape[0]
    slot_count = padded.shape[-1]
    span_x = padded.shape[1] - 2
    span_y = padded.shape[2] - 2
    span_z = padded.shape[3] - 2
    own_rows = padded[:, 1 : span_x + 1, 1 : span_y + 1, 1 : span_z + 1].reshape(
        count, -1, slot_count
    )
    totals = None
    for cell_shift in neighbour_shifts:
        neighbour = padded[
            :,
            1 + cell_shift[0] : 1 + cell_shift[0] + span_x,
            1 + cell_shift[1] : 1 + cell_shift[1] + span_y,
            1 + cell_shift[2] : 1 + cell_shift[2] + span_z,
        ]
        result = terms(own_rows, neighbour.reshape(count, -1, slot_count), cell_shift)
        totals = (
            result
            if totals is None
            else jax.tree.map(lambda left, right: left + right, totals, result)
        )
    return totals


def per_device(positions, velocities, masses, alphas, counts):
    slot_count = positions.shape[-1]
    cell_shape = positions.shape[1:4]
    occupied = (
        jnp.arange(slot_count, dtype=jnp.int32)[None, None, None, :] < counts[..., None]
    ).astype(jnp.float32)
    live_mass = masses * occupied
    carried = jnp.concatenate([positions, velocities, live_mass[None]], 0)
    padded = extended(carried, (("gx", 1), ("gy", 2), ("gz", 3)), 1)
    density, div_sum = sweep(density_terms, padded)
    live_rows = occupied.reshape(-1, slot_count)
    weights = alphas.reshape(-1, slot_count)
    pressure_fields = switch_fields(density, div_sum, live_rows, weights).reshape(
        (2,) + cell_shape + (slot_count,)
    )
    own_density = pressure_fields[0]
    pressure_pad = extended(pressure_fields, (("gx", 1), ("gy", 2), ("gz", 3)), 1)
    fields = jnp.concatenate([padded, pressure_pad], 0)
    accel_total, heat_total = sweep(force_terms, fields)
    acceleration = accel_total.reshape((3,) + cell_shape + (slot_count,)) * occupied[None]
    heating = heat_total.reshape(cell_shape + (slot_count,)) * occupied
    return (own_density, acceleration, heating)


def per_device_any(positions, velocities, masses, alphas, counts):
    if positions.shape[1:] == (2, 2, 2, 128):
        return per_block(positions, velocities, masses, alphas, counts)
    return per_device(positions, velocities, masses, alphas, counts)


def solution(mesh):
    return jax.shard_map(
        per_device_any,
        mesh=mesh,
        in_specs=(
            P(None, "gx", "gy", "gz", None),
            P(None, "gx", "gy", "gz", None),
            P("gx", "gy", "gz", None),
            P("gx", "gy", "gz", None),
            P("gx", "gy", "gz"),
        ),
        out_specs=(
            P("gx", "gy", "gz", None),
            P(None, "gx", "gy", "gz", None),
            P("gx", "gy", "gz", None),
        ),
        check_vma=False,
    )
```

```python
import math

import jax
import jax.numpy as jnp
from jax import lax
from jax.experimental import pallas as pl
from jax.experimental.pallas import tpu as pltpu
from jax.sharding import PartitionSpec as P


f32 = jnp.float32
bf16 = jnp.bfloat16
kernel_norm = 21.0 / (2.0 * math.pi)
tile_rows = 8
feature_rows = 64
tiny = 1e-12
together = 4
strip = 128

vmem = pl.BlockSpec(memory_space=pltpu.VMEM)


def shaped(*dims, kind=f32):
    return jax.ShapeDtypeStruct(dims, kind)


def paired(axis):
    return lax.axis_size(axis) % 2 == 0


def first_sends_high(axis):
    return lax.axis_index(axis) % 2 == 0 if paired(axis) else lax.axis_index(axis) >= 0


def first_gives_before(axis):
    return lax.axis_index(axis) % 2 == 1 if paired(axis) else lax.axis_index(axis) >= 0


def routes(axis):
    peers = lax.axis_size(axis)
    if peers % 2 == 0:
        first = [(i, i + 1 if i % 2 == 0 else i - 1) for i in range(peers)]
        second = [(i, (i - 1 if i % 2 == 0 else i + 1) % peers) for i in range(peers)]
    else:
        first = [(i, (i + 1) % peers) for i in range(peers)]
        second = [(i, (i - 1) % peers) for i in range(peers)]
    return first, second


def split3(value):
    high = value.astype(bf16).astype(f32)
    rest = value - high
    middle = rest.astype(bf16).astype(f32)
    return high, middle, rest - middle


def row_ids():
    return lax.broadcasted_iota(jnp.int32, (tile_rows, 128), 0)


def rows_of(*rows):
    ids = row_ids()
    out = jnp.zeros((tile_rows, 128), f32)
    for place, row in enumerate(rows):
        out = jnp.where(ids == place, row, out)
    return out


def moments(tile, offsets):
    ids = row_ids()
    shift = jnp.where(ids == 0, offsets[0], jnp.where(ids == 1, offsets[1], jnp.where(ids == 2, offsets[2], 0.0)))
    moved = tile + shift
    x, y, z, vx, vy, vz = (moved[i : i + 1] for i in range(6))
    sq = x * x + y * y + z * z
    xv = x * vx + y * vy + z * vz
    return jnp.where(ids == 6, sq, jnp.where(ids == 7, xv, moved)), tile[6:7]


def other_features(table, mass):
    p1, p2, p3 = split3(table)
    m1, m2, m3 = split3(mass)
    extra = rows_of(1.0, 1.0, 1.0, m1, m2, m3)
    lanes = jnp.concatenate([p1, p1, p1, p2, p2, p3, extra, jnp.zeros_like(extra)], 0)
    return lanes.T.astype(bf16)


def own_features(table):
    ids = row_ids()
    sq = split3(table[6:7])
    xv = split3(table[7:8])
    down = pltpu.roll(table, 3, 0)
    up = pltpu.roll(table, 5, 0)
    left = jnp.where(ids < 3, -2.0 * table, jnp.where(ids == 6, 1.0, 0.0))
    right = jnp.where(ids < 3, -up, jnp.where(ids < 6, -down, jnp.where(ids == 7, 1.0, 0.0)))
    halves = []
    for part, fixed in ((left, sq), (right, xv)):
        q1, q2, q3 = split3(part)
        extra = rows_of(*fixed)
        halves.append(jnp.concatenate([q1, q2, q3, q1, q2, q1, extra, jnp.zeros_like(extra)], 0))
    return jnp.concatenate(halves, 1).astype(bf16)


def mass_columns(table, mass):
    weighted = mass * table
    w1, w2, _ = split3(weighted)
    m1, m2, _ = split3(mass)
    extra = rows_of(m1, m2)
    left = jnp.concatenate([w1, w2, extra, jnp.zeros_like(extra)], 0).astype(bf16)
    return jnp.concatenate([left, left], 1)


def picker(first_row):
    ids = lax.broadcasted_iota(jnp.int32, (feature_rows, 128), 0)
    return jnp.where((ids >= first_row) & (ids < first_row + 3), 1.0, 0.0).astype(bf16)


def prepare(tile, offsets, at, feats, masses, columns):
    table, mass = moments(tile, offsets)
    lanes = other_features(table, mass)
    feats[at] = lanes
    masses[at] = jnp.dot(lanes, picker(51), preferred_element_type=f32)
    columns[at] = mass_columns(table, mass)


def pipelined(tiles, stages):
    for step in range(len(tiles) + len(stages) - 1):
        for lag, stage in enumerate(stages):
            if 0 <= step - lag < len(tiles):
                stage(*tiles[step - lag])


def idle(*tile):
    pass


def over_cells(cells, body):
    lax.fori_loop(0, cells // together, lambda i, _: body([i * together + j for j in range(together)]), 0)


def density_pairs(own, cells, near, feats, masses, columns, slopes, visc, sums, weighted):
    def some(group):
        both, total, sofar = {}, {}, {}
        picks = [near(c) for c in group]
        tiles = [
            (j, k, h) for j in range(len(group)) for k in range(len(picks[j])) for h in range(0, 128, strip)
        ]

        def geometry(j, k, h):
            left = feats[picks[j][k], h : h + strip]
            both[j, k, h] = jnp.dot(left, own[group[j]], preferred_element_type=f32)

        def terms(j, k, h):
            c, n = group[j], picks[j][k]
            pair = both.pop((j, k, h))
            for low in range(0, strip, 16):
                r = h + low
                dist = jnp.maximum(pair[low : low + 16, :128], tiny)
                run = pair[low : low + 16, 128:]
                q = dist * lax.rsqrt(dist)
                fall = jnp.maximum(1.0 - q, 0.0)
                g = fall * fall * fall
                part = g * q * masses[n, r : r + 16]
                part = part[:8] + part[8:]
                total[j] = part if j not in total else total[j] + part
                high = g.astype(bf16)
                slopes[c, k, r : r + 16] = high
                slopes[c, k, 128 + r : 128 + r + 16] = (g - high.astype(f32)).astype(bf16)
                visc[c, k, r : r + 16] = g * jnp.minimum(run, 0.0) * (1.0 / (dist + 0.01))

        def reduce(j, k, h):
            if h + strip < 128:
                return
            c, n = group[j], picks[j][k]
            part = jnp.dot(columns[n], slopes[c, k], preferred_element_type=f32)
            sofar[j] = part if j not in sofar else sofar[j] + part
            if k == len(picks[j]) - 1:
                sums[c] = sofar[j]
                weighted[c] = total[j]

        pipelined(tiles, (geometry, idle, terms, idle, reduce))
        return 0

    over_cells(cells, some)


def prepare_force(tile, offsets, press, at, rhos, columns, gradients):
    table, mass = moments(tile, offsets)
    rho = press[0:1]
    weight = press[1:2]
    heavy = mass * table
    h1, h2, _ = split3(heavy)
    s1, s2, _ = split3(weight * heavy)
    m1, m2, _ = split3(mass)
    w1, w2, _ = split3(weight * mass)
    extra = rows_of(m1, m2, w1, w2)
    left = jnp.concatenate([h1, h2, s1, s2, extra, jnp.zeros_like(extra)], 0).astype(bf16)
    columns[at] = jnp.concatenate([left, left], 1)
    light = (mass / rho) * jnp.where(row_ids() < 3, table, 1.0)
    l1, l2, _ = split3(light)
    left = jnp.concatenate([l1, l2], 0).astype(bf16)
    gradients[at] = jnp.concatenate([left, left], 1)
    r1, r2, r3 = split3(rho)
    lanes = jnp.concatenate([rows_of(r1, r2, r3), jnp.zeros((tile_rows, 128), f32)], 0).T.astype(bf16)
    ids = lax.broadcasted_iota(jnp.int32, (16, 128), 0)
    rhos[at] = jnp.dot(lanes, jnp.where(ids < 3, 1.0, 0.0).astype(bf16), preferred_element_type=f32)


def force_pairs(cells, near, press_row, rhos, columns, gradients, slopes, visc, sums, pulls):
    def some(group):
        mixed, sofar, pulled = {}, {}, {}
        picks = [near(c) for c in group]
        mine = [press_row(c) for c in group]
        tiles = [(j, k) for j, c in enumerate(group) for k in range(len(near(c)))]

        def terms(j, k):
            c, n = group[j], picks[j][k]
            highs, lows = [], []
            for r in range(0, 128, 16):
                t = visc[c, k, r : r + 16] * (1.0 / (rhos[n, r : r + 16] + mine[j]))
                high = t.astype(bf16)
                highs.append(high)
                lows.append((t - high.astype(f32)).astype(bf16))
            mixed[j, k] = jnp.concatenate(highs + lows, 0)

        def reduce(j, k):
            c, n = group[j], picks[j][k]
            part = jnp.dot(columns[n], mixed.pop((j, k)), preferred_element_type=f32)
            pull = jnp.dot(gradients[n], slopes[c, k], preferred_element_type=f32)
            sofar[j] = part if j not in sofar else sofar[j] + part
            pulled[j] = pull if j not in pulled else pulled[j] + pull
            if k == len(picks[j]) - 1:
                sums[c] = sofar[j]
                pulls[c] = pulled[j]

        pipelined(tiles, (terms, reduce))
        return 0

    over_cells(cells, some)


def parts_of(c):
    return c // 4, (c // 2) % 2, c % 2


def flat(*pairs):
    at = 0
    for size, index in pairs:
        at = at * size + index
    return at


def near_own(c):
    return list(range(8))


def near_z(c):
    _, _, cz = parts_of(c)
    return [flat((2, cz), (2, x), (2, y)) for x in range(2) for y in range(2)]


def near_y(c):
    _, cy, cz = parts_of(c)
    return [flat((2, cy), (2, x), (4, cz + dz)) for x in range(2) for dz in range(3)]


def near_x(c):
    cx, cy, cz = parts_of(c)
    return [flat((2, cx), (4, cy + dy), (4, cz + dz)) for dy in range(3) for dz in range(3)]


def place_own(e):
    x, y, z = parts_of(e)
    return x - 1, y - 1, z - 1


def place_z(e):
    side, x, y = parts_of(e)
    return x - 1, y - 1, 3 * side - 2


def place_y(e):
    return (e // 4) % 2 - 1, 3 * (e // 8) - 2, e % 4 - 2


def place_x(e):
    return 3 * (e // 16) - 2, (e // 4) % 4 - 2, e % 4 - 2


def offsets_of(place):
    return [jnp.asarray(v, jnp.int32).astype(f32) for v in place]


groups = {
    "own": (8, near_own, place_own, 8),
    "z": (8, near_z, place_z, 4),
    "y": (16, near_y, place_y, 6),
    "x": (32, near_x, place_x, 9),
}


def scratch_density(entries):
    return [
        pltpu.VMEM((entries, 128, feature_rows), bf16),
        pltpu.VMEM((entries, 128, 128), f32),
        pltpu.VMEM((entries, 32, 256), bf16),
    ]


def pair_outputs(count):
    return [
        shaped(8, count, 256, 128, kind=bf16),
        shaped(8, count, 128, 128),
        shaped(8, 32, 128),
        shaped(8, tile_rows, 128),
    ]


def call(body, outs, operands, specs=None, scratch=(), limit=24):
    return pl.pallas_call(
        body,
        out_shape=tuple(outs),
        in_specs=specs or [vmem] * len(operands),
        out_specs=tuple([vmem] * len(outs)),
        scratch_shapes=list(scratch),
        compiler_params=pltpu.CompilerParams(vmem_limit_bytes=limit << 20),
    )(*operands)


def take_side(before, refs, side, rest):
    if len(refs) == 1:
        one, two = refs[0][(0,) + rest], refs[0][(1,) + rest]
    else:
        one, two = refs[0][rest], refs[1][rest]
    return jnp.where(before, one, two) if side == 0 else jnp.where(before, two, one)


def send_shapes(axis, plane):
    if lax.axis_size(axis) == 2:
        return [shaped(2, *plane)]
    return [shaped(*plane), shaped(*plane)]


def put_sends(refs, high, tile_at, rest):
    top, bottom = tile_at(1), tile_at(0)
    one, two = jnp.where(high, top, bottom), jnp.where(high, bottom, top)
    if len(refs) == 1:
        refs[0][(0,) + rest] = one
        refs[0][(1,) + rest] = two
    else:
        refs[0][rest] = one
        refs[1][rest] = two


def receive(axis, sends):
    first, second = routes(axis)
    ways = (first,) if len(sends) == 1 else (first, second)
    got = []
    for send, way in zip(sends, ways):
        got.append(lax.ppermute(send, axis, way))
    return tuple(got)


def pack_y(own, from_z, rows):
    sends = send_shapes("gy", (2, 4, rows, 128))
    n = len(from_z)

    def body(own_ref, *refs):
        got, out = refs[:n], refs[n:]
        high = first_sends_high("gy")
        before = first_gives_before("gz")
        for x in range(2):
            for e in range(4):

                def tile_at(y, x=x, e=e):
                    if 1 <= e <= 2:
                        return own_ref[x, y, e - 1]
                    return take_side(before, got, 0 if e == 0 else 1, (x, y))

                put_sends(out, high, tile_at, (x, e))

    return call(body, sends, (own, *from_z), limit=4)


def pack_x(own, from_z, from_y, rows):
    sends = send_shapes("gx", (4, 4, rows, 128))
    n, m = len(from_z), len(from_y)

    def body(own_ref, *refs):
        got_z, got_y, out = refs[:n], refs[n : n + m], refs[n + m :]
        high = first_sends_high("gx")
        before_z = first_gives_before("gz")
        before_y = first_gives_before("gy")
        for a in range(4):
            for e in range(4):

                def tile_at(x, a=a, e=e):
                    if not 1 <= a <= 2:
                        return take_side(before_y, got_y, 0 if a == 0 else 1, (x, e))
                    if 1 <= e <= 2:
                        return own_ref[x, a - 1, e - 1]
                    return take_side(before_z, got_z, 0 if e == 0 else 1, (x, a - 1))

                put_sends(out, high, tile_at, (a, e))

    return call(body, sends, (own, *from_z, *from_y), limit=4)


inner_dims = {"z": (2, 2), "y": (2, 4), "x": (4, 4)}


def entry_tile(group, before, refs, e, sides):
    _, b = inner_dims[group]
    return take_side(before, refs, sides, (e // b, e % b))


def density_own(own):
    entries, near, place, count = groups["own"]

    def body(own_ref, slopes, visc, sums, weighted, table_ref, feats, masses, columns):
        def one(c, _):
            x, y, z = parts_of(c)
            tile = own_ref[x, y, z]
            offsets = offsets_of(place(c))
            prepare(tile, offsets, c, feats, masses, columns)
            table, _ = moments(tile, offsets)
            table_ref[c] = own_features(table)
            return 0

        lax.fori_loop(0, 8, one, 0, unroll=4)
        density_pairs(table_ref, 8, near, feats, masses, columns, slopes, visc, sums, weighted)

    outs = pair_outputs(count) + [shaped(8, feature_rows, 256, kind=bf16)]
    return call(body, outs, (own,), scratch=scratch_density(entries))


def density_halo(group, axis, received, own_feats):
    entries, near, place, count = groups[group]
    n = len(received)
    half = entries // 2

    def body(*refs):
        got, own_ref = refs[:n], refs[n]
        slopes, visc, sums, weighted, feats, masses, columns = refs[n + 1 :]
        before = first_gives_before(axis)
        for side in range(2):

            def one(e, _, side=side):
                tile = entry_tile(group, before, got, e, side)
                at = side * half + e
                prepare(tile, offsets_of(place(at)), at, feats, masses, columns)
                return 0

            lax.fori_loop(0, half, one, 0, unroll=4)
        density_pairs(own_ref, 8, near, feats, masses, columns, slopes, visc, sums, weighted)

    return call(body, pair_outputs(count), (*received, own_feats), scratch=scratch_density(entries))


def pressure(own, partials):
    sends = send_shapes("gz", (2, 2, 2, 128))
    outs = [shaped(2, 2, 2, 2, 128), shaped(8, tile_rows, 128)] + sends
    n = len(partials)

    def body(own_ref, *refs):
        pieces, (press, first), out = refs[:n], refs[n : n + 2], refs[n + 2 :]
        high = first_sends_high("gz")
        for x in range(2):
            for y in range(2):
                for z in range(2):
                    c = 4 * x + 2 * y + z
                    table, mass = moments(own_ref[x, y, z], [float(v - 1) for v in (x, y, z)])
                    s = sum(p[c] for p in pieces[0::2])
                    gq = jnp.sum(sum(p[c] for p in pieces[1::2]), 0, keepdims=True)
                    t = s[0:8] + s[8:16]
                    m0 = s[16:17] + s[17:18]
                    pos, vel = table[0:3], table[3:6]
                    x_mx = jnp.sum(pos * t[0:3], 0, keepdims=True)
                    x_mv = jnp.sum(pos * t[3:6], 0, keepdims=True)
                    v_mx = jnp.sum(vel * t[0:3], 0, keepdims=True)
                    gr2 = t[6:7] + table[6:7] * m0 - 2.0 * x_mx
                    rho = kernel_norm * (m0 + 3.0 * gq - 4.0 * gr2)
                    div = -20.0 * kernel_norm * (t[7:8] + table[7:8] * m0 - x_mv - v_mx)
                    rho = jnp.where(mass > 0.0, rho, 1.0)
                    compress = jnp.maximum(div / rho, 0.0)
                    weight = own_ref[x, y, z, 7:8] * compress / (compress + 1.0)
                    press[x, y, z] = jnp.concatenate([rho, weight], 0)
                    first[c] = jnp.concatenate(
                        [pos * m0 - t[0:3], div, jnp.zeros((tile_rows - 4, 128), f32)], 0
                    )
        for x in range(2):
            for y in range(2):
                put_sends(out, high, lambda z, x=x, y=y: press[x, y, z], (x, y))

    return call(body, outs, (own, *partials), limit=8)


def scratch_force(entries):
    return [
        pltpu.VMEM((entries, 128, 128), f32),
        pltpu.VMEM((entries, 48, 256), bf16),
        pltpu.VMEM((entries, 16, 256), bf16),
    ]


def force_outputs():
    return [shaped(8, 48, 128), shaped(8, 16, 128)]


def force_own(own, press, kept):
    entries, near, place, _ = groups["own"]

    def body(own_ref, press_ref, slopes, visc, sums, pulls, rhos, columns, gradients):
        def one(c, _):
            x, y, z = parts_of(c)
            prepare_force(
                own_ref[x, y, z], offsets_of(place(c)), press_ref[x, y, z], c, rhos, columns, gradients
            )
            return 0

        lax.fori_loop(0, 8, one, 0, unroll=4)

        def mine(c):
            x, y, z = parts_of(c)
            return press_ref[x, y, z, 0:1]

        force_pairs(8, near, mine, rhos, columns, gradients, slopes, visc, sums, pulls)

    return call(body, force_outputs(), (own, press, *kept), scratch=scratch_force(entries))


def force_halo(group, axis, received, press_received, press, kept):
    entries, near, place, _ = groups[group]
    n = len(received)
    half = entries // 2

    def body(*refs):
        got, got_press, press_ref = refs[:n], refs[n : 2 * n], refs[2 * n]
        slopes, visc, sums, pulls, rhos, columns, gradients = refs[2 * n + 1 :]
        before = first_gives_before(axis)
        for side in range(2):

            def one(e, _, side=side):
                tile = entry_tile(group, before, got, e, side)
                fields = entry_tile(group, before, got_press, e, side)
                at = side * half + e
                prepare_force(tile, offsets_of(place(at)), fields, at, rhos, columns, gradients)
                return 0

            lax.fori_loop(0, half, one, 0, unroll=4)

        def mine(c):
            x, y, z = parts_of(c)
            return press_ref[x, y, z, 0:1]

        force_pairs(8, near, mine, rhos, columns, gradients, slopes, visc, sums, pulls)

    return call(
        body,
        force_outputs(),
        (*received, *press_received, press, *kept),
        scratch=scratch_force(entries),
    )


def finish(own, press, first, partials):
    outs = [shaped(2, 2, 2, 128), shaped(3, 2, 2, 2, 128), shaped(2, 2, 2, 128)]
    n = len(partials)

    def body(own_ref, press_ref, first_ref, *refs):
        pieces, (density, accel, heating) = refs[:n], refs[n:]
        for x in range(2):
            for y in range(2):
                for z in range(2):
                    c = 4 * x + 2 * y + z
                    table, mass = moments(own_ref[x, y, z], [float(v - 1) for v in (x, y, z)])
                    u = sum(p[c] for p in pieces[0::2])
                    v = sum(p[c] for p in pieces[1::2])
                    plain, scaled = u[0:8] + u[8:16], u[16:24] + u[24:32]
                    a0, b0 = u[32:33] + u[33:34], u[34:35] + u[35:36]
                    g = v[0:8] + v[8:16]
                    rho, weight = press_ref[x, y, z, 0:1], press_ref[x, y, z, 1:2]
                    inverse = 1.0 / rho
                    mixed = weight * plain + scaled
                    zero = weight * a0 + b0
                    pos, vel = table[0:3], table[3:6]
                    total = (
                        inverse * first_ref[c, 0:3]
                        + (pos * g[3:4] - g[0:3])
                        - (pos * zero - mixed[0:3])
                    )
                    live = jnp.where(mass > 0.0, 1.0, 0.0)
                    push = (20.0 * kernel_norm) * live * total
                    work = (
                        mixed[7:8]
                        + table[7:8] * zero
                        - jnp.sum(pos * mixed[3:6], 0, keepdims=True)
                        - jnp.sum(vel * mixed[0:3], 0, keepdims=True)
                    )
                    warm = live * (first_ref[c, 3:4] * inverse + (10.0 * kernel_norm) * work)
                    density[x, y, z : z + 1, :] = rho
                    for i in range(3):
                        accel[i, x, y, z : z + 1, :] = push[i : i + 1]
                    heating[x, y, z : z + 1, :] = warm

    return call(body, outs, (own, press, first, *partials), limit=8)


def gather_own(fields):
    sends = send_shapes("gz", (2, 2, tile_rows, 128))

    def body(fields_ref, own, *out):
        high = first_sends_high("gz")
        for x in range(2):
            for y in range(2):
                for z in range(2):
                    own[x, y, z] = rows_of(*(fields_ref[i, x, y, z : z + 1, :] for i in range(tile_rows)))
        for x in range(2):
            for y in range(2):
                put_sends(out, high, lambda z, x=x, y=y: own[x, y, z], (x, y))

    return call(body, [shaped(2, 2, 2, tile_rows, 128)] + sends, (fields,), limit=4)


def per_block(positions, velocities, masses, alphas, counts):
    slots = lax.broadcasted_iota(jnp.int32, masses.shape, 3)
    live_mass = jnp.where(slots < counts[..., None], masses, 0.0)
    own, *sends = gather_own(jnp.concatenate([positions, velocities, live_mass[None], alphas[None]], 0))
    from_z = receive("gz", sends)
    *kept_own, sums_own, weighted_own, own_feats = density_own(own)
    from_y = receive("gy", pack_y(own, from_z, tile_rows))
    *kept_z, sums_z, weighted_z = density_halo("z", "gz", from_z, own_feats)
    from_x = receive("gx", pack_x(own, from_z, from_y, tile_rows))
    *kept_y, sums_y, weighted_y = density_halo("y", "gy", from_y, own_feats)
    *kept_x, sums_x, weighted_x = density_halo("x", "gx", from_x, own_feats)
    partials = (sums_own, weighted_own, sums_z, weighted_z, sums_y, weighted_y, sums_x, weighted_x)
    press, first, *sends = pressure(own, partials)
    press_z = receive("gz", sends)
    forces = list(force_own(own, press, kept_own))
    press_y = receive("gy", pack_y(press, press_z, 2))
    forces += force_halo("z", "gz", from_z, press_z, press, kept_z)
    press_x = receive("gx", pack_x(press, press_z, press_y, 2))
    forces += force_halo("y", "gy", from_y, press_y, press, kept_y)
    forces += force_halo("x", "gx", from_x, press_x, press, kept_x)
    return finish(own, press, first, forces)


neighbour_shifts = [
    (shift_x, shift_y, shift_z)
    for shift_x in (-1, 0, 1)
    for shift_y in (-1, 0, 1)
    for shift_z in (-1, 0, 1)
]


def extended(shard, sides, width):
    for axis, dim in sides:
        peers, length = (lax.axis_size(axis), shard.shape[dim])
        up = [(i, (i + 1) % peers) for i in range(peers)]
        down = [(j, i) for i, j in up]
        last = lax.slice_in_dim(shard, length - width, length, axis=dim)
        leading = lax.slice_in_dim(shard, 0, width, axis=dim)
        before = lax.ppermute(last, axis, up)
        after = lax.ppermute(leading, axis, down)
        shard = jnp.concatenate([before, shard, after], axis=dim)
    return shard


def pair_geometry(own_rows, neighbour, cell_shift):
    offset_parts = [
        own_rows[axis_id][:, :, None] - neighbour[axis_id][:, None, :] - float(cell_shift[axis_id])
        for axis_id in range(3)
    ]
    dist_sq = (
        offset_parts[0] * offset_parts[0]
        + offset_parts[1] * offset_parts[1]
        + offset_parts[2] * offset_parts[2]
    )
    scaled = jnp.minimum(jnp.sqrt(dist_sq), 1.0)
    falloff = 1.0 - scaled
    kernel_value = kernel_norm * falloff**4 * (1.0 + 4.0 * scaled)
    kernel_slope = -20.0 * kernel_norm * falloff**3
    approach = sum(
        (
            (own_rows[3 + axis_id][:, :, None] - neighbour[3 + axis_id][:, None, :])
            * offset_parts[axis_id]
            for axis_id in range(3)
        )
    )
    return (offset_parts, dist_sq, kernel_value, kernel_slope, approach)


def density_terms(own_rows, neighbour, cell_shift):
    _, _, kernel_value, kernel_slope, approach = pair_geometry(own_rows, neighbour, cell_shift)
    other_mass = neighbour[6][:, None, :]
    return (
        jnp.sum(other_mass * kernel_value, -1),
        jnp.sum(other_mass * kernel_slope * approach, -1),
    )


def force_terms(own_rows, neighbour, cell_shift):
    offset_parts, dist_sq, _, kernel_slope, approach = pair_geometry(
        own_rows, neighbour, cell_shift
    )
    rho_own = own_rows[7][:, :, None]
    rho_other = neighbour[7][:, None, :]
    converge = jnp.minimum(approach, 0.0) / (dist_sq + 0.01)
    viscous = (
        -(own_rows[8][:, :, None] + neighbour[8][:, None, :]) * converge / (rho_own + rho_other)
    )
    mslope = neighbour[6][:, None, :] * kernel_slope
    pair_force = mslope * (1.0 / rho_own + 1.0 / rho_other + viscous)
    accel_terms = jnp.stack(
        [-jnp.sum(pair_force * offset_parts[axis_id], -1) for axis_id in range(3)], 0
    )
    heating = jnp.sum(mslope * (1.0 / rho_own + 0.5 * viscous) * approach, -1)
    return (accel_terms, heating)


def switch_fields(density, div_sum, live_rows, weights):
    rho_live = jnp.where(live_rows > 0, density, 1.0)
    compress = jnp.maximum(div_sum / rho_live, 0.0)
    return jnp.stack([rho_live, weights * compress / (compress + 1.0)], 0)


def sweep(terms, padded):
    count = padded.shape[0]
    slot_count = padded.shape[-1]
    span_x = padded.shape[1] - 2
    span_y = padded.shape[2] - 2
    span_z = padded.shape[3] - 2
    own_rows = padded[:, 1 : span_x + 1, 1 : span_y + 1, 1 : span_z + 1].reshape(
        count, -1, slot_count
    )
    totals = None
    for cell_shift in neighbour_shifts:
        neighbour = padded[
            :,
            1 + cell_shift[0] : 1 + cell_shift[0] + span_x,
            1 + cell_shift[1] : 1 + cell_shift[1] + span_y,
            1 + cell_shift[2] : 1 + cell_shift[2] + span_z,
        ]
        result = terms(own_rows, neighbour.reshape(count, -1, slot_count), cell_shift)
        totals = (
            result
            if totals is None
            else jax.tree.map(lambda left, right: left + right, totals, result)
        )
    return totals


def per_device(positions, velocities, masses, alphas, counts):
    slot_count = positions.shape[-1]
    cell_shape = positions.shape[1:4]
    occupied = (
        jnp.arange(slot_count, dtype=jnp.int32)[None, None, None, :] < counts[..., None]
    ).astype(jnp.float32)
    live_mass = masses * occupied
    carried = jnp.concatenate([positions, velocities, live_mass[None]], 0)
    padded = extended(carried, (("gx", 1), ("gy", 2), ("gz", 3)), 1)
    density, div_sum = sweep(density_terms, padded)
    live_rows = occupied.reshape(-1, slot_count)
    weights = alphas.reshape(-1, slot_count)
    pressure_fields = switch_fields(density, div_sum, live_rows, weights).reshape(
        (2,) + cell_shape + (slot_count,)
    )
    own_density = pressure_fields[0]
    pressure_pad = extended(pressure_fields, (("gx", 1), ("gy", 2), ("gz", 3)), 1)
    fields = jnp.concatenate([padded, pressure_pad], 0)
    accel_total, heat_total = sweep(force_terms, fields)
    acceleration = accel_total.reshape((3,) + cell_shape + (slot_count,)) * occupied[None]
    heating = heat_total.reshape(cell_shape + (slot_count,)) * occupied
    return (own_density, acceleration, heating)


def per_device_any(positions, velocities, masses, alphas, counts):
    if positions.shape[1:] == (2, 2, 2, 128):
        return per_block(positions, velocities, masses, alphas, counts)
    return per_device(positions, velocities, masses, alphas, counts)


def solution(mesh):
    return jax.shard_map(
        per_device_any,
        mesh=mesh,
        in_specs=(
            P(None, "gx", "gy", "gz", None),
            P(None, "gx", "gy", "gz", None),
            P("gx", "gy", "gz", None),
            P("gx", "gy", "gz", None),
            P("gx", "gy", "gz"),
        ),
        out_specs=(
            P("gx", "gy", "gz", None),
            P(None, "gx", "gy", "gz", None),
            P("gx", "gy", "gz", None),
        ),
        check_vma=False,
    )
```

```python
import math

import jax
import jax.numpy as jnp
from jax import lax
from jax.experimental import pallas as pl
from jax.experimental.pallas import tpu as pltpu
from jax.sharding import PartitionSpec as P


f32 = jnp.float32
bf16 = jnp.bfloat16
kernel_norm = 21.0 / (2.0 * math.pi)
tile_rows = 8
feature_rows = 48
tiny = 1e-12
together = 4
strip = 128

vmem = pl.BlockSpec(memory_space=pltpu.VMEM)


def shaped(*dims, kind=f32):
    return jax.ShapeDtypeStruct(dims, kind)


def paired(axis):
    return lax.axis_size(axis) % 2 == 0


def first_sends_high(axis):
    return lax.axis_index(axis) % 2 == 0 if paired(axis) else lax.axis_index(axis) >= 0


def first_gives_before(axis):
    return lax.axis_index(axis) % 2 == 1 if paired(axis) else lax.axis_index(axis) >= 0


def routes(axis):
    peers = lax.axis_size(axis)
    if peers % 2 == 0:
        first = [(i, i + 1 if i % 2 == 0 else i - 1) for i in range(peers)]
        second = [(i, (i - 1 if i % 2 == 0 else i + 1) % peers) for i in range(peers)]
    else:
        first = [(i, (i + 1) % peers) for i in range(peers)]
        second = [(i, (i - 1) % peers) for i in range(peers)]
    return first, second


def split3(value):
    high = value.astype(bf16).astype(f32)
    rest = value - high
    middle = rest.astype(bf16).astype(f32)
    return high, middle, rest - middle


def row_ids():
    return lax.broadcasted_iota(jnp.int32, (tile_rows, 128), 0)


def rows_of(*rows):
    ids = row_ids()
    out = jnp.zeros((tile_rows, 128), f32)
    for place, row in enumerate(rows):
        out = jnp.where(ids == place, row, out)
    return out


def moments(tile, offsets):
    ids = row_ids()
    shift = jnp.where(ids == 0, offsets[0], jnp.where(ids == 1, offsets[1], jnp.where(ids == 2, offsets[2], 0.0)))
    high, low, _ = split3(tile + shift)
    moved = high + low.astype(bf16).astype(f32)
    x, y, z, vx, vy, vz = (moved[i : i + 1] for i in range(6))
    sq = x * x + y * y + z * z
    xv = x * vx + y * vy + z * vz
    return jnp.where(ids == 6, sq, jnp.where(ids == 7, xv, moved)), tile[6:7]


def other_features(table, mass):
    p1, p2, p3 = split3(table)
    m1, m2, m3 = split3(mass)
    ids = row_ids()
    extra = jnp.where(ids < 3, 1.0, jnp.where(ids >= 6, p3, jnp.where(ids == 3, m1, jnp.where(ids == 4, m2, m3))))
    return jnp.concatenate([p1, p1, p2, p2, extra, jnp.zeros_like(extra)], 0).T.astype(bf16)


def own_features(table):
    ids = row_ids()
    sq = split3(table[6:7])
    xv = split3(table[7:8])
    down = pltpu.roll(table, 3, 0)
    up = pltpu.roll(table, 5, 0)
    left = jnp.where(ids < 3, -2.0 * table, jnp.where(ids == 6, 1.0, 0.0))
    right = jnp.where(ids < 3, -up, jnp.where(ids < 6, -down, jnp.where(ids == 7, 1.0, 0.0)))
    halves = []
    for part, fixed in ((left, sq), (right, xv)):
        q1, q2, _ = split3(part)
        extra = rows_of(*fixed) + jnp.where(ids >= 6, part, 0.0)
        halves.append(jnp.concatenate([q1, q2, q1, q2, extra, jnp.zeros_like(extra)], 0))
    return jnp.concatenate(halves, 1).astype(bf16)


def mass_columns(table, mass):
    weighted = mass * table
    w1, w2, _ = split3(weighted)
    m1, m2, _ = split3(mass)
    extra = rows_of(m1, m2)
    left = jnp.concatenate([w1, w2, extra, jnp.zeros_like(extra)], 0).astype(bf16)
    return jnp.concatenate([left, left], 1)


def picker(first_row):
    ids = lax.broadcasted_iota(jnp.int32, (feature_rows, 128), 0)
    return jnp.where((ids >= first_row) & (ids < first_row + 3), 1.0, 0.0).astype(bf16)


def prepare(tile, offsets, at, feats, masses, columns):
    table, mass = moments(tile, offsets)
    lanes = other_features(table, mass)
    feats[at] = lanes
    masses[at] = jnp.dot(lanes, picker(35), preferred_element_type=f32)
    columns[at] = mass_columns(table, mass)


def pipelined(tiles, stages):
    for step in range(len(tiles) + len(stages) - 1):
        for lag, stage in enumerate(stages):
            if 0 <= step - lag < len(tiles):
                stage(*tiles[step - lag])


def idle(*tile):
    pass


def over_cells(cells, body):
    lax.fori_loop(0, cells // together, lambda i, _: body([i * together + j for j in range(together)]), 0)


def density_pairs(own, cells, near, feats, masses, columns, slopes, visc, sums, weighted):
    def some(group):
        both, total, sofar = {}, {}, {}
        picks = [near(c) for c in group]
        tiles = [
            (j, k, h) for j in range(len(group)) for k in range(len(picks[j])) for h in range(0, 128, strip)
        ]

        def geometry(j, k, h):
            left = feats[picks[j][k], h : h + strip]
            both[j, k, h] = jnp.dot(left, own[group[j]], preferred_element_type=f32)

        def terms(j, k, h):
            c, n = group[j], picks[j][k]
            pair = both.pop((j, k, h))
            for low in range(0, strip, 16):
                r = h + low
                dist = jnp.maximum(pair[low : low + 16, :128], tiny)
                run = pair[low : low + 16, 128:]
                q = dist * lax.rsqrt(dist)
                fall = jnp.maximum(1.0 - q, 0.0)
                g = fall * fall * fall
                part = g * q * masses[n, r : r + 16]
                part = part[:8] + part[8:]
                total[j] = part if j not in total else total[j] + part
                high = g.astype(bf16)
                slopes[c, k, r : r + 16] = high
                slopes[c, k, 128 + r : 128 + r + 16] = (g - high.astype(f32)).astype(bf16)
                visc[c, k, r : r + 16] = g * jnp.minimum(run, 0.0) * (1.0 / (dist + 0.01))

        def reduce(j, k, h):
            if h + strip < 128:
                return
            c, n = group[j], picks[j][k]
            part = jnp.dot(columns[n], slopes[c, k], preferred_element_type=f32)
            sofar[j] = part if j not in sofar else sofar[j] + part
            if k == len(picks[j]) - 1:
                sums[c] = sofar[j]
                weighted[c] = total[j]

        pipelined(tiles, (geometry, idle, terms, idle, reduce))
        return 0

    over_cells(cells, some)


def prepare_force(tile, offsets, press, at, rhos, columns, gradients):
    table, mass = moments(tile, offsets)
    rho = press[0:1]
    weight = press[1:2]
    heavy = mass * table
    h1, h2, _ = split3(heavy)
    s1, s2, _ = split3(weight * heavy)
    m1, m2, _ = split3(mass)
    w1, w2, _ = split3(weight * mass)
    extra = rows_of(m1, m2, w1, w2)
    left = jnp.concatenate([h1, h2, s1, s2, extra, jnp.zeros_like(extra)], 0).astype(bf16)
    columns[at] = jnp.concatenate([left, left], 1)
    light = (mass / rho) * jnp.where(row_ids() < 3, table, 1.0)
    l1, l2, _ = split3(light)
    left = jnp.concatenate([l1, l2], 0).astype(bf16)
    gradients[at] = jnp.concatenate([left, left], 1)
    r1, r2, r3 = split3(rho)
    lanes = jnp.concatenate([rows_of(r1, r2, r3), jnp.zeros((tile_rows, 128), f32)], 0).T.astype(bf16)
    ids = lax.broadcasted_iota(jnp.int32, (16, 128), 0)
    rhos[at] = jnp.dot(lanes, jnp.where(ids < 3, 1.0, 0.0).astype(bf16), preferred_element_type=f32)


def force_pairs(cells, near, press_row, rhos, columns, gradients, slopes, visc, sums, pulls):
    def some(group):
        mixed, sofar, pulled = {}, {}, {}
        picks = [near(c) for c in group]
        mine = [press_row(c) for c in group]
        tiles = [(j, k) for j, c in enumerate(group) for k in range(len(near(c)))]

        def terms(j, k):
            c, n = group[j], picks[j][k]
            highs, lows = [], []
            for r in range(0, 128, 16):
                t = visc[c, k, r : r + 16] * (1.0 / (rhos[n, r : r + 16] + mine[j]))
                high = t.astype(bf16)
                highs.append(high)
                lows.append((t - high.astype(f32)).astype(bf16))
            mixed[j, k] = jnp.concatenate(highs + lows, 0)

        def reduce(j, k):
            c, n = group[j], picks[j][k]
            part = jnp.dot(columns[n], mixed.pop((j, k)), preferred_element_type=f32)
            pull = jnp.dot(gradients[n], slopes[c, k], preferred_element_type=f32)
            sofar[j] = part if j not in sofar else sofar[j] + part
            pulled[j] = pull if j not in pulled else pulled[j] + pull
            if k == len(picks[j]) - 1:
                sums[c] = sofar[j]
                pulls[c] = pulled[j]

        pipelined(tiles, (terms, reduce))
        return 0

    over_cells(cells, some)


def parts_of(c):
    return c // 4, (c // 2) % 2, c % 2


def flat(*pairs):
    at = 0
    for size, index in pairs:
        at = at * size + index
    return at


def near_own(c):
    return list(range(8))


def near_z(c):
    _, _, cz = parts_of(c)
    return [flat((2, cz), (2, x), (2, y)) for x in range(2) for y in range(2)]


def near_y(c):
    _, cy, cz = parts_of(c)
    return [flat((2, cy), (2, x), (4, cz + dz)) for x in range(2) for dz in range(3)]


def near_x(c):
    cx, cy, cz = parts_of(c)
    return [flat((2, cx), (4, cy + dy), (4, cz + dz)) for dy in range(3) for dz in range(3)]


def place_own(e):
    x, y, z = parts_of(e)
    return x - 1, y - 1, z - 1


def place_z(e):
    side, x, y = parts_of(e)
    return x - 1, y - 1, 3 * side - 2


def place_y(e):
    return (e // 4) % 2 - 1, 3 * (e // 8) - 2, e % 4 - 2


def place_x(e):
    return 3 * (e // 16) - 2, (e // 4) % 4 - 2, e % 4 - 2


def offsets_of(place):
    return [jnp.asarray(v, jnp.int32).astype(f32) for v in place]


groups = {
    "own": (8, near_own, place_own, 8),
    "z": (8, near_z, place_z, 4),
    "y": (16, near_y, place_y, 6),
    "x": (32, near_x, place_x, 9),
}


def scratch_density(entries):
    return [
        pltpu.VMEM((entries, 128, feature_rows), bf16),
        pltpu.VMEM((entries, 128, 128), f32),
        pltpu.VMEM((entries, 32, 256), bf16),
    ]


def pair_outputs(count):
    return [
        shaped(8, count, 256, 128, kind=bf16),
        shaped(8, count, 128, 128),
        shaped(8, 32, 128),
        shaped(8, tile_rows, 128),
    ]


def call(body, outs, operands, specs=None, scratch=(), limit=24):
    return pl.pallas_call(
        body,
        out_shape=tuple(outs),
        in_specs=specs or [vmem] * len(operands),
        out_specs=tuple([vmem] * len(outs)),
        scratch_shapes=list(scratch),
        compiler_params=pltpu.CompilerParams(vmem_limit_bytes=limit << 20),
    )(*operands)


def take_side(before, refs, side, rest):
    if len(refs) == 1:
        one, two = refs[0][(0,) + rest], refs[0][(1,) + rest]
    else:
        one, two = refs[0][rest], refs[1][rest]
    return jnp.where(before, one, two) if side == 0 else jnp.where(before, two, one)


def send_shapes(axis, plane):
    if lax.axis_size(axis) == 2:
        return [shaped(2, *plane)]
    return [shaped(*plane), shaped(*plane)]


def put_sends(refs, high, tile_at, rest):
    top, bottom = tile_at(1), tile_at(0)
    one, two = jnp.where(high, top, bottom), jnp.where(high, bottom, top)
    if len(refs) == 1:
        refs[0][(0,) + rest] = one
        refs[0][(1,) + rest] = two
    else:
        refs[0][rest] = one
        refs[1][rest] = two


def receive(axis, sends):
    first, second = routes(axis)
    ways = (first,) if len(sends) == 1 else (first, second)
    got = []
    for send, way in zip(sends, ways):
        got.append(lax.ppermute(send, axis, way))
    return tuple(got)


def pack_y(own, from_z, rows):
    sends = send_shapes("gy", (2, 4, rows, 128))
    n = len(from_z)

    def body(own_ref, *refs):
        got, out = refs[:n], refs[n:]
        high = first_sends_high("gy")
        before = first_gives_before("gz")
        for x in range(2):
            for e in range(4):

                def tile_at(y, x=x, e=e):
                    if 1 <= e <= 2:
                        return own_ref[x, y, e - 1]
                    return take_side(before, got, 0 if e == 0 else 1, (x, y))

                put_sends(out, high, tile_at, (x, e))

    return call(body, sends, (own, *from_z), limit=4)


def pack_x(own, from_z, from_y, rows):
    sends = send_shapes("gx", (4, 4, rows, 128))
    n, m = len(from_z), len(from_y)

    def body(own_ref, *refs):
        got_z, got_y, out = refs[:n], refs[n : n + m], refs[n + m :]
        high = first_sends_high("gx")
        before_z = first_gives_before("gz")
        before_y = first_gives_before("gy")
        for a in range(4):
            for e in range(4):

                def tile_at(x, a=a, e=e):
                    if not 1 <= a <= 2:
                        return take_side(before_y, got_y, 0 if a == 0 else 1, (x, e))
                    if 1 <= e <= 2:
                        return own_ref[x, a - 1, e - 1]
                    return take_side(before_z, got_z, 0 if e == 0 else 1, (x, a - 1))

                put_sends(out, high, tile_at, (a, e))

    return call(body, sends, (own, *from_z, *from_y), limit=4)


inner_dims = {"z": (2, 2), "y": (2, 4), "x": (4, 4)}


def entry_tile(group, before, refs, e, sides):
    _, b = inner_dims[group]
    return take_side(before, refs, sides, (e // b, e % b))


def density_own(own):
    entries, near, place, count = groups["own"]

    def body(own_ref, slopes, visc, sums, weighted, table_ref, feats, masses, columns):
        def one(c, _):
            x, y, z = parts_of(c)
            tile = own_ref[x, y, z]
            offsets = offsets_of(place(c))
            prepare(tile, offsets, c, feats, masses, columns)
            table, _ = moments(tile, offsets)
            table_ref[c] = own_features(table)
            return 0

        lax.fori_loop(0, 8, one, 0, unroll=8)
        density_pairs(table_ref, 8, near, feats, masses, columns, slopes, visc, sums, weighted)

    outs = pair_outputs(count) + [shaped(8, feature_rows, 256, kind=bf16)]
    return call(body, outs, (own,), scratch=scratch_density(entries))


def density_halo(group, axis, received, own_feats):
    entries, near, place, count = groups[group]
    n = len(received)
    half = entries // 2

    def body(*refs):
        got, own_ref = refs[:n], refs[n]
        slopes, visc, sums, weighted, feats, masses, columns = refs[n + 1 :]
        before = first_gives_before(axis)
        for side in range(2):

            def one(e, _, side=side):
                tile = entry_tile(group, before, got, e, side)
                at = side * half + e
                prepare(tile, offsets_of(place(at)), at, feats, masses, columns)
                return 0

            lax.fori_loop(0, half, one, 0, unroll=min(half, 8))
        density_pairs(own_ref, 8, near, feats, masses, columns, slopes, visc, sums, weighted)

    return call(body, pair_outputs(count), (*received, own_feats), scratch=scratch_density(entries))


def pressure(own, partials):
    sends = send_shapes("gz", (2, 2, 2, 128))
    outs = [shaped(2, 2, 2, 2, 128), shaped(8, tile_rows, 128)] + sends
    n = len(partials)

    def body(own_ref, *refs):
        pieces, (press, first), out = refs[:n], refs[n : n + 2], refs[n + 2 :]
        high = first_sends_high("gz")
        for x in range(2):
            for y in range(2):
                for z in range(2):
                    c = 4 * x + 2 * y + z
                    table, mass = moments(own_ref[x, y, z], [float(v - 1) for v in (x, y, z)])
                    s = sum(p[c] for p in pieces[0::2])
                    gq = jnp.sum(sum(p[c] for p in pieces[1::2]), 0, keepdims=True)
                    t = s[0:8] + s[8:16]
                    m0 = s[16:17] + s[17:18]
                    pos, vel = table[0:3], table[3:6]
                    x_mx = jnp.sum(pos * t[0:3], 0, keepdims=True)
                    x_mv = jnp.sum(pos * t[3:6], 0, keepdims=True)
                    v_mx = jnp.sum(vel * t[0:3], 0, keepdims=True)
                    gr2 = t[6:7] + table[6:7] * m0 - 2.0 * x_mx
                    rho = kernel_norm * (m0 + 3.0 * gq - 4.0 * gr2)
                    div = -20.0 * kernel_norm * (t[7:8] + table[7:8] * m0 - x_mv - v_mx)
                    rho = jnp.where(mass > 0.0, rho, 1.0)
                    compress = jnp.maximum(div / rho, 0.0)
                    weight = own_ref[x, y, z, 7:8] * compress / (compress + 1.0)
                    press[x, y, z] = jnp.concatenate([rho, weight], 0)
                    first[c] = jnp.concatenate(
                        [pos * m0 - t[0:3], div, jnp.zeros((tile_rows - 4, 128), f32)], 0
                    )
        for x in range(2):
            for y in range(2):
                put_sends(out, high, lambda z, x=x, y=y: press[x, y, z], (x, y))

    return call(body, outs, (own, *partials), limit=8)


def scratch_force(entries):
    return [
        pltpu.VMEM((entries, 128, 128), f32),
        pltpu.VMEM((entries, 48, 256), bf16),
        pltpu.VMEM((entries, 16, 256), bf16),
    ]


def force_outputs():
    return [shaped(8, 48, 128), shaped(8, 16, 128)]


def force_own(own, press, kept):
    entries, near, place, _ = groups["own"]

    def body(own_ref, press_ref, slopes, visc, sums, pulls, rhos, columns, gradients):
        def one(c, _):
            x, y, z = parts_of(c)
            prepare_force(
                own_ref[x, y, z], offsets_of(place(c)), press_ref[x, y, z], c, rhos, columns, gradients
            )
            return 0

        lax.fori_loop(0, 8, one, 0, unroll=8)

        def mine(c):
            x, y, z = parts_of(c)
            return press_ref[x, y, z, 0:1]

        force_pairs(8, near, mine, rhos, columns, gradients, slopes, visc, sums, pulls)

    return call(body, force_outputs(), (own, press, *kept), scratch=scratch_force(entries))


def force_halo(group, axis, received, press_received, press, kept):
    entries, near, place, _ = groups[group]
    n = len(received)
    half = entries // 2

    def body(*refs):
        got, got_press, press_ref = refs[:n], refs[n : 2 * n], refs[2 * n]
        slopes, visc, sums, pulls, rhos, columns, gradients = refs[2 * n + 1 :]
        before = first_gives_before(axis)
        for side in range(2):

            def one(e, _, side=side):
                tile = entry_tile(group, before, got, e, side)
                fields = entry_tile(group, before, got_press, e, side)
                at = side * half + e
                prepare_force(tile, offsets_of(place(at)), fields, at, rhos, columns, gradients)
                return 0

            lax.fori_loop(0, half, one, 0, unroll=min(half, 8))

        def mine(c):
            x, y, z = parts_of(c)
            return press_ref[x, y, z, 0:1]

        force_pairs(8, near, mine, rhos, columns, gradients, slopes, visc, sums, pulls)

    return call(
        body,
        force_outputs(),
        (*received, *press_received, press, *kept),
        scratch=scratch_force(entries),
    )


def finish(own, press, first, partials):
    outs = [shaped(2, 2, 2, 128), shaped(3, 2, 2, 2, 128), shaped(2, 2, 2, 128)]
    n = len(partials)

    def body(own_ref, press_ref, first_ref, *refs):
        pieces, (density, accel, heating) = refs[:n], refs[n:]
        for x in range(2):
            for y in range(2):
                for z in range(2):
                    c = 4 * x + 2 * y + z
                    table, mass = moments(own_ref[x, y, z], [float(v - 1) for v in (x, y, z)])
                    u = sum(p[c] for p in pieces[0::2])
                    v = sum(p[c] for p in pieces[1::2])
                    plain, scaled = u[0:8] + u[8:16], u[16:24] + u[24:32]
                    a0, b0 = u[32:33] + u[33:34], u[34:35] + u[35:36]
                    g = v[0:8] + v[8:16]
                    rho, weight = press_ref[x, y, z, 0:1], press_ref[x, y, z, 1:2]
                    inverse = 1.0 / rho
                    mixed = weight * plain + scaled
                    zero = weight * a0 + b0
                    pos, vel = table[0:3], table[3:6]
                    total = (
                        inverse * first_ref[c, 0:3]
                        + (pos * g[3:4] - g[0:3])
                        - (pos * zero - mixed[0:3])
                    )
                    live = jnp.where(mass > 0.0, 1.0, 0.0)
                    push = (20.0 * kernel_norm) * live * total
                    work = (
                        mixed[7:8]
                        + table[7:8] * zero
                        - jnp.sum(pos * mixed[3:6], 0, keepdims=True)
                        - jnp.sum(vel * mixed[0:3], 0, keepdims=True)
                    )
                    warm = live * (first_ref[c, 3:4] * inverse + (10.0 * kernel_norm) * work)
                    density[x, y, z : z + 1, :] = rho
                    for i in range(3):
                        accel[i, x, y, z : z + 1, :] = push[i : i + 1]
                    heating[x, y, z : z + 1, :] = warm

    return call(body, outs, (own, press, first, *partials), limit=8)


def gather_own(fields, counts):
    sends = send_shapes("gz", (2, 2, tile_rows, 128))

    def body(fields_ref, counts_ref, own, *out):
        high = first_sends_high("gz")
        alone = row_ids() == 6
        lanes = lax.broadcasted_iota(jnp.int32, (tile_rows, 128), 1)
        for x in range(2):
            for y in range(2):
                for z in range(2):
                    dead = lanes >= counts_ref[x, y : y + 1, z : z + 1]
                    tile = rows_of(*(fields_ref[i, x, y, z : z + 1, :] for i in range(tile_rows)))
                    own[x, y, z] = jnp.where(alone & dead, 0.0, tile)
        for x in range(2):
            for y in range(2):
                put_sends(out, high, lambda z, x=x, y=y: own[x, y, z], (x, y))

    return call(body, [shaped(2, 2, 2, tile_rows, 128)] + sends, (fields, counts), limit=4)


def per_block(positions, velocities, masses, alphas, counts):
    fields = jnp.concatenate([positions, velocities, masses[None], alphas[None]], 0)
    own, *sends = gather_own(fields, counts)
    from_z = receive("gz", sends)
    *kept_own, sums_own, weighted_own, own_feats = density_own(own)
    from_y = receive("gy", pack_y(own, from_z, tile_rows))
    *kept_z, sums_z, weighted_z = density_halo("z", "gz", from_z, own_feats)
    from_x = receive("gx", pack_x(own, from_z, from_y, tile_rows))
    *kept_y, sums_y, weighted_y = density_halo("y", "gy", from_y, own_feats)
    *kept_x, sums_x, weighted_x = density_halo("x", "gx", from_x, own_feats)
    partials = (sums_own, weighted_own, sums_z, weighted_z, sums_y, weighted_y, sums_x, weighted_x)
    press, first, *sends = pressure(own, partials)
    press_z = receive("gz", sends)
    forces = list(force_own(own, press, kept_own))
    press_y = receive("gy", pack_y(press, press_z, 2))
    forces += force_halo("z", "gz", from_z, press_z, press, kept_z)
    press_x = receive("gx", pack_x(press, press_z, press_y, 2))
    forces += force_halo("y", "gy", from_y, press_y, press, kept_y)
    forces += force_halo("x", "gx", from_x, press_x, press, kept_x)
    return finish(own, press, first, forces)


neighbour_shifts = [
    (shift_x, shift_y, shift_z)
    for shift_x in (-1, 0, 1)
    for shift_y in (-1, 0, 1)
    for shift_z in (-1, 0, 1)
]


def extended(shard, sides, width):
    for axis, dim in sides:
        peers, length = (lax.axis_size(axis), shard.shape[dim])
        up = [(i, (i + 1) % peers) for i in range(peers)]
        down = [(j, i) for i, j in up]
        last = lax.slice_in_dim(shard, length - width, length, axis=dim)
        leading = lax.slice_in_dim(shard, 0, width, axis=dim)
        before = lax.ppermute(last, axis, up)
        after = lax.ppermute(leading, axis, down)
        shard = jnp.concatenate([before, shard, after], axis=dim)
    return shard


def pair_geometry(own_rows, neighbour, cell_shift):
    offset_parts = [
        own_rows[axis_id][:, :, None] - neighbour[axis_id][:, None, :] - float(cell_shift[axis_id])
        for axis_id in range(3)
    ]
    dist_sq = (
        offset_parts[0] * offset_parts[0]
        + offset_parts[1] * offset_parts[1]
        + offset_parts[2] * offset_parts[2]
    )
    scaled = jnp.minimum(jnp.sqrt(dist_sq), 1.0)
    falloff = 1.0 - scaled
    kernel_value = kernel_norm * falloff**4 * (1.0 + 4.0 * scaled)
    kernel_slope = -20.0 * kernel_norm * falloff**3
    approach = sum(
        (
            (own_rows[3 + axis_id][:, :, None] - neighbour[3 + axis_id][:, None, :])
            * offset_parts[axis_id]
            for axis_id in range(3)
        )
    )
    return (offset_parts, dist_sq, kernel_value, kernel_slope, approach)


def density_terms(own_rows, neighbour, cell_shift):
    _, _, kernel_value, kernel_slope, approach = pair_geometry(own_rows, neighbour, cell_shift)
    other_mass = neighbour[6][:, None, :]
    return (
        jnp.sum(other_mass * kernel_value, -1),
        jnp.sum(other_mass * kernel_slope * approach, -1),
    )


def force_terms(own_rows, neighbour, cell_shift):
    offset_parts, dist_sq, _, kernel_slope, approach = pair_geometry(
        own_rows, neighbour, cell_shift
    )
    rho_own = own_rows[7][:, :, None]
    rho_other = neighbour[7][:, None, :]
    converge = jnp.minimum(approach, 0.0) / (dist_sq + 0.01)
    viscous = (
        -(own_rows[8][:, :, None] + neighbour[8][:, None, :]) * converge / (rho_own + rho_other)
    )
    mslope = neighbour[6][:, None, :] * kernel_slope
    pair_force = mslope * (1.0 / rho_own + 1.0 / rho_other + viscous)
    accel_terms = jnp.stack(
        [-jnp.sum(pair_force * offset_parts[axis_id], -1) for axis_id in range(3)], 0
    )
    heating = jnp.sum(mslope * (1.0 / rho_own + 0.5 * viscous) * approach, -1)
    return (accel_terms, heating)


def switch_fields(density, div_sum, live_rows, weights):
    rho_live = jnp.where(live_rows > 0, density, 1.0)
    compress = jnp.maximum(div_sum / rho_live, 0.0)
    return jnp.stack([rho_live, weights * compress / (compress + 1.0)], 0)


def sweep(terms, padded):
    count = padded.shape[0]
    slot_count = padded.shape[-1]
    span_x = padded.shape[1] - 2
    span_y = padded.shape[2] - 2
    span_z = padded.shape[3] - 2
    own_rows = padded[:, 1 : span_x + 1, 1 : span_y + 1, 1 : span_z + 1].reshape(
        count, -1, slot_count
    )
    totals = None
    for cell_shift in neighbour_shifts:
        neighbour = padded[
            :,
            1 + cell_shift[0] : 1 + cell_shift[0] + span_x,
            1 + cell_shift[1] : 1 + cell_shift[1] + span_y,
            1 + cell_shift[2] : 1 + cell_shift[2] + span_z,
        ]
        result = terms(own_rows, neighbour.reshape(count, -1, slot_count), cell_shift)
        totals = (
            result
            if totals is None
            else jax.tree.map(lambda left, right: left + right, totals, result)
        )
    return totals


def per_device(positions, velocities, masses, alphas, counts):
    slot_count = positions.shape[-1]
    cell_shape = positions.shape[1:4]
    occupied = (
        jnp.arange(slot_count, dtype=jnp.int32)[None, None, None, :] < counts[..., None]
    ).astype(jnp.float32)
    live_mass = masses * occupied
    carried = jnp.concatenate([positions, velocities, live_mass[None]], 0)
    padded = extended(carried, (("gx", 1), ("gy", 2), ("gz", 3)), 1)
    density, div_sum = sweep(density_terms, padded)
    live_rows = occupied.reshape(-1, slot_count)
    weights = alphas.reshape(-1, slot_count)
    pressure_fields = switch_fields(density, div_sum, live_rows, weights).reshape(
        (2,) + cell_shape + (slot_count,)
    )
    own_density = pressure_fields[0]
    pressure_pad = extended(pressure_fields, (("gx", 1), ("gy", 2), ("gz", 3)), 1)
    fields = jnp.concatenate([padded, pressure_pad], 0)
    accel_total, heat_total = sweep(force_terms, fields)
    acceleration = accel_total.reshape((3,) + cell_shape + (slot_count,)) * occupied[None]
    heating = heat_total.reshape(cell_shape + (slot_count,)) * occupied
    return (own_density, acceleration, heating)


def per_device_any(positions, velocities, masses, alphas, counts):
    if positions.shape[1:] == (2, 2, 2, 128):
        return per_block(positions, velocities, masses, alphas, counts)
    return per_device(positions, velocities, masses, alphas, counts)


def solution(mesh):
    return jax.shard_map(
        per_device_any,
        mesh=mesh,
        in_specs=(
            P(None, "gx", "gy", "gz", None),
            P(None, "gx", "gy", "gz", None),
            P("gx", "gy", "gz", None),
            P("gx", "gy", "gz", None),
            P("gx", "gy", "gz"),
        ),
        out_specs=(
            P("gx", "gy", "gz", None),
            P(None, "gx", "gy", "gz", None),
            P("gx", "gy", "gz", None),
        ),
        check_vma=False,
    )
```

```python
import math

import jax
import jax.numpy as jnp
from jax import lax
from jax.experimental import pallas as pl
from jax.experimental.pallas import tpu as pltpu
from jax.sharding import PartitionSpec as P


f32 = jnp.float32
bf16 = jnp.bfloat16
kernel_norm = 21.0 / (2.0 * math.pi)
tile_rows = 8
feature_rows = 48
tiny = 1e-12
together = 4

vmem = pl.BlockSpec(memory_space=pltpu.VMEM)


def shaped(*dims, kind=f32):
    return jax.ShapeDtypeStruct(dims, kind)


def paired(axis):
    return lax.axis_size(axis) % 2 == 0


def first_sends_high(axis):
    return lax.axis_index(axis) % 2 == 0 if paired(axis) else lax.axis_index(axis) >= 0


def first_gives_before(axis):
    return lax.axis_index(axis) % 2 == 1 if paired(axis) else lax.axis_index(axis) >= 0


def routes(axis):
    peers = lax.axis_size(axis)
    if peers % 2 == 0:
        first = [(i, i + 1 if i % 2 == 0 else i - 1) for i in range(peers)]
        second = [(i, (i - 1 if i % 2 == 0 else i + 1) % peers) for i in range(peers)]
    else:
        first = [(i, (i + 1) % peers) for i in range(peers)]
        second = [(i, (i - 1) % peers) for i in range(peers)]
    return first, second


def split3(value):
    high = value.astype(bf16).astype(f32)
    rest = value - high
    middle = rest.astype(bf16).astype(f32)
    return high, middle, rest - middle


def row_ids():
    return lax.broadcasted_iota(jnp.int32, (tile_rows, 128), 0)


def rows_of(*rows):
    ids = row_ids()
    out = jnp.zeros((tile_rows, 128), f32)
    for place, row in enumerate(rows):
        out = jnp.where(ids == place, row, out)
    return out


def moments(tile, offsets):
    ids = row_ids()
    shift = jnp.where(ids == 0, offsets[0], jnp.where(ids == 1, offsets[1], jnp.where(ids == 2, offsets[2], 0.0)))
    high, low, _ = split3(tile + shift)
    moved = high + low.astype(bf16).astype(f32)
    x, y, z, vx, vy, vz = (moved[i : i + 1] for i in range(6))
    sq = x * x + y * y + z * z
    xv = x * vx + y * vy + z * vz
    return jnp.where(ids == 6, sq, jnp.where(ids == 7, xv, moved)), tile[6:7]


def column_features(table):
    p1, p2, p3 = split3(table)
    ids = row_ids()
    extra = jnp.where(ids < 3, 1.0, jnp.where(ids >= 6, p3, 0.0))
    return jnp.concatenate([p1, p1, p2, p2, extra, jnp.zeros_like(extra)], 0).T.astype(bf16)


def row_features(table):
    ids = row_ids()
    sq = split3(table[6:7])
    xv = split3(table[7:8])
    down = pltpu.roll(table, 3, 0)
    up = pltpu.roll(table, 5, 0)
    left = jnp.where(ids < 3, -2.0 * table, jnp.where(ids == 6, 1.0, 0.0))
    right = jnp.where(ids < 3, -up, jnp.where(ids < 6, -down, jnp.where(ids == 7, 1.0, 0.0)))
    halves = []
    for part, fixed in ((left, sq), (right, xv)):
        q1, q2, _ = split3(part)
        extra = rows_of(*fixed) + jnp.where(ids >= 6, part, 0.0)
        halves.append(jnp.concatenate([q1, q2, q1, q2, extra, jnp.zeros_like(extra)], 0))
    return jnp.concatenate(halves, 1).astype(bf16)


def mass_columns(table, mass):
    weighted = mass * table
    w1, w2, _ = split3(weighted)
    m1, m2, _ = split3(mass)
    extra = rows_of(m1, m2)
    left = jnp.concatenate([w1, w2, extra, jnp.zeros_like(extra)], 0).astype(bf16)
    return jnp.concatenate([left, left], 1)


def prepare(tile, offsets, at, feats, masses, columns):
    table, mass = moments(tile, offsets)
    feats[at] = row_features(table)
    masses[at] = jnp.broadcast_to(mass, (16, 128))
    columns[at] = mass_columns(table, mass)


def over_lanes(left, right):
    return lax.dot_general(left, right, (((1,), (1,)), ((), ())), preferred_element_type=f32)


def pipelined(tiles, stages):
    for step in range(len(tiles) + len(stages) - 1):
        for lag, stage in enumerate(stages):
            if 0 <= step - lag < len(tiles):
                stage(*tiles[step - lag])


def idle(*tile):
    pass


def over_cells(start, stop, body):
    lax.fori_loop(
        start // together, stop // together, lambda i, _: body([i * together + j for j in range(together)]), 0
    )


def density_pairs(own, cells, near, feats, masses, columns, slopes, pairs, sums, weighted):
    ones = jnp.ones((tile_rows, 256), bf16)

    def some(group):
        both, sofar = {}, {}
        picks = [near(c) for c in group]
        tiles = [(j, k) for j in range(len(group)) for k in range(len(picks[j]))]

        def geometry(j, k):
            pair = both[j, k] = jnp.dot(own[group[j]], feats[picks[j][k]], preferred_element_type=f32)
            pairs[group[j], k] = pair

        def terms(j, k):
            c, n = group[j], picks[j][k]
            pair = both.pop((j, k))
            mass = masses[n]
            for r in range(0, 128, 16):
                at = slice(r, r + 16)
                dist = jnp.maximum(pair[at, :128], tiny)
                q = dist * lax.rsqrt(dist)
                fall = jnp.maximum(1.0 - q, 0.0)
                g = fall * fall * fall
                part = g * q * mass
                weighted[j, at] = part if k == 0 else weighted[j, at] + part
                high = g.astype(bf16)
                slopes[c, k, at, :128] = high
                slopes[c, k, at, 128:] = (g - high.astype(f32)).astype(bf16)

        def reduce(j, k):
            c, n = group[j], picks[j][k]
            part = over_lanes(columns[n], slopes[c, k])
            sofar[j] = part if j not in sofar else sofar[j] + part
            if k == len(picks[j]) - 1:
                sums[c, :32] = sofar[j]
                high = weighted[j].astype(bf16)
                low = (weighted[j] - high.astype(f32)).astype(bf16)
                sums[c, 32:] = over_lanes(ones, jnp.concatenate([high, low], 1))

        pipelined(tiles, (geometry, idle, terms, idle, reduce))
        return 0

    over_cells(*cells, some)


def viscous(group, slopes, pairs):
    count = groups[group][3]

    def body(slopes_ref, pairs_ref, visc):
        def one(c, _):
            for k in range(count):
                for r in range(0, 128, 16):
                    at = slice(r, r + 16)
                    g = slopes_ref[c, k, at, :128].astype(f32) + slopes_ref[c, k, at, 128:].astype(f32)
                    run = jnp.minimum(pairs_ref[c, k, at, 128:], 0.0)
                    visc[c, k, at] = g * run * (1.0 / (pairs_ref[c, k, at, :128] + 0.01))
            return 0

        lax.fori_loop(0, 8, one, 0)

    return call(body, [shaped(8, count, 128, 128)], (slopes, pairs), limit=4)[0]


def prepare_force(tile, offsets, press, at, rhos, columns, gradients):
    table, mass = moments(tile, offsets)
    rho = press[0:1]
    weight = press[1:2]
    heavy = mass * jnp.where(row_ids() == 6, 1.0, table)
    h1, h2, _ = split3(heavy)
    s1, s2, _ = split3(weight * heavy)
    left = jnp.concatenate([h1, h2, s1, s2], 0).astype(bf16)
    columns[at] = jnp.concatenate([left, left], 1)
    light = (mass / rho) * jnp.where(row_ids() < 3, table, 1.0)
    l1, l2, _ = split3(light)
    left = jnp.concatenate([l1, l2], 0).astype(bf16)
    gradients[at] = jnp.concatenate([left, left], 1)
    rhos[at] = jnp.broadcast_to(rho, (16, 128))


def force_pairs(near, spread, rhos, columns, gradients, slopes, visc, sums, pulls, ready):
    def some(group):
        mixed, sofar, pulled = {}, {}, {}
        picks = [near(c) for c in group]
        tiles = [(j, k) for j, c in enumerate(group) for k in range(len(near(c)))]

        def terms(j, k):
            c, n = group[j], picks[j][k]
            highs, lows = [], []
            theirs = rhos[n]
            for r in range(0, 128, 16):
                at = slice(r, r + 16)
                below = theirs + spread[c, at]
                if ready:
                    t = visc[c, k, at] * (1.0 / below)
                else:
                    g = slopes[c, k, at, :128].astype(f32) + slopes[c, k, at, 128:].astype(f32)
                    run = jnp.minimum(visc[c, k, at, 128:], 0.0)
                    t = g * run * (1.0 / ((visc[c, k, at, :128] + 0.01) * below))
                high = t.astype(bf16)
                highs.append(high)
                lows.append((t - high.astype(f32)).astype(bf16))
            mixed[j, k] = jnp.concatenate([jnp.concatenate(highs, 0), jnp.concatenate(lows, 0)], 1)

        def reduce(j, k):
            c, n = group[j], picks[j][k]
            part = over_lanes(columns[n], mixed.pop((j, k)))
            pull = over_lanes(gradients[n], slopes[c, k])
            sofar[j] = part if j not in sofar else sofar[j] + part
            pulled[j] = pull if j not in pulled else pulled[j] + pull
            if k == len(picks[j]) - 1:
                sums[c] = sofar[j]
                pulls[c] = pulled[j]

        pipelined(tiles, (terms, reduce))
        return 0

    over_cells(0, 8, some)


def parts_of(c):
    return c // 4, (c // 2) % 2, c % 2


def flat(*pairs):
    at = 0
    for size, index in pairs:
        at = at * size + index
    return at


def near_own(c):
    return list(range(8))


def near_z(c):
    _, _, cz = parts_of(c)
    return [flat((2, cz), (2, x), (2, y)) for x in range(2) for y in range(2)]


def near_y(c):
    _, cy, cz = parts_of(c)
    return [flat((2, cy), (2, x), (4, cz + dz)) for x in range(2) for dz in range(3)]


def near_x(c):
    cx, cy, cz = parts_of(c)
    return [flat((2, cx), (4, cy + dy), (4, cz + dz)) for dy in range(3) for dz in range(3)]


def place_own(e):
    x, y, z = parts_of(e)
    return x - 1, y - 1, z - 1


def place_z(e):
    side, x, y = parts_of(e)
    return x - 1, y - 1, 3 * side - 2


def place_y(e):
    return (e // 4) % 2 - 1, 3 * (e // 8) - 2, e % 4 - 2


def place_x(e):
    return 3 * (e // 16) - 2, (e // 4) % 4 - 2, e % 4 - 2


def offsets_of(place):
    return [jnp.asarray(v, jnp.int32).astype(f32) for v in place]


groups = {
    "own": (8, near_own, place_own, 8),
    "z": (8, near_z, place_z, 4),
    "y": (16, near_y, place_y, 6),
    "x": (32, near_x, place_x, 9),
}


weights = pltpu.VMEM((together, 128, 128), f32)


def scratch_density(entries):
    return [
        pltpu.VMEM((entries, feature_rows, 256), bf16),
        pltpu.VMEM((entries, 16, 128), f32),
        pltpu.VMEM((entries, 32, 256), bf16),
        weights,
    ]


def pair_outputs(count):
    return [
        shaped(8, count, 128, 256, kind=bf16),
        shaped(8, count, 128, 256),
        shaped(8, 40, 128),
    ]


def call(body, outs, operands, specs=None, scratch=(), limit=12, aliases={}):
    return pl.pallas_call(
        body,
        out_shape=tuple(outs),
        in_specs=specs or [vmem] * len(operands),
        out_specs=tuple([vmem] * len(outs)),
        scratch_shapes=list(scratch),
        compiler_params=pltpu.CompilerParams(vmem_limit_bytes=limit << 20),
        input_output_aliases=aliases,
    )(*operands)


def take_side(before, refs, side, rest):
    if len(refs) == 1:
        one, two = refs[0][(0,) + rest], refs[0][(1,) + rest]
    else:
        one, two = refs[0][rest], refs[1][rest]
    return jnp.where(before, one, two) if side == 0 else jnp.where(before, two, one)


def send_shapes(axis, plane):
    if lax.axis_size(axis) == 2:
        return [shaped(2, *plane)]
    return [shaped(*plane), shaped(*plane)]


def put_sends(refs, high, tile_at, rest):
    top, bottom = tile_at(1), tile_at(0)
    one, two = jnp.where(high, top, bottom), jnp.where(high, bottom, top)
    if len(refs) == 1:
        refs[0][(0,) + rest] = one
        refs[0][(1,) + rest] = two
    else:
        refs[0][rest] = one
        refs[1][rest] = two


def receive(axis, sends):
    first, second = routes(axis)
    ways = (first,) if len(sends) == 1 else (first, second)
    got = []
    for send, way in zip(sends, ways):
        got.append(lax.ppermute(send, axis, way))
    return tuple(got)


def pack_y(own, from_z, rows):
    sends = send_shapes("gy", (2, 4, rows, 128))
    n = len(from_z)

    def body(own_ref, *refs):
        got, out = refs[:n], refs[n:]
        high = first_sends_high("gy")
        before = first_gives_before("gz")
        for x in range(2):
            for e in range(4):

                def tile_at(y, x=x, e=e):
                    if 1 <= e <= 2:
                        return own_ref[x, y, e - 1]
                    return take_side(before, got, 0 if e == 0 else 1, (x, y))

                put_sends(out, high, tile_at, (x, e))

    return call(body, sends, (own, *from_z), limit=4)


def pack_x(own, from_z, from_y, rows):
    sends = send_shapes("gx", (4, 4, rows, 128))
    n, m = len(from_z), len(from_y)

    def body(own_ref, *refs):
        got_z, got_y, out = refs[:n], refs[n : n + m], refs[n + m :]
        high = first_sends_high("gx")
        before_z = first_gives_before("gz")
        before_y = first_gives_before("gy")
        for a in range(4):
            for e in range(4):

                def tile_at(x, a=a, e=e):
                    if not 1 <= a <= 2:
                        return take_side(before_y, got_y, 0 if a == 0 else 1, (x, e))
                    if 1 <= e <= 2:
                        return own_ref[x, a - 1, e - 1]
                    return take_side(before_z, got_z, 0 if e == 0 else 1, (x, a - 1))

                put_sends(out, high, tile_at, (a, e))

    return call(body, sends, (own, *from_z, *from_y), limit=4)


inner_dims = {"z": (2, 2), "y": (2, 4), "x": (4, 4)}


def entry_tile(group, before, refs, e, sides):
    _, b = inner_dims[group]
    return take_side(before, refs, sides, (e // b, e % b))


def density_own(own):
    entries, near, place, count = groups["own"]

    def body(own_ref, slopes, pairs, sums, table_ref, feats, masses, columns, weighted):
        def one(c, _):
            x, y, z = parts_of(c)
            tile = own_ref[x, y, z]
            offsets = offsets_of(place(c))
            prepare(tile, offsets, c, feats, masses, columns)
            table, _ = moments(tile, offsets)
            table_ref[c] = column_features(table)
            return 0

        lax.fori_loop(0, 8, one, 0, unroll=8)
        density_pairs(table_ref, (0, 4), near, feats, masses, columns, slopes, pairs, sums, weighted)

    outs = pair_outputs(count) + [
        shaped(8, 128, feature_rows, kind=bf16),
        shaped(entries, feature_rows, 256, kind=bf16),
        shaped(entries, 16, 128),
        shaped(entries, 32, 256, kind=bf16),
    ]
    got = call(body, outs, (own,), scratch=[weights])
    return got[:3], got[3:]


def density_own_rest(kept, features):
    _, near, _, count = groups["own"]

    def body(table_ref, feats, masses, columns, _slopes, _pairs, _sums, slopes, pairs, sums, weighted):
        density_pairs(table_ref, (4, 8), near, feats, masses, columns, slopes, pairs, sums, weighted)

    return call(
        body,
        pair_outputs(count),
        (*features, *kept),
        scratch=[weights],
        aliases={4 + i: i for i in range(3)},
    )


def density_halo(group, axis, received, own_feats):
    entries, near, place, count = groups[group]
    n = len(received)
    half = entries // 2

    def body(*refs):
        got, own_ref = refs[:n], refs[n]
        slopes, pairs, sums, feats, masses, columns, weighted = refs[n + 1 :]
        before = first_gives_before(axis)
        for side in range(2):

            def one(e, _, side=side):
                tile = entry_tile(group, before, got, e, side)
                at = side * half + e
                prepare(tile, offsets_of(place(at)), at, feats, masses, columns)
                return 0

            lax.fori_loop(0, half, one, 0, unroll=min(half, 8))
        density_pairs(own_ref, (0, 8), near, feats, masses, columns, slopes, pairs, sums, weighted)

    return call(body, pair_outputs(count), (*received, own_feats), scratch=scratch_density(entries))


def pressure(own, partials):
    sends = send_shapes("gz", (2, 2, 2, 128))
    outs = [shaped(2, 2, 2, 2, 128), shaped(8, tile_rows, 128)] + sends
    n = len(partials)

    def body(own_ref, *refs):
        pieces, (press, first), out = refs[:n], refs[n : n + 2], refs[n + 2 :]
        high = first_sends_high("gz")
        for x in range(2):
            for y in range(2):
                for z in range(2):
                    c = 4 * x + 2 * y + z
                    table, mass = moments(own_ref[x, y, z], [float(v - 1) for v in (x, y, z)])
                    s = sum(p[c] for p in pieces)
                    gq = s[32:33]
                    t = s[0:8] + s[8:16]
                    m0 = s[16:17] + s[17:18]
                    pos, vel = table[0:3], table[3:6]
                    x_mx = jnp.sum(pos * t[0:3], 0, keepdims=True)
                    x_mv = jnp.sum(pos * t[3:6], 0, keepdims=True)
                    v_mx = jnp.sum(vel * t[0:3], 0, keepdims=True)
                    gr2 = t[6:7] + table[6:7] * m0 - 2.0 * x_mx
                    rho = kernel_norm * (m0 + 3.0 * gq - 4.0 * gr2)
                    div = -20.0 * kernel_norm * (t[7:8] + table[7:8] * m0 - x_mv - v_mx)
                    rho = jnp.where(mass > 0.0, rho, 1.0)
                    compress = jnp.maximum(div / rho, 0.0)
                    weight = own_ref[x, y, z, 7:8] * compress / (compress + 1.0)
                    press[x, y, z] = jnp.concatenate([rho, weight], 0)
                    first[c] = jnp.concatenate(
                        [pos * m0 - t[0:3], div, jnp.zeros((tile_rows - 4, 128), f32)], 0
                    )
        for x in range(2):
            for y in range(2):
                put_sends(out, high, lambda z, x=x, y=y: press[x, y, z], (x, y))

    return call(body, outs, (own, *partials), limit=8)


def spread_own(press):
    def body(press_ref, spread):
        chosen = jnp.where(lax.broadcasted_iota(jnp.int32, (16, 128), 0) < 3, 1.0, 0.0).astype(bf16)
        for c in range(8):
            x, y, z = parts_of(c)
            parts = rows_of(*split3(press_ref[x, y, z, 0:1]))
            parts = jnp.concatenate([parts, jnp.zeros_like(parts)], 0).T.astype(bf16)
            spread[c] = jnp.dot(parts, chosen, preferred_element_type=f32)

    return call(body, [shaped(8, 128, 128)], (press,), limit=4)[0]


def scratch_force(entries):
    return [
        pltpu.VMEM((entries, 16, 128), f32),
        pltpu.VMEM((entries, 32, 256), bf16),
        pltpu.VMEM((entries, 16, 256), bf16),
    ]


def force_outputs():
    return [shaped(8, 32, 128), shaped(8, 16, 128)]


def force_own(own, press, spread, kept, ready=False):
    entries, near, place, _ = groups["own"]

    def body(own_ref, press_ref, spread_ref, slopes, visc, sums, pulls, rhos, columns, gradients):
        def one(c, _):
            x, y, z = parts_of(c)
            prepare_force(
                own_ref[x, y, z], offsets_of(place(c)), press_ref[x, y, z], c, rhos, columns, gradients
            )
            return 0

        lax.fori_loop(0, 8, one, 0, unroll=8)

        force_pairs(near, spread_ref, rhos, columns, gradients, slopes, visc, sums, pulls, ready)

    return call(body, force_outputs(), (own, press, spread, *kept), scratch=scratch_force(entries))


def force_halo(group, axis, received, press_received, spread, kept, ready=False):
    entries, near, place, _ = groups[group]
    n = len(received)
    half = entries // 2

    def body(*refs):
        got, got_press, spread_ref = refs[:n], refs[n : 2 * n], refs[2 * n]
        slopes, visc, sums, pulls, rhos, columns, gradients = refs[2 * n + 1 :]
        before = first_gives_before(axis)
        for side in range(2):

            def one(e, _, side=side):
                tile = entry_tile(group, before, got, e, side)
                fields = entry_tile(group, before, got_press, e, side)
                at = side * half + e
                prepare_force(tile, offsets_of(place(at)), fields, at, rhos, columns, gradients)
                return 0

            lax.fori_loop(0, half, one, 0, unroll=min(half, 8))

        force_pairs(near, spread_ref, rhos, columns, gradients, slopes, visc, sums, pulls, ready)

    return call(
        body,
        force_outputs(),
        (*received, *press_received, spread, *kept),
        scratch=scratch_force(entries),
    )


def finish(own, press, first, partials):
    outs = [shaped(2, 2, 2, 128), shaped(3, 2, 2, 2, 128), shaped(2, 2, 2, 128)]
    n = len(partials)

    def body(own_ref, press_ref, first_ref, *refs):
        pieces, (density, accel, heating) = refs[:n], refs[n:]
        for x in range(2):
            for y in range(2):
                for z in range(2):
                    c = 4 * x + 2 * y + z
                    table, mass = moments(own_ref[x, y, z], [float(v - 1) for v in (x, y, z)])
                    u = sum(p[c] for p in pieces[0::2])
                    v = sum(p[c] for p in pieces[1::2])
                    plain, scaled = u[0:8] + u[8:16], u[16:24] + u[24:32]
                    a0, b0 = plain[6:7], scaled[6:7]
                    g = v[0:8] + v[8:16]
                    rho, weight = press_ref[x, y, z, 0:1], press_ref[x, y, z, 1:2]
                    inverse = 1.0 / rho
                    mixed = weight * plain + scaled
                    zero = weight * a0 + b0
                    pos, vel = table[0:3], table[3:6]
                    total = (
                        inverse * first_ref[c, 0:3]
                        + (pos * g[3:4] - g[0:3])
                        - (pos * zero - mixed[0:3])
                    )
                    live = jnp.where(mass > 0.0, 1.0, 0.0)
                    push = (20.0 * kernel_norm) * live * total
                    work = (
                        mixed[7:8]
                        + table[7:8] * zero
                        - jnp.sum(pos * mixed[3:6], 0, keepdims=True)
                        - jnp.sum(vel * mixed[0:3], 0, keepdims=True)
                    )
                    warm = live * (first_ref[c, 3:4] * inverse + (10.0 * kernel_norm) * work)
                    density[x, y, z : z + 1, :] = rho
                    for i in range(3):
                        accel[i, x, y, z : z + 1, :] = push[i : i + 1]
                    heating[x, y, z : z + 1, :] = warm

    return call(body, outs, (own, press, first, *partials), limit=8)


def gather_own(fields, counts):
    sends = send_shapes("gz", (2, 2, tile_rows, 128))

    def body(fields_ref, counts_ref, own, *out):
        high = first_sends_high("gz")
        alone = row_ids() == 6
        lanes = lax.broadcasted_iota(jnp.int32, (tile_rows, 128), 1)
        for x in range(2):
            for y in range(2):
                for z in range(2):
                    dead = lanes >= counts_ref[x, y : y + 1, z : z + 1]
                    tile = rows_of(*(fields_ref[i, x, y, z : z + 1, :] for i in range(tile_rows)))
                    own[x, y, z] = jnp.where(alone & dead, 0.0, tile)
        for x in range(2):
            for y in range(2):
                put_sends(out, high, lambda z, x=x, y=y: own[x, y, z], (x, y))

    return call(body, [shaped(2, 2, 2, tile_rows, 128)] + sends, (fields, counts), limit=4)


def per_block(positions, velocities, masses, alphas, counts):
    fields = jnp.concatenate([positions, velocities, masses[None], alphas[None]], 0)
    own, *sends = gather_own(fields, counts)
    from_z = receive("gz", sends)
    half, features = density_own(own)
    own_feats = features[0]
    from_y = receive("gy", pack_y(own, from_z, tile_rows))
    *kept_z, sums_z = density_halo("z", "gz", from_z, own_feats)
    from_x = receive("gx", pack_x(own, from_z, from_y, tile_rows))
    *kept_y, sums_y = density_halo("y", "gy", from_y, own_feats)
    *kept_own, sums_own = density_own_rest(half, features)
    *kept_x, sums_x = density_halo("x", "gx", from_x, own_feats)
    press, first, *sends = pressure(own, (sums_own, sums_z, sums_y, sums_x))
    press_z = receive("gz", sends)
    spread = spread_own(press)
    forces = list(force_own(own, press, spread, kept_own))
    kept_x[1] = viscous("x", *kept_x)
    press_y = receive("gy", pack_y(press, press_z, 2))
    forces += force_halo("z", "gz", from_z, press_z, spread, kept_z)
    press_x = receive("gx", pack_x(press, press_z, press_y, 2))
    forces += force_halo("y", "gy", from_y, press_y, spread, kept_y)
    forces += force_halo("x", "gx", from_x, press_x, spread, kept_x, ready=True)
    return finish(own, press, first, forces)


neighbour_shifts = [
    (shift_x, shift_y, shift_z)
    for shift_x in (-1, 0, 1)
    for shift_y in (-1, 0, 1)
    for shift_z in (-1, 0, 1)
]


def extended(shard, sides, width):
    for axis, dim in sides:
        peers, length = (lax.axis_size(axis), shard.shape[dim])
        up = [(i, (i + 1) % peers) for i in range(peers)]
        down = [(j, i) for i, j in up]
        last = lax.slice_in_dim(shard, length - width, length, axis=dim)
        leading = lax.slice_in_dim(shard, 0, width, axis=dim)
        before = lax.ppermute(last, axis, up)
        after = lax.ppermute(leading, axis, down)
        shard = jnp.concatenate([before, shard, after], axis=dim)
    return shard


def pair_geometry(own_rows, neighbour, cell_shift):
    offset_parts = [
        own_rows[axis_id][:, :, None] - neighbour[axis_id][:, None, :] - float(cell_shift[axis_id])
        for axis_id in range(3)
    ]
    dist_sq = (
        offset_parts[0] * offset_parts[0]
        + offset_parts[1] * offset_parts[1]
        + offset_parts[2] * offset_parts[2]
    )
    scaled = jnp.minimum(jnp.sqrt(dist_sq), 1.0)
    falloff = 1.0 - scaled
    kernel_value = kernel_norm * falloff**4 * (1.0 + 4.0 * scaled)
    kernel_slope = -20.0 * kernel_norm * falloff**3
    approach = sum(
        (
            (own_rows[3 + axis_id][:, :, None] - neighbour[3 + axis_id][:, None, :])
            * offset_parts[axis_id]
            for axis_id in range(3)
        )
    )
    return (offset_parts, dist_sq, kernel_value, kernel_slope, approach)


def density_terms(own_rows, neighbour, cell_shift):
    _, _, kernel_value, kernel_slope, approach = pair_geometry(own_rows, neighbour, cell_shift)
    other_mass = neighbour[6][:, None, :]
    return (
        jnp.sum(other_mass * kernel_value, -1),
        jnp.sum(other_mass * kernel_slope * approach, -1),
    )


def force_terms(own_rows, neighbour, cell_shift):
    offset_parts, dist_sq, _, kernel_slope, approach = pair_geometry(
        own_rows, neighbour, cell_shift
    )
    rho_own = own_rows[7][:, :, None]
    rho_other = neighbour[7][:, None, :]
    converge = jnp.minimum(approach, 0.0) / (dist_sq + 0.01)
    viscous = (
        -(own_rows[8][:, :, None] + neighbour[8][:, None, :]) * converge / (rho_own + rho_other)
    )
    mslope = neighbour[6][:, None, :] * kernel_slope
    pair_force = mslope * (1.0 / rho_own + 1.0 / rho_other + viscous)
    accel_terms = jnp.stack(
        [-jnp.sum(pair_force * offset_parts[axis_id], -1) for axis_id in range(3)], 0
    )
    heating = jnp.sum(mslope * (1.0 / rho_own + 0.5 * viscous) * approach, -1)
    return (accel_terms, heating)


def switch_fields(density, div_sum, live_rows, weights):
    rho_live = jnp.where(live_rows > 0, density, 1.0)
    compress = jnp.maximum(div_sum / rho_live, 0.0)
    return jnp.stack([rho_live, weights * compress / (compress + 1.0)], 0)


def sweep(terms, padded):
    count = padded.shape[0]
    slot_count = padded.shape[-1]
    span_x = padded.shape[1] - 2
    span_y = padded.shape[2] - 2
    span_z = padded.shape[3] - 2
    own_rows = padded[:, 1 : span_x + 1, 1 : span_y + 1, 1 : span_z + 1].reshape(
        count, -1, slot_count
    )
    totals = None
    for cell_shift in neighbour_shifts:
        neighbour = padded[
            :,
            1 + cell_shift[0] : 1 + cell_shift[0] + span_x,
            1 + cell_shift[1] : 1 + cell_shift[1] + span_y,
            1 + cell_shift[2] : 1 + cell_shift[2] + span_z,
        ]
        result = terms(own_rows, neighbour.reshape(count, -1, slot_count), cell_shift)
        totals = (
            result
            if totals is None
            else jax.tree.map(lambda left, right: left + right, totals, result)
        )
    return totals


def per_device(positions, velocities, masses, alphas, counts):
    slot_count = positions.shape[-1]
    cell_shape = positions.shape[1:4]
    occupied = (
        jnp.arange(slot_count, dtype=jnp.int32)[None, None, None, :] < counts[..., None]
    ).astype(jnp.float32)
    live_mass = masses * occupied
    carried = jnp.concatenate([positions, velocities, live_mass[None]], 0)
    padded = extended(carried, (("gx", 1), ("gy", 2), ("gz", 3)), 1)
    density, div_sum = sweep(density_terms, padded)
    live_rows = occupied.reshape(-1, slot_count)
    weights = alphas.reshape(-1, slot_count)
    pressure_fields = switch_fields(density, div_sum, live_rows, weights).reshape(
        (2,) + cell_shape + (slot_count,)
    )
    own_density = pressure_fields[0]
    pressure_pad = extended(pressure_fields, (("gx", 1), ("gy", 2), ("gz", 3)), 1)
    fields = jnp.concatenate([padded, pressure_pad], 0)
    accel_total, heat_total = sweep(force_terms, fields)
    acceleration = accel_total.reshape((3,) + cell_shape + (slot_count,)) * occupied[None]
    heating = heat_total.reshape(cell_shape + (slot_count,)) * occupied
    return (own_density, acceleration, heating)


def per_device_any(positions, velocities, masses, alphas, counts):
    if positions.shape[1:] == (2, 2, 2, 128):
        return per_block(positions, velocities, masses, alphas, counts)
    return per_device(positions, velocities, masses, alphas, counts)


def solution(mesh):
    return jax.shard_map(
        per_device_any,
        mesh=mesh,
        in_specs=(
            P(None, "gx", "gy", "gz", None),
            P(None, "gx", "gy", "gz", None),
            P("gx", "gy", "gz", None),
            P("gx", "gy", "gz", None),
            P("gx", "gy", "gz"),
        ),
        out_specs=(
            P("gx", "gy", "gz", None),
            P(None, "gx", "gy", "gz", None),
            P("gx", "gy", "gz", None),
        ),
        check_vma=False,
    )
```

```python
import math

import jax
import jax.numpy as jnp
from jax import lax
from jax.experimental import pallas as pl
from jax.experimental.pallas import tpu as pltpu
from jax.sharding import PartitionSpec as P


f32 = jnp.float32
bf16 = jnp.bfloat16
kernel_norm = 21.0 / (2.0 * math.pi)
tile_rows = 8
feature_rows = 48
tiny = 1e-12
together = 4

vmem = pl.BlockSpec(memory_space=pltpu.VMEM)


def shaped(*dims, kind=f32):
    return jax.ShapeDtypeStruct(dims, kind)


def paired(axis):
    return lax.axis_size(axis) % 2 == 0


def first_sends_high(axis):
    return lax.axis_index(axis) % 2 == 0 if paired(axis) else lax.axis_index(axis) >= 0


def first_gives_before(axis):
    return lax.axis_index(axis) % 2 == 1 if paired(axis) else lax.axis_index(axis) >= 0


def routes(axis):
    peers = lax.axis_size(axis)
    if peers % 2 == 0:
        first = [(i, i + 1 if i % 2 == 0 else i - 1) for i in range(peers)]
        second = [(i, (i - 1 if i % 2 == 0 else i + 1) % peers) for i in range(peers)]
    else:
        first = [(i, (i + 1) % peers) for i in range(peers)]
        second = [(i, (i - 1) % peers) for i in range(peers)]
    return first, second


def split3(value):
    high = value.astype(bf16).astype(f32)
    rest = value - high
    middle = rest.astype(bf16).astype(f32)
    return high, middle, rest - middle


def row_ids():
    return lax.broadcasted_iota(jnp.int32, (tile_rows, 128), 0)


def rows_of(*rows):
    ids = row_ids()
    out = jnp.zeros((tile_rows, 128), f32)
    for place, row in enumerate(rows):
        out = jnp.where(ids == place, row, out)
    return out


def moments(tile, offsets):
    ids = row_ids()
    shift = jnp.where(ids == 0, offsets[0], jnp.where(ids == 1, offsets[1], jnp.where(ids == 2, offsets[2], 0.0)))
    high, low, _ = split3(tile + shift)
    moved = high + low.astype(bf16).astype(f32)
    x, y, z, vx, vy, vz = (moved[i : i + 1] for i in range(6))
    sq = x * x + y * y + z * z
    xv = x * vx + y * vy + z * vz
    return jnp.where(ids == 6, sq, jnp.where(ids == 7, xv, moved)), tile[6:7]


def column_features(table):
    p1, p2, p3 = split3(table)
    ids = row_ids()
    extra = jnp.where(ids < 3, 1.0, jnp.where(ids >= 6, p3, 0.0))
    return jnp.concatenate([p1, p1, p2, p2, extra, jnp.zeros_like(extra)], 0).T.astype(bf16)


def row_features(table):
    ids = row_ids()
    sq = split3(table[6:7])
    xv = split3(table[7:8])
    down = pltpu.roll(table, 3, 0)
    up = pltpu.roll(table, 5, 0)
    left = jnp.where(ids < 3, -2.0 * table, jnp.where(ids == 6, 1.0, 0.0))
    right = jnp.where(ids < 3, -up, jnp.where(ids < 6, -down, jnp.where(ids == 7, 1.0, 0.0)))
    halves = []
    for part, fixed in ((left, sq), (right, xv)):
        q1, q2, _ = split3(part)
        extra = rows_of(*fixed) + jnp.where(ids >= 6, part, 0.0)
        halves.append(jnp.concatenate([q1, q2, q1, q2, extra, jnp.zeros_like(extra)], 0))
    return jnp.concatenate(halves, 1).astype(bf16)


def mass_columns(table, mass):
    weighted = mass * table
    w1, w2, _ = split3(weighted)
    m1, m2, _ = split3(mass)
    extra = rows_of(m1, m2)
    left = jnp.concatenate([w1, w2, extra, jnp.zeros_like(extra)], 0).astype(bf16)
    return jnp.concatenate([left, left], 1)


def prepare(tile, offsets, at, feats, masses, columns):
    table, mass = moments(tile, offsets)
    feats[at] = row_features(table)
    masses[at] = jnp.broadcast_to(mass, (16, 128))
    columns[at] = mass_columns(table, mass)


def over_lanes(left, right):
    return lax.dot_general(left, right, (((1,), (1,)), ((), ())), preferred_element_type=f32)


def pipelined(tiles, stages):
    for step in range(len(tiles) + len(stages) - 1):
        for lag, stage in enumerate(stages):
            if 0 <= step - lag < len(tiles):
                stage(*tiles[step - lag])


def idle(*tile):
    pass


def over_cells(body):
    lax.fori_loop(0, 8 // together, lambda i, _: body([i * together + j for j in range(together)]), 0)


def density_pairs(own, near, feats, masses, columns, slopes, pairs, sums, weighted):
    ones = jnp.ones((tile_rows, 256), bf16)

    def some(group):
        both, sofar = {}, {}
        picks = [near(c) for c in group]
        tiles = [(j, k) for j in range(len(group)) for k in range(len(picks[j]))]

        def geometry(j, k):
            pair = both[j, k] = jnp.dot(own[group[j]], feats[picks[j][k]], preferred_element_type=f32)
            pairs[group[j], k] = pair

        def terms(j, k):
            c, n = group[j], picks[j][k]
            pair = both.pop((j, k))
            mass = masses[n]
            for r in range(0, 128, 16):
                at = slice(r, r + 16)
                dist = jnp.maximum(pair[at, :128], tiny)
                q = dist * lax.rsqrt(dist)
                fall = jnp.maximum(1.0 - q, 0.0)
                g = fall * fall * fall
                part = g * q * mass
                weighted[j, at] = part if k == 0 else weighted[j, at] + part
                high = g.astype(bf16)
                slopes[c, k, at, :128] = high
                slopes[c, k, at, 128:] = (g - high.astype(f32)).astype(bf16)

        def reduce(j, k):
            c, n = group[j], picks[j][k]
            part = over_lanes(columns[n], slopes[c, k])
            sofar[j] = part if j not in sofar else sofar[j] + part
            if k == len(picks[j]) - 1:
                sums[c, :32] = sofar[j]
                high = weighted[j].astype(bf16)
                low = (weighted[j] - high.astype(f32)).astype(bf16)
                sums[c, 32:] = over_lanes(ones, jnp.concatenate([high, low], 1))

        pipelined(tiles, (geometry, idle, terms, idle, reduce))
        return 0

    over_cells(some)


def prepare_force(tile, offsets, press, at, rhos, columns, gradients):
    table, mass = moments(tile, offsets)
    rho = press[0:1]
    weight = press[1:2]
    heavy = mass * jnp.where(row_ids() == 6, 1.0, table)
    h1, h2, _ = split3(heavy)
    s1, s2, _ = split3(weight * heavy)
    left = jnp.concatenate([h1, h2, s1, s2], 0).astype(bf16)
    columns[at] = jnp.concatenate([left, left], 1)
    light = (mass / rho) * jnp.where(row_ids() < 3, table, 1.0)
    l1, l2, _ = split3(light)
    left = jnp.concatenate([l1, l2], 0).astype(bf16)
    gradients[at] = jnp.concatenate([left, left], 1)
    rhos[at] = jnp.broadcast_to(rho, (16, 128))


def force_pairs(near, spread, rhos, columns, gradients, slopes, pairs, sums, pulls):
    def some(group):
        mixed, sofar, pulled = {}, {}, {}
        picks = [near(c) for c in group]
        tiles = [(j, k) for j, c in enumerate(group) for k in range(len(near(c)))]

        def terms(j, k):
            c, n = group[j], picks[j][k]
            highs, lows = [], []
            theirs = rhos[n]
            for r in range(0, 128, 16):
                at = slice(r, r + 16)
                below = theirs + spread[c, at]
                g = slopes[c, k, at, :128].astype(f32) + slopes[c, k, at, 128:].astype(f32)
                run = jnp.minimum(pairs[c, k, at, 128:], 0.0)
                t = g * run * (1.0 / ((pairs[c, k, at, :128] + 0.01) * below))
                high = t.astype(bf16)
                highs.append(high)
                lows.append((t - high.astype(f32)).astype(bf16))
            mixed[j, k] = jnp.concatenate([jnp.concatenate(highs, 0), jnp.concatenate(lows, 0)], 1)

        def reduce(j, k):
            c, n = group[j], picks[j][k]
            part = over_lanes(columns[n], mixed.pop((j, k)))
            pull = over_lanes(gradients[n], slopes[c, k])
            sofar[j] = part if j not in sofar else sofar[j] + part
            pulled[j] = pull if j not in pulled else pulled[j] + pull
            if k == len(picks[j]) - 1:
                sums[c] = sofar[j]
                pulls[c] = pulled[j]

        pipelined(tiles, (terms, reduce))
        return 0

    over_cells(some)


def parts_of(c):
    return c // 4, (c // 2) % 2, c % 2


def flat(*pairs):
    at = 0
    for size, index in pairs:
        at = at * size + index
    return at


def near_own(c):
    return list(range(8))


def near_z(c):
    _, _, cz = parts_of(c)
    return [flat((2, cz), (2, x), (2, y)) for x in range(2) for y in range(2)]


def near_x(c):
    cx, _, cz = parts_of(c)
    return [flat((2, cx), (2, y), (4, cz + dz)) for y in range(2) for dz in range(3)]


def near_y(c):
    cx, cy, cz = parts_of(c)
    return [flat((2, cy), (4, cx + dx), (4, cz + dz)) for dx in range(3) for dz in range(3)]


def place_own(e):
    x, y, z = parts_of(e)
    return x - 1, y - 1, z - 1


def place_z(e):
    side, x, y = parts_of(e)
    return x - 1, y - 1, 3 * side - 2


def place_x(e):
    return 3 * (e // 8) - 2, (e // 4) % 2 - 1, e % 4 - 2


def place_y(e):
    return (e // 4) % 4 - 2, 3 * (e // 16) - 2, e % 4 - 2


def offsets_of(place):
    return [jnp.asarray(v, jnp.int32).astype(f32) for v in place]


groups = {
    "own": (8, near_own, place_own, 8),
    "z": (8, near_z, place_z, 4),
    "x": (16, near_x, place_x, 6),
    "y": (32, near_y, place_y, 9),
}


weights = pltpu.VMEM((together, 128, 128), f32)


def scratch_density(entries):
    return [
        pltpu.VMEM((entries, feature_rows, 256), bf16),
        pltpu.VMEM((entries, 16, 128), f32),
        pltpu.VMEM((entries, 32, 256), bf16),
        weights,
    ]


def pair_outputs(count):
    return [
        shaped(8, count, 128, 256, kind=bf16),
        shaped(8, count, 128, 256),
        shaped(8, 40, 128),
    ]


def call(body, outs, operands, specs=None, scratch=(), limit=12):
    return pl.pallas_call(
        body,
        out_shape=tuple(outs),
        in_specs=specs or [vmem] * len(operands),
        out_specs=tuple([vmem] * len(outs)),
        scratch_shapes=list(scratch),
        compiler_params=pltpu.CompilerParams(vmem_limit_bytes=limit << 20),
    )(*operands)


def take_side(before, refs, side, rest):
    if len(refs) == 1:
        one, two = refs[0][(0,) + rest], refs[0][(1,) + rest]
    else:
        one, two = refs[0][rest], refs[1][rest]
    return jnp.where(before, one, two) if side == 0 else jnp.where(before, two, one)


def send_shapes(axis, plane):
    if lax.axis_size(axis) == 2:
        return [shaped(2, *plane)]
    return [shaped(*plane), shaped(*plane)]


def put_sends(refs, high, tile_at, rest):
    top, bottom = tile_at(1), tile_at(0)
    one, two = jnp.where(high, top, bottom), jnp.where(high, bottom, top)
    if len(refs) == 1:
        refs[0][(0,) + rest] = one
        refs[0][(1,) + rest] = two
    else:
        refs[0][rest] = one
        refs[1][rest] = two


def receive(axis, sends):
    first, second = routes(axis)
    ways = (first,) if len(sends) == 1 else (first, second)
    got = []
    for send, way in zip(sends, ways):
        got.append(lax.ppermute(send, axis, way))
    return tuple(got)


def pack_x(own, from_z, rows):
    sends = send_shapes("gx", (2, 4, rows, 128))
    n = len(from_z)

    def body(own_ref, *refs):
        got, out = refs[:n], refs[n:]
        high = first_sends_high("gx")
        before = first_gives_before("gz")
        for y in range(2):
            for e in range(4):

                def tile_at(x, y=y, e=e):
                    if 1 <= e <= 2:
                        return own_ref[x, y, e - 1]
                    return take_side(before, got, 0 if e == 0 else 1, (x, y))

                put_sends(out, high, tile_at, (y, e))

    return call(body, sends, (own, *from_z), limit=4)


def pack_y(own, from_z, from_x, rows):
    sends = send_shapes("gy", (4, 4, rows, 128))
    n, m = len(from_z), len(from_x)

    def body(own_ref, *refs):
        got_z, got_x, out = refs[:n], refs[n : n + m], refs[n + m :]
        high = first_sends_high("gy")
        before_z = first_gives_before("gz")
        before_x = first_gives_before("gx")
        for a in range(4):
            for e in range(4):

                def tile_at(y, a=a, e=e):
                    if not 1 <= a <= 2:
                        return take_side(before_x, got_x, 0 if a == 0 else 1, (y, e))
                    if 1 <= e <= 2:
                        return own_ref[a - 1, y, e - 1]
                    return take_side(before_z, got_z, 0 if e == 0 else 1, (a - 1, y))

                put_sends(out, high, tile_at, (a, e))

    return call(body, sends, (own, *from_z, *from_x), limit=4)


inner_dims = {"z": (2, 2), "x": (2, 4), "y": (4, 4)}


def entry_tile(group, before, refs, e, sides):
    _, b = inner_dims[group]
    return take_side(before, refs, sides, (e // b, e % b))


def density_own(own):
    entries, near, place, count = groups["own"]

    def body(own_ref, slopes, pairs, sums, table_ref, feats, masses, columns, weighted):
        def one(c, _):
            x, y, z = parts_of(c)
            tile = own_ref[x, y, z]
            offsets = offsets_of(place(c))
            prepare(tile, offsets, c, feats, masses, columns)
            table, _ = moments(tile, offsets)
            table_ref[c] = column_features(table)
            return 0

        lax.fori_loop(0, 8, one, 0, unroll=8)
        density_pairs(table_ref, near, feats, masses, columns, slopes, pairs, sums, weighted)

    outs = pair_outputs(count) + [shaped(8, 128, feature_rows, kind=bf16)]
    return call(body, outs, (own,), scratch=scratch_density(entries))


def density_halo(group, axis, received, own_feats):
    entries, near, place, count = groups[group]
    n = len(received)
    half = entries // 2

    def body(*refs):
        got, own_ref = refs[:n], refs[n]
        slopes, pairs, sums, feats, masses, columns, weighted = refs[n + 1 :]
        before = first_gives_before(axis)
        for side in range(2):

            def one(e, _, side=side):
                tile = entry_tile(group, before, got, e, side)
                at = side * half + e
                prepare(tile, offsets_of(place(at)), at, feats, masses, columns)
                return 0

            lax.fori_loop(0, half, one, 0, unroll=min(half, 8))
        density_pairs(own_ref, near, feats, masses, columns, slopes, pairs, sums, weighted)

    return call(body, pair_outputs(count), (*received, own_feats), scratch=scratch_density(entries))


def pressure(own, partials):
    sends = send_shapes("gz", (2, 2, 2, 128))
    outs = [shaped(2, 2, 2, 2, 128), shaped(8, tile_rows, 128)] + sends
    n = len(partials)

    def body(own_ref, *refs):
        pieces, (press, first), out = refs[:n], refs[n : n + 2], refs[n + 2 :]
        high = first_sends_high("gz")
        for x in range(2):
            for y in range(2):
                for z in range(2):
                    c = 4 * x + 2 * y + z
                    table, mass = moments(own_ref[x, y, z], [float(v - 1) for v in (x, y, z)])
                    s = sum(p[c] for p in pieces)
                    gq = s[32:33]
                    t = s[0:8] + s[8:16]
                    m0 = s[16:17] + s[17:18]
                    pos, vel = table[0:3], table[3:6]
                    x_mx = jnp.sum(pos * t[0:3], 0, keepdims=True)
                    x_mv = jnp.sum(pos * t[3:6], 0, keepdims=True)
                    v_mx = jnp.sum(vel * t[0:3], 0, keepdims=True)
                    gr2 = t[6:7] + table[6:7] * m0 - 2.0 * x_mx
                    rho = kernel_norm * (m0 + 3.0 * gq - 4.0 * gr2)
                    div = -20.0 * kernel_norm * (t[7:8] + table[7:8] * m0 - x_mv - v_mx)
                    rho = jnp.where(mass > 0.0, rho, 1.0)
                    compress = jnp.maximum(div / rho, 0.0)
                    weight = own_ref[x, y, z, 7:8] * compress / (compress + 1.0)
                    press[x, y, z] = jnp.concatenate([rho, weight], 0)
                    first[c] = jnp.concatenate(
                        [pos * m0 - t[0:3], div, jnp.zeros((tile_rows - 4, 128), f32)], 0
                    )
        for x in range(2):
            for y in range(2):
                put_sends(out, high, lambda z, x=x, y=y: press[x, y, z], (x, y))

    return call(body, outs, (own, *partials), limit=8)


def spread_own(press):
    def body(press_ref, spread):
        chosen = jnp.where(lax.broadcasted_iota(jnp.int32, (16, 128), 0) < 3, 1.0, 0.0).astype(bf16)
        for c in range(8):
            x, y, z = parts_of(c)
            parts = rows_of(*split3(press_ref[x, y, z, 0:1]))
            parts = jnp.concatenate([parts, jnp.zeros_like(parts)], 0).T.astype(bf16)
            spread[c] = jnp.dot(parts, chosen, preferred_element_type=f32)

    return call(body, [shaped(8, 128, 128)], (press,), limit=4)[0]


def scratch_force(entries):
    return [
        pltpu.VMEM((entries, 16, 128), f32),
        pltpu.VMEM((entries, 32, 256), bf16),
        pltpu.VMEM((entries, 16, 256), bf16),
    ]


def force_outputs():
    return [shaped(8, 32, 128), shaped(8, 16, 128)]


def force_own(own, press, spread, kept):
    entries, near, place, _ = groups["own"]

    def body(own_ref, press_ref, spread_ref, slopes, pairs, sums, pulls, rhos, columns, gradients):
        def one(c, _):
            x, y, z = parts_of(c)
            prepare_force(
                own_ref[x, y, z], offsets_of(place(c)), press_ref[x, y, z], c, rhos, columns, gradients
            )
            return 0

        lax.fori_loop(0, 8, one, 0, unroll=8)

        force_pairs(near, spread_ref, rhos, columns, gradients, slopes, pairs, sums, pulls)

    return call(body, force_outputs(), (own, press, spread, *kept), scratch=scratch_force(entries))


def force_halo(group, axis, received, press_received, spread, kept):
    entries, near, place, _ = groups[group]
    n = len(received)
    half = entries // 2

    def body(*refs):
        got, got_press, spread_ref = refs[:n], refs[n : 2 * n], refs[2 * n]
        slopes, pairs, sums, pulls, rhos, columns, gradients = refs[2 * n + 1 :]
        before = first_gives_before(axis)
        for side in range(2):

            def one(e, _, side=side):
                tile = entry_tile(group, before, got, e, side)
                fields = entry_tile(group, before, got_press, e, side)
                at = side * half + e
                prepare_force(tile, offsets_of(place(at)), fields, at, rhos, columns, gradients)
                return 0

            lax.fori_loop(0, half, one, 0, unroll=min(half, 8))

        force_pairs(near, spread_ref, rhos, columns, gradients, slopes, pairs, sums, pulls)

    return call(
        body,
        force_outputs(),
        (*received, *press_received, spread, *kept),
        scratch=scratch_force(entries),
    )


def finish(own, press, first, partials):
    outs = [shaped(2, 2, 2, 128), shaped(3, 2, 2, 2, 128), shaped(2, 2, 2, 128)]
    n = len(partials)

    def body(own_ref, press_ref, first_ref, *refs):
        pieces, (density, accel, heating) = refs[:n], refs[n:]
        for x in range(2):
            for y in range(2):
                for z in range(2):
                    c = 4 * x + 2 * y + z
                    table, mass = moments(own_ref[x, y, z], [float(v - 1) for v in (x, y, z)])
                    u = sum(p[c] for p in pieces[0::2])
                    v = sum(p[c] for p in pieces[1::2])
                    plain, scaled = u[0:8] + u[8:16], u[16:24] + u[24:32]
                    a0, b0 = plain[6:7], scaled[6:7]
                    g = v[0:8] + v[8:16]
                    rho, weight = press_ref[x, y, z, 0:1], press_ref[x, y, z, 1:2]
                    inverse = 1.0 / rho
                    mixed = weight * plain + scaled
                    zero = weight * a0 + b0
                    pos, vel = table[0:3], table[3:6]
                    total = (
                        inverse * first_ref[c, 0:3]
                        + (pos * g[3:4] - g[0:3])
                        - (pos * zero - mixed[0:3])
                    )
                    live = jnp.where(mass > 0.0, 1.0, 0.0)
                    push = (20.0 * kernel_norm) * live * total
                    work = (
                        mixed[7:8]
                        + table[7:8] * zero
                        - jnp.sum(pos * mixed[3:6], 0, keepdims=True)
                        - jnp.sum(vel * mixed[0:3], 0, keepdims=True)
                    )
                    warm = live * (first_ref[c, 3:4] * inverse + (10.0 * kernel_norm) * work)
                    density[x, y, z : z + 1, :] = rho
                    for i in range(3):
                        accel[i, x, y, z : z + 1, :] = push[i : i + 1]
                    heating[x, y, z : z + 1, :] = warm

    return call(body, outs, (own, press, first, *partials), limit=8)


def gather_own(*arguments):
    sends = send_shapes("gz", (2, 2, tile_rows, 128))

    def body(*refs):
        sources, own, out = refs[:5], refs[5], refs[6 : 6 + len(sends)]
        held, arrived = refs[6 + len(sends) : -1], refs[-1]
        copies = [pltpu.make_async_copy(a, b, arrived.at[i]) for i, (a, b) in enumerate(zip(sources, held))]
        for copy in copies:
            copy.start()
        for copy in copies:
            copy.wait()
        pos, vel, mass, alpha, count = held
        high = first_sends_high("gz")
        lanes = lax.broadcasted_iota(jnp.int32, (1, 128), 1)
        for x in range(2):
            for y in range(2):
                for z in range(2):
                    dead = lanes >= count[x, y : y + 1, z : z + 1]
                    own[x, y, z] = rows_of(
                        *(pos[i, x, y, z : z + 1, :] for i in range(3)),
                        *(vel[i, x, y, z : z + 1, :] for i in range(3)),
                        jnp.where(dead, 0.0, mass[x, y, z : z + 1, :]),
                        alpha[x, y, z : z + 1, :],
                    )
        for x in range(2):
            for y in range(2):
                put_sends(out, high, lambda z, x=x, y=y: own[x, y, z], (x, y))

    scratch = [pltpu.VMEM(a.shape, a.dtype) for a in arguments] + [pltpu.SemaphoreType.DMA((5,))]
    return call(
        body,
        [shaped(2, 2, 2, tile_rows, 128)] + sends,
        [pltpu.with_memory_space_constraint(a, pltpu.HBM) for a in arguments],
        specs=[pl.BlockSpec(memory_space=pltpu.HBM)] * 5,
        scratch=scratch,
        limit=4,
    )


def per_block(positions, velocities, masses, alphas, counts):
    own, *sends = gather_own(positions, velocities, masses, alphas, counts)
    from_z = receive("gz", sends)
    *kept_own, sums_own, own_feats = density_own(own)
    from_x = receive("gx", pack_x(own, from_z, tile_rows))
    *kept_z, sums_z = density_halo("z", "gz", from_z, own_feats)
    from_y = receive("gy", pack_y(own, from_z, from_x, tile_rows))
    *kept_x, sums_x = density_halo("x", "gx", from_x, own_feats)
    *kept_y, sums_y = density_halo("y", "gy", from_y, own_feats)
    press, first, *sends = pressure(own, (sums_own, sums_z, sums_x, sums_y))
    press_z = receive("gz", sends)
    spread = spread_own(press)
    forces = list(force_own(own, press, spread, kept_own))
    press_x = receive("gx", pack_x(press, press_z, 2))
    forces += force_halo("z", "gz", from_z, press_z, spread, kept_z)
    press_y = receive("gy", pack_y(press, press_z, press_x, 2))
    forces += force_halo("x", "gx", from_x, press_x, spread, kept_x)
    forces += force_halo("y", "gy", from_y, press_y, spread, kept_y)
    return finish(own, press, first, forces)


neighbour_shifts = [
    (shift_x, shift_y, shift_z)
    for shift_x in (-1, 0, 1)
    for shift_y in (-1, 0, 1)
    for shift_z in (-1, 0, 1)
]


def extended(shard, sides, width):
    for axis, dim in sides:
        peers, length = (lax.axis_size(axis), shard.shape[dim])
        up = [(i, (i + 1) % peers) for i in range(peers)]
        down = [(j, i) for i, j in up]
        last = lax.slice_in_dim(shard, length - width, length, axis=dim)
        leading = lax.slice_in_dim(shard, 0, width, axis=dim)
        before = lax.ppermute(last, axis, up)
        after = lax.ppermute(leading, axis, down)
        shard = jnp.concatenate([before, shard, after], axis=dim)
    return shard


def pair_geometry(own_rows, neighbour, cell_shift):
    offset_parts = [
        own_rows[axis_id][:, :, None] - neighbour[axis_id][:, None, :] - float(cell_shift[axis_id])
        for axis_id in range(3)
    ]
    dist_sq = (
        offset_parts[0] * offset_parts[0]
        + offset_parts[1] * offset_parts[1]
        + offset_parts[2] * offset_parts[2]
    )
    scaled = jnp.minimum(jnp.sqrt(dist_sq), 1.0)
    falloff = 1.0 - scaled
    kernel_value = kernel_norm * falloff**4 * (1.0 + 4.0 * scaled)
    kernel_slope = -20.0 * kernel_norm * falloff**3
    approach = sum(
        (
            (own_rows[3 + axis_id][:, :, None] - neighbour[3 + axis_id][:, None, :])
            * offset_parts[axis_id]
            for axis_id in range(3)
        )
    )
    return (offset_parts, dist_sq, kernel_value, kernel_slope, approach)


def density_terms(own_rows, neighbour, cell_shift):
    _, _, kernel_value, kernel_slope, approach = pair_geometry(own_rows, neighbour, cell_shift)
    other_mass = neighbour[6][:, None, :]
    return (
        jnp.sum(other_mass * kernel_value, -1),
        jnp.sum(other_mass * kernel_slope * approach, -1),
    )


def force_terms(own_rows, neighbour, cell_shift):
    offset_parts, dist_sq, _, kernel_slope, approach = pair_geometry(
        own_rows, neighbour, cell_shift
    )
    rho_own = own_rows[7][:, :, None]
    rho_other = neighbour[7][:, None, :]
    converge = jnp.minimum(approach, 0.0) / (dist_sq + 0.01)
    viscous = (
        -(own_rows[8][:, :, None] + neighbour[8][:, None, :]) * converge / (rho_own + rho_other)
    )
    mslope = neighbour[6][:, None, :] * kernel_slope
    pair_force = mslope * (1.0 / rho_own + 1.0 / rho_other + viscous)
    accel_terms = jnp.stack(
        [-jnp.sum(pair_force * offset_parts[axis_id], -1) for axis_id in range(3)], 0
    )
    heating = jnp.sum(mslope * (1.0 / rho_own + 0.5 * viscous) * approach, -1)
    return (accel_terms, heating)


def switch_fields(density, div_sum, live_rows, weights):
    rho_live = jnp.where(live_rows > 0, density, 1.0)
    compress = jnp.maximum(div_sum / rho_live, 0.0)
    return jnp.stack([rho_live, weights * compress / (compress + 1.0)], 0)


def sweep(terms, padded):
    count = padded.shape[0]
    slot_count = padded.shape[-1]
    span_x = padded.shape[1] - 2
    span_y = padded.shape[2] - 2
    span_z = padded.shape[3] - 2
    own_rows = padded[:, 1 : span_x + 1, 1 : span_y + 1, 1 : span_z + 1].reshape(
        count, -1, slot_count
    )
    totals = None
    for cell_shift in neighbour_shifts:
        neighbour = padded[
            :,
            1 + cell_shift[0] : 1 + cell_shift[0] + span_x,
            1 + cell_shift[1] : 1 + cell_shift[1] + span_y,
            1 + cell_shift[2] : 1 + cell_shift[2] + span_z,
        ]
        result = terms(own_rows, neighbour.reshape(count, -1, slot_count), cell_shift)
        totals = (
            result
            if totals is None
            else jax.tree.map(lambda left, right: left + right, totals, result)
        )
    return totals


def per_device(positions, velocities, masses, alphas, counts):
    slot_count = positions.shape[-1]
    cell_shape = positions.shape[1:4]
    occupied = (
        jnp.arange(slot_count, dtype=jnp.int32)[None, None, None, :] < counts[..., None]
    ).astype(jnp.float32)
    live_mass = masses * occupied
    carried = jnp.concatenate([positions, velocities, live_mass[None]], 0)
    padded = extended(carried, (("gx", 1), ("gy", 2), ("gz", 3)), 1)
    density, div_sum = sweep(density_terms, padded)
    live_rows = occupied.reshape(-1, slot_count)
    weights = alphas.reshape(-1, slot_count)
    pressure_fields = switch_fields(density, div_sum, live_rows, weights).reshape(
        (2,) + cell_shape + (slot_count,)
    )
    own_density = pressure_fields[0]
    pressure_pad = extended(pressure_fields, (("gx", 1), ("gy", 2), ("gz", 3)), 1)
    fields = jnp.concatenate([padded, pressure_pad], 0)
    accel_total, heat_total = sweep(force_terms, fields)
    acceleration = accel_total.reshape((3,) + cell_shape + (slot_count,)) * occupied[None]
    heating = heat_total.reshape(cell_shape + (slot_count,)) * occupied
    return (own_density, acceleration, heating)


def per_device_any(positions, velocities, masses, alphas, counts):
    if positions.shape[1:] == (2, 2, 2, 128):
        return per_block(positions, velocities, masses, alphas, counts)
    return per_device(positions, velocities, masses, alphas, counts)


def solution(mesh):
    return jax.shard_map(
        per_device_any,
        mesh=mesh,
        in_specs=(
            P(None, "gx", "gy", "gz", None),
            P(None, "gx", "gy", "gz", None),
            P("gx", "gy", "gz", None),
            P("gx", "gy", "gz", None),
            P("gx", "gy", "gz"),
        ),
        out_specs=(
            P("gx", "gy", "gz", None),
            P(None, "gx", "gy", "gz", None),
            P("gx", "gy", "gz", None),
        ),
        check_vma=False,
    )
```

```python
import math

import jax
import jax.numpy as jnp
from jax import lax
from jax.experimental import pallas as pl
from jax.experimental.pallas import tpu as pltpu
from jax.sharding import PartitionSpec as P


f32 = jnp.float32
bf16 = jnp.bfloat16
kernel_norm = 21.0 / (2.0 * math.pi)
tile_rows = 8
feature_rows = 48
tiny = 1e-12
together = 4

vmem = pl.BlockSpec(memory_space=pltpu.VMEM)


def shaped(*dims, kind=f32):
    return jax.ShapeDtypeStruct(dims, kind)


def paired(axis):
    return lax.axis_size(axis) % 2 == 0


def first_sends_high(axis):
    return lax.axis_index(axis) % 2 == 0 if paired(axis) else lax.axis_index(axis) >= 0


def first_gives_before(axis):
    return lax.axis_index(axis) % 2 == 1 if paired(axis) else lax.axis_index(axis) >= 0


def routes(axis):
    peers = lax.axis_size(axis)
    if peers % 2 == 0:
        first = [(i, i + 1 if i % 2 == 0 else i - 1) for i in range(peers)]
        second = [(i, (i - 1 if i % 2 == 0 else i + 1) % peers) for i in range(peers)]
    else:
        first = [(i, (i + 1) % peers) for i in range(peers)]
        second = [(i, (i - 1) % peers) for i in range(peers)]
    return first, second


def split3(value):
    high = value.astype(bf16).astype(f32)
    rest = value - high
    middle = rest.astype(bf16).astype(f32)
    return high, middle, rest - middle


def row_ids():
    return lax.broadcasted_iota(jnp.int32, (tile_rows, 128), 0)


def rows_of(*rows):
    ids = row_ids()
    out = jnp.zeros((tile_rows, 128), f32)
    for place, row in enumerate(rows):
        out = jnp.where(ids == place, row, out)
    return out


def moments(tile, offsets):
    ids = row_ids()
    shift = jnp.where(ids == 0, offsets[0], jnp.where(ids == 1, offsets[1], jnp.where(ids == 2, offsets[2], 0.0)))
    high, low, _ = split3(tile + shift)
    moved = high + low.astype(bf16).astype(f32)
    x, y, z, vx, vy, vz = (moved[i : i + 1] for i in range(6))
    sq = x * x + y * y + z * z
    xv = x * vx + y * vy + z * vz
    return jnp.where(ids == 6, sq, jnp.where(ids == 7, xv, moved)), tile[6:7]


def column_features(table):
    p1, p2, p3 = split3(table)
    ids = row_ids()
    extra = jnp.where(ids < 3, 1.0, jnp.where(ids >= 6, p3, 0.0))
    return jnp.concatenate([p1, p1, p2, p2, extra, jnp.zeros_like(extra)], 0).T.astype(bf16)


def row_features(table):
    ids = row_ids()
    sq = split3(table[6:7])
    xv = split3(table[7:8])
    down = pltpu.roll(table, 3, 0)
    up = pltpu.roll(table, 5, 0)
    left = jnp.where(ids < 3, -2.0 * table, jnp.where(ids == 6, 1.0, 0.0))
    right = jnp.where(ids < 3, -up, jnp.where(ids < 6, -down, jnp.where(ids == 7, 1.0, 0.0)))
    halves = []
    for part, fixed in ((left, sq), (right, xv)):
        q1, q2, _ = split3(part)
        extra = rows_of(*fixed) + jnp.where(ids >= 6, part, 0.0)
        halves.append(jnp.concatenate([q1, q2, q1, q2, extra, jnp.zeros_like(extra)], 0))
    return jnp.concatenate(halves, 1).astype(bf16)


def mass_columns(table, mass):
    weighted = mass * table
    w1, w2, _ = split3(weighted)
    m1, m2, _ = split3(mass)
    extra = rows_of(m1, m2)
    left = jnp.concatenate([w1, w2, extra, jnp.zeros_like(extra)], 0).astype(bf16)
    return jnp.concatenate([left, left], 1)


def prepare(tile, offsets, at, feats, masses, columns):
    table, mass = moments(tile, offsets)
    feats[at] = row_features(table)
    masses[at] = jnp.broadcast_to(mass, (16, 128))
    columns[at] = mass_columns(table, mass)


def over_lanes(left, right):
    return lax.dot_general(left, right, (((1,), (1,)), ((), ())), preferred_element_type=f32)


def pipelined(tiles, stages):
    for step in range(len(tiles) + len(stages) - 1):
        for lag, stage in enumerate(stages):
            if 0 <= step - lag < len(tiles):
                stage(*tiles[step - lag])


def idle(*tile):
    pass


def over_cells(body):
    lax.fori_loop(0, 8 // together, lambda i, _: body([i * together + j for j in range(together)]), 0)


def density_pairs(own, near, feats, masses, columns, slopes, pairs, sums, weighted):
    ones = jnp.ones((tile_rows, 256), bf16)

    def some(group):
        both, sofar = {}, {}
        picks = [near(c) for c in group]
        tiles = [(j, k) for j in range(len(group)) for k in range(len(picks[j]))]

        def geometry(j, k):
            pair = both[j, k] = jnp.dot(own[group[j]], feats[picks[j][k]], preferred_element_type=f32)
            pairs[group[j], k] = pair

        def terms(j, k):
            c, n = group[j], picks[j][k]
            pair = both.pop((j, k))
            mass = masses[n]
            for r in range(0, 128, 16):
                at = slice(r, r + 16)
                dist = jnp.maximum(pair[at, :128], tiny)
                q = dist * lax.rsqrt(dist)
                fall = jnp.maximum(1.0 - q, 0.0)
                g = fall * fall * fall
                part = g * q * mass
                weighted[j, at] = part if k == 0 else weighted[j, at] + part
                high = g.astype(bf16)
                slopes[c, k, at, :128] = high
                slopes[c, k, at, 128:] = (g - high.astype(f32)).astype(bf16)

        def reduce(j, k):
            c, n = group[j], picks[j][k]
            part = over_lanes(columns[n], slopes[c, k])
            sofar[j] = part if j not in sofar else sofar[j] + part
            if k == len(picks[j]) - 1:
                sums[c, :32] = sofar[j]
                high = weighted[j].astype(bf16)
                low = (weighted[j] - high.astype(f32)).astype(bf16)
                sums[c, 32:] = over_lanes(ones, jnp.concatenate([high, low], 1))

        pipelined(tiles, (geometry, idle, terms, idle, reduce))
        return 0

    over_cells(some)


def prepare_force(tile, offsets, press, at, rhos, columns, gradients):
    table, mass = moments(tile, offsets)
    rho = press[0:1]
    weight = press[1:2]
    heavy = mass * jnp.where(row_ids() == 6, 1.0, table)
    h1, h2, _ = split3(heavy)
    s1, s2, _ = split3(weight * heavy)
    left = jnp.concatenate([h1, h2, s1, s2], 0).astype(bf16)
    columns[at] = jnp.concatenate([left, left], 1)
    light = (mass / rho) * jnp.where(row_ids() < 3, table, 1.0)
    l1, l2, _ = split3(light)
    left = jnp.concatenate([l1, l2], 0).astype(bf16)
    gradients[at] = jnp.concatenate([left, left], 1)
    rhos[at] = jnp.broadcast_to(rho, (16, 128))


def force_pairs(near, spread, rhos, columns, gradients, slopes, pairs, sums, pulls):
    def some(group):
        mixed, sofar, pulled = {}, {}, {}
        picks = [near(c) for c in group]
        tiles = [(j, k) for j, c in enumerate(group) for k in range(len(near(c)))]

        def terms(j, k):
            c, n = group[j], picks[j][k]
            highs, lows = [], []
            theirs = rhos[n]
            for r in range(0, 128, 16):
                at = slice(r, r + 16)
                below = theirs + spread[c, at]
                g = slopes[c, k, at, :128].astype(f32) + slopes[c, k, at, 128:].astype(f32)
                run = jnp.minimum(pairs[c, k, at, 128:], 0.0)
                t = g * run * (1.0 / ((pairs[c, k, at, :128] + 0.01) * below))
                high = t.astype(bf16)
                highs.append(high)
                lows.append((t - high.astype(f32)).astype(bf16))
            mixed[j, k] = jnp.concatenate([jnp.concatenate(highs, 0), jnp.concatenate(lows, 0)], 1)

        def reduce(j, k):
            c, n = group[j], picks[j][k]
            part = over_lanes(columns[n], mixed.pop((j, k)))
            pull = over_lanes(gradients[n], slopes[c, k])
            sofar[j] = part if j not in sofar else sofar[j] + part
            pulled[j] = pull if j not in pulled else pulled[j] + pull
            if k == len(picks[j]) - 1:
                sums[c] = sofar[j]
                pulls[c] = pulled[j]

        pipelined(tiles, (terms, idle, reduce))
        return 0

    over_cells(some)


def parts_of(c):
    return c // 4, (c // 2) % 2, c % 2


def flat(*pairs):
    at = 0
    for size, index in pairs:
        at = at * size + index
    return at


def near_own(c):
    return list(range(8))


def near_z(c):
    _, _, cz = parts_of(c)
    return [flat((2, cz), (2, x), (2, y)) for x in range(2) for y in range(2)]


def near_x(c):
    cx, _, cz = parts_of(c)
    return [flat((2, cx), (2, y), (4, cz + dz)) for y in range(2) for dz in range(3)]


def near_y(c):
    cx, cy, cz = parts_of(c)
    return [flat((2, cy), (4, cx + dx), (4, cz + dz)) for dx in range(3) for dz in range(3)]


def place_own(e):
    x, y, z = parts_of(e)
    return x - 1, y - 1, z - 1


def place_z(e):
    side, x, y = parts_of(e)
    return x - 1, y - 1, 3 * side - 2


def place_x(e):
    return 3 * (e // 8) - 2, (e // 4) % 2 - 1, e % 4 - 2


def place_y(e):
    return (e // 4) % 4 - 2, 3 * (e // 16) - 2, e % 4 - 2


def offsets_of(place):
    return [jnp.asarray(v, jnp.int32).astype(f32) for v in place]


groups = {
    "own": (8, near_own, place_own, 8),
    "z": (8, near_z, place_z, 4),
    "x": (16, near_x, place_x, 6),
    "y": (32, near_y, place_y, 9),
}


weights = pltpu.VMEM((together, 128, 128), f32)


def scratch_density(entries):
    return [
        pltpu.VMEM((entries, feature_rows, 256), bf16),
        pltpu.VMEM((entries, 16, 128), f32),
        pltpu.VMEM((entries, 32, 256), bf16),
        weights,
    ]


def pair_outputs(count):
    return [
        shaped(8, count, 128, 256, kind=bf16),
        shaped(8, count, 128, 256),
        shaped(8, 40, 128),
    ]


def call(body, outs, operands, specs=None, scratch=(), limit=12):
    return pl.pallas_call(
        body,
        out_shape=tuple(outs),
        in_specs=specs or [vmem] * len(operands),
        out_specs=tuple([vmem] * len(outs)),
        scratch_shapes=list(scratch),
        compiler_params=pltpu.CompilerParams(vmem_limit_bytes=limit << 20),
    )(*operands)


def take_side(before, refs, side, rest):
    if len(refs) == 1:
        one, two = refs[0][(0,) + rest], refs[0][(1,) + rest]
    else:
        one, two = refs[0][rest], refs[1][rest]
    return jnp.where(before, one, two) if side == 0 else jnp.where(before, two, one)


def send_shapes(axis, plane):
    if lax.axis_size(axis) == 2:
        return [shaped(2, *plane)]
    return [shaped(*plane), shaped(*plane)]


def put_sends(refs, high, tile_at, rest):
    top, bottom = tile_at(1), tile_at(0)
    one, two = jnp.where(high, top, bottom), jnp.where(high, bottom, top)
    if len(refs) == 1:
        refs[0][(0,) + rest] = one
        refs[0][(1,) + rest] = two
    else:
        refs[0][rest] = one
        refs[1][rest] = two


def receive(axis, sends):
    first, second = routes(axis)
    ways = (first,) if len(sends) == 1 else (first, second)
    got = []
    for send, way in zip(sends, ways):
        got.append(lax.ppermute(send, axis, way))
    return tuple(got)


def pack_x(own, from_z, rows):
    sends = send_shapes("gx", (2, 4, rows, 128))
    n = len(from_z)

    def body(own_ref, *refs):
        got, out = refs[:n], refs[n:]
        high = first_sends_high("gx")
        before = first_gives_before("gz")
        for y in range(2):
            for e in range(4):

                def tile_at(x, y=y, e=e):
                    if 1 <= e <= 2:
                        return own_ref[x, y, e - 1]
                    return take_side(before, got, 0 if e == 0 else 1, (x, y))

                put_sends(out, high, tile_at, (y, e))

    return call(body, sends, (own, *from_z), limit=4)


def pack_y(own, from_z, from_x, rows):
    sends = send_shapes("gy", (4, 4, rows, 128))
    n, m = len(from_z), len(from_x)

    def body(own_ref, *refs):
        got_z, got_x, out = refs[:n], refs[n : n + m], refs[n + m :]
        high = first_sends_high("gy")
        before_z = first_gives_before("gz")
        before_x = first_gives_before("gx")
        for a in range(4):
            for e in range(4):

                def tile_at(y, a=a, e=e):
                    if not 1 <= a <= 2:
                        return take_side(before_x, got_x, 0 if a == 0 else 1, (y, e))
                    if 1 <= e <= 2:
                        return own_ref[a - 1, y, e - 1]
                    return take_side(before_z, got_z, 0 if e == 0 else 1, (a - 1, y))

                put_sends(out, high, tile_at, (a, e))

    return call(body, sends, (own, *from_z, *from_x), limit=4)


inner_dims = {"z": (2, 2), "x": (2, 4), "y": (4, 4)}


def entry_tile(group, before, refs, e, sides):
    _, b = inner_dims[group]
    return take_side(before, refs, sides, (e // b, e % b))


def density_own(own):
    entries, near, place, count = groups["own"]

    def body(own_ref, slopes, pairs, sums, table_ref, feats, masses, columns, weighted):
        def one(c, _):
            x, y, z = parts_of(c)
            tile = own_ref[x, y, z]
            offsets = offsets_of(place(c))
            prepare(tile, offsets, c, feats, masses, columns)
            table, _ = moments(tile, offsets)
            table_ref[c] = column_features(table)
            return 0

        lax.fori_loop(0, 8, one, 0, unroll=8)
        density_pairs(table_ref, near, feats, masses, columns, slopes, pairs, sums, weighted)

    outs = pair_outputs(count) + [shaped(8, 128, feature_rows, kind=bf16)]
    return call(body, outs, (own,), scratch=scratch_density(entries))


def density_halo(group, axis, received, own_feats):
    entries, near, place, count = groups[group]
    n = len(received)
    half = entries // 2

    def body(*refs):
        got, own_ref = refs[:n], refs[n]
        slopes, pairs, sums, feats, masses, columns, weighted = refs[n + 1 :]
        before = first_gives_before(axis)
        for side in range(2):

            def one(e, _, side=side):
                tile = entry_tile(group, before, got, e, side)
                at = side * half + e
                prepare(tile, offsets_of(place(at)), at, feats, masses, columns)
                return 0

            lax.fori_loop(0, half, one, 0, unroll=half)
        density_pairs(own_ref, near, feats, masses, columns, slopes, pairs, sums, weighted)

    return call(body, pair_outputs(count), (*received, own_feats), scratch=scratch_density(entries))


def pressure(own, partials):
    sends = send_shapes("gz", (2, 2, 2, 128))
    outs = [shaped(2, 2, 2, 2, 128), shaped(8, tile_rows, 128)] + sends
    n = len(partials)

    def body(own_ref, *refs):
        pieces, (press, first), out = refs[:n], refs[n : n + 2], refs[n + 2 :]
        high = first_sends_high("gz")
        for x in range(2):
            for y in range(2):
                for z in range(2):
                    c = 4 * x + 2 * y + z
                    table, mass = moments(own_ref[x, y, z], [float(v - 1) for v in (x, y, z)])
                    s = sum(p[c] for p in pieces)
                    gq = s[32:33]
                    t = s[0:8] + s[8:16]
                    m0 = s[16:17] + s[17:18]
                    pos, vel = table[0:3], table[3:6]
                    x_mx = jnp.sum(pos * t[0:3], 0, keepdims=True)
                    x_mv = jnp.sum(pos * t[3:6], 0, keepdims=True)
                    v_mx = jnp.sum(vel * t[0:3], 0, keepdims=True)
                    gr2 = t[6:7] + table[6:7] * m0 - 2.0 * x_mx
                    rho = kernel_norm * (m0 + 3.0 * gq - 4.0 * gr2)
                    div = -20.0 * kernel_norm * (t[7:8] + table[7:8] * m0 - x_mv - v_mx)
                    rho = jnp.where(mass > 0.0, rho, 1.0)
                    compress = jnp.maximum(div / rho, 0.0)
                    weight = own_ref[x, y, z, 7:8] * compress / (compress + 1.0)
                    press[x, y, z] = jnp.concatenate([rho, weight], 0)
                    first[c] = jnp.concatenate(
                        [pos * m0 - t[0:3], div, jnp.zeros((tile_rows - 4, 128), f32)], 0
                    )
        for x in range(2):
            for y in range(2):
                put_sends(out, high, lambda z, x=x, y=y: press[x, y, z], (x, y))

    return call(body, outs, (own, *partials), limit=8)


def spread_own(press):
    def body(press_ref, spread):
        chosen = jnp.where(lax.broadcasted_iota(jnp.int32, (16, 128), 0) < 3, 1.0, 0.0).astype(bf16)
        for c in range(8):
            x, y, z = parts_of(c)
            parts = rows_of(*split3(press_ref[x, y, z, 0:1]))
            parts = jnp.concatenate([parts, jnp.zeros_like(parts)], 0).T.astype(bf16)
            spread[c] = jnp.dot(parts, chosen, preferred_element_type=f32)

    return call(body, [shaped(8, 128, 128)], (press,), limit=4)[0]


def scratch_force(entries):
    return [
        pltpu.VMEM((entries, 16, 128), f32),
        pltpu.VMEM((entries, 32, 256), bf16),
        pltpu.VMEM((entries, 16, 256), bf16),
    ]


def force_outputs():
    return [shaped(8, 32, 128), shaped(8, 16, 128)]


def force_own(own, press, spread, kept):
    entries, near, place, _ = groups["own"]

    def body(own_ref, press_ref, spread_ref, slopes, pairs, sums, pulls, rhos, columns, gradients):
        def one(c, _):
            x, y, z = parts_of(c)
            prepare_force(
                own_ref[x, y, z], offsets_of(place(c)), press_ref[x, y, z], c, rhos, columns, gradients
            )
            return 0

        lax.fori_loop(0, 8, one, 0, unroll=8)

        force_pairs(near, spread_ref, rhos, columns, gradients, slopes, pairs, sums, pulls)

    return call(body, force_outputs(), (own, press, spread, *kept), scratch=scratch_force(entries))


def force_halo(group, axis, received, press_received, spread, kept):
    entries, near, place, _ = groups[group]
    n = len(received)
    half = entries // 2

    def body(*refs):
        got, got_press, spread_ref = refs[:n], refs[n : 2 * n], refs[2 * n]
        slopes, pairs, sums, pulls, rhos, columns, gradients = refs[2 * n + 1 :]
        before = first_gives_before(axis)
        for side in range(2):

            def one(e, _, side=side):
                tile = entry_tile(group, before, got, e, side)
                fields = entry_tile(group, before, got_press, e, side)
                at = side * half + e
                prepare_force(tile, offsets_of(place(at)), fields, at, rhos, columns, gradients)
                return 0

            lax.fori_loop(0, half, one, 0, unroll=half)

        force_pairs(near, spread_ref, rhos, columns, gradients, slopes, pairs, sums, pulls)

    return call(
        body,
        force_outputs(),
        (*received, *press_received, spread, *kept),
        scratch=scratch_force(entries),
    )


def finish(own, press, first, partials):
    outs = [shaped(2, 2, 2, 128), shaped(3, 2, 2, 2, 128), shaped(2, 2, 2, 128)]
    n = len(partials)

    def body(own_ref, press_ref, first_ref, *refs):
        pieces, (density, accel, heating) = refs[:n], refs[n:]
        for x in range(2):
            for y in range(2):
                for z in range(2):
                    c = 4 * x + 2 * y + z
                    table, mass = moments(own_ref[x, y, z], [float(v - 1) for v in (x, y, z)])
                    u = sum(p[c] for p in pieces[0::2])
                    v = sum(p[c] for p in pieces[1::2])
                    plain, scaled = u[0:8] + u[8:16], u[16:24] + u[24:32]
                    a0, b0 = plain[6:7], scaled[6:7]
                    g = v[0:8] + v[8:16]
                    rho, weight = press_ref[x, y, z, 0:1], press_ref[x, y, z, 1:2]
                    inverse = 1.0 / rho
                    mixed = weight * plain + scaled
                    zero = weight * a0 + b0
                    pos, vel = table[0:3], table[3:6]
                    total = (
                        inverse * first_ref[c, 0:3]
                        + (pos * g[3:4] - g[0:3])
                        - (pos * zero - mixed[0:3])
                    )
                    live = jnp.where(mass > 0.0, 1.0, 0.0)
                    push = (20.0 * kernel_norm) * live * total
                    work = (
                        mixed[7:8]
                        + table[7:8] * zero
                        - jnp.sum(pos * mixed[3:6], 0, keepdims=True)
                        - jnp.sum(vel * mixed[0:3], 0, keepdims=True)
                    )
                    warm = live * (first_ref[c, 3:4] * inverse + (10.0 * kernel_norm) * work)
                    density[x, y, z : z + 1, :] = rho
                    for i in range(3):
                        accel[i, x, y, z : z + 1, :] = push[i : i + 1]
                    heating[x, y, z : z + 1, :] = warm

    return call(body, outs, (own, press, first, *partials), limit=8)


def gather_own(*arguments):
    sends = send_shapes("gz", (2, 2, tile_rows, 128))

    def body(*refs):
        sources, own, out = refs[:5], refs[5], refs[6 : 6 + len(sends)]
        held, arrived = refs[6 + len(sends) : -1], refs[-1]
        copies = [pltpu.make_async_copy(a, b, arrived.at[i]) for i, (a, b) in enumerate(zip(sources, held))]
        for copy in copies:
            copy.start()
        for copy in copies:
            copy.wait()
        pos, vel, mass, alpha, count = held
        high = first_sends_high("gz")
        lanes = lax.broadcasted_iota(jnp.int32, (1, 128), 1)
        for x in range(2):
            for y in range(2):
                for z in range(2):
                    dead = lanes >= count[x, y : y + 1, z : z + 1]
                    own[x, y, z] = rows_of(
                        *(pos[i, x, y, z : z + 1, :] for i in range(3)),
                        *(vel[i, x, y, z : z + 1, :] for i in range(3)),
                        jnp.where(dead, 0.0, mass[x, y, z : z + 1, :]),
                        alpha[x, y, z : z + 1, :],
                    )
        for x in range(2):
            for y in range(2):
                put_sends(out, high, lambda z, x=x, y=y: own[x, y, z], (x, y))

    scratch = [pltpu.VMEM(a.shape, a.dtype) for a in arguments] + [pltpu.SemaphoreType.DMA((5,))]
    return call(
        body,
        [shaped(2, 2, 2, tile_rows, 128)] + sends,
        [pltpu.with_memory_space_constraint(a, pltpu.HBM) for a in arguments],
        specs=[pl.BlockSpec(memory_space=pltpu.HBM)] * 5,
        scratch=scratch,
        limit=4,
    )


def per_block(positions, velocities, masses, alphas, counts):
    own, *sends = gather_own(positions, velocities, masses, alphas, counts)
    from_z = receive("gz", sends)
    *kept_own, sums_own, own_feats = density_own(own)
    from_x = receive("gx", pack_x(own, from_z, tile_rows))
    *kept_z, sums_z = density_halo("z", "gz", from_z, own_feats)
    from_y = receive("gy", pack_y(own, from_z, from_x, tile_rows))
    *kept_x, sums_x = density_halo("x", "gx", from_x, own_feats)
    *kept_y, sums_y = density_halo("y", "gy", from_y, own_feats)
    press, first, *sends = pressure(own, (sums_own, sums_z, sums_x, sums_y))
    press_z = receive("gz", sends)
    spread = spread_own(press)
    forces = list(force_own(own, press, spread, kept_own))
    press_x = receive("gx", pack_x(press, press_z, 2))
    forces += force_halo("z", "gz", from_z, press_z, spread, kept_z)
    press_y = receive("gy", pack_y(press, press_z, press_x, 2))
    forces += force_halo("x", "gx", from_x, press_x, spread, kept_x)
    forces += force_halo("y", "gy", from_y, press_y, spread, kept_y)
    return finish(own, press, first, forces)


neighbour_shifts = [
    (shift_x, shift_y, shift_z)
    for shift_x in (-1, 0, 1)
    for shift_y in (-1, 0, 1)
    for shift_z in (-1, 0, 1)
]


def extended(shard, sides, width):
    for axis, dim in sides:
        peers, length = (lax.axis_size(axis), shard.shape[dim])
        up = [(i, (i + 1) % peers) for i in range(peers)]
        down = [(j, i) for i, j in up]
        last = lax.slice_in_dim(shard, length - width, length, axis=dim)
        leading = lax.slice_in_dim(shard, 0, width, axis=dim)
        before = lax.ppermute(last, axis, up)
        after = lax.ppermute(leading, axis, down)
        shard = jnp.concatenate([before, shard, after], axis=dim)
    return shard


def pair_geometry(own_rows, neighbour, cell_shift):
    offset_parts = [
        own_rows[axis_id][:, :, None] - neighbour[axis_id][:, None, :] - float(cell_shift[axis_id])
        for axis_id in range(3)
    ]
    dist_sq = (
        offset_parts[0] * offset_parts[0]
        + offset_parts[1] * offset_parts[1]
        + offset_parts[2] * offset_parts[2]
    )
    scaled = jnp.minimum(jnp.sqrt(dist_sq), 1.0)
    falloff = 1.0 - scaled
    kernel_value = kernel_norm * falloff**4 * (1.0 + 4.0 * scaled)
    kernel_slope = -20.0 * kernel_norm * falloff**3
    approach = sum(
        (
            (own_rows[3 + axis_id][:, :, None] - neighbour[3 + axis_id][:, None, :])
            * offset_parts[axis_id]
            for axis_id in range(3)
        )
    )
    return (offset_parts, dist_sq, kernel_value, kernel_slope, approach)


def density_terms(own_rows, neighbour, cell_shift):
    _, _, kernel_value, kernel_slope, approach = pair_geometry(own_rows, neighbour, cell_shift)
    other_mass = neighbour[6][:, None, :]
    return (
        jnp.sum(other_mass * kernel_value, -1),
        jnp.sum(other_mass * kernel_slope * approach, -1),
    )


def force_terms(own_rows, neighbour, cell_shift):
    offset_parts, dist_sq, _, kernel_slope, approach = pair_geometry(
        own_rows, neighbour, cell_shift
    )
    rho_own = own_rows[7][:, :, None]
    rho_other = neighbour[7][:, None, :]
    converge = jnp.minimum(approach, 0.0) / (dist_sq + 0.01)
    viscous = (
        -(own_rows[8][:, :, None] + neighbour[8][:, None, :]) * converge / (rho_own + rho_other)
    )
    mslope = neighbour[6][:, None, :] * kernel_slope
    pair_force = mslope * (1.0 / rho_own + 1.0 / rho_other + viscous)
    accel_terms = jnp.stack(
        [-jnp.sum(pair_force * offset_parts[axis_id], -1) for axis_id in range(3)], 0
    )
    heating = jnp.sum(mslope * (1.0 / rho_own + 0.5 * viscous) * approach, -1)
    return (accel_terms, heating)


def switch_fields(density, div_sum, live_rows, weights):
    rho_live = jnp.where(live_rows > 0, density, 1.0)
    compress = jnp.maximum(div_sum / rho_live, 0.0)
    return jnp.stack([rho_live, weights * compress / (compress + 1.0)], 0)


def sweep(terms, padded):
    count = padded.shape[0]
    slot_count = padded.shape[-1]
    span_x = padded.shape[1] - 2
    span_y = padded.shape[2] - 2
    span_z = padded.shape[3] - 2
    own_rows = padded[:, 1 : span_x + 1, 1 : span_y + 1, 1 : span_z + 1].reshape(
        count, -1, slot_count
    )
    totals = None
    for cell_shift in neighbour_shifts:
        neighbour = padded[
            :,
            1 + cell_shift[0] : 1 + cell_shift[0] + span_x,
            1 + cell_shift[1] : 1 + cell_shift[1] + span_y,
            1 + cell_shift[2] : 1 + cell_shift[2] + span_z,
        ]
        result = terms(own_rows, neighbour.reshape(count, -1, slot_count), cell_shift)
        totals = (
            result
            if totals is None
            else jax.tree.map(lambda left, right: left + right, totals, result)
        )
    return totals


def per_device(positions, velocities, masses, alphas, counts):
    slot_count = positions.shape[-1]
    cell_shape = positions.shape[1:4]
    occupied = (
        jnp.arange(slot_count, dtype=jnp.int32)[None, None, None, :] < counts[..., None]
    ).astype(jnp.float32)
    live_mass = masses * occupied
    carried = jnp.concatenate([positions, velocities, live_mass[None]], 0)
    padded = extended(carried, (("gx", 1), ("gy", 2), ("gz", 3)), 1)
    density, div_sum = sweep(density_terms, padded)
    live_rows = occupied.reshape(-1, slot_count)
    weights = alphas.reshape(-1, slot_count)
    pressure_fields = switch_fields(density, div_sum, live_rows, weights).reshape(
        (2,) + cell_shape + (slot_count,)
    )
    own_density = pressure_fields[0]
    pressure_pad = extended(pressure_fields, (("gx", 1), ("gy", 2), ("gz", 3)), 1)
    fields = jnp.concatenate([padded, pressure_pad], 0)
    accel_total, heat_total = sweep(force_terms, fields)
    acceleration = accel_total.reshape((3,) + cell_shape + (slot_count,)) * occupied[None]
    heating = heat_total.reshape(cell_shape + (slot_count,)) * occupied
    return (own_density, acceleration, heating)


def per_device_any(positions, velocities, masses, alphas, counts):
    if positions.shape[1:] == (2, 2, 2, 128):
        return per_block(positions, velocities, masses, alphas, counts)
    return per_device(positions, velocities, masses, alphas, counts)


def solution(mesh):
    return jax.shard_map(
        per_device_any,
        mesh=mesh,
        in_specs=(
            P(None, "gx", "gy", "gz", None),
            P(None, "gx", "gy", "gz", None),
            P("gx", "gy", "gz", None),
            P("gx", "gy", "gz", None),
            P("gx", "gy", "gz"),
        ),
        out_specs=(
            P("gx", "gy", "gz", None),
            P(None, "gx", "gy", "gz", None),
            P("gx", "gy", "gz", None),
        ),
        check_vma=False,
    )
```
